128 devices in a mesh: clus: 16 (over y, x_hi, core), theta: 8 (over x_lo, z).
Axes of the slice: x: 4 (x_hi: 2, x_lo: 2; x = x_hi * 2 + x_lo), y: 4, z: 4, core: 2. Of those that a mesh axis runs over, the one named last changes fastest.
Arguments:
- children: float32 [128, 2, 2, 128, 256], P('clus', None, None, 'theta'), may hold values from -6 to 6
- theta_band: float32 [256, 8], P('theta'), may hold values from -2 to 2
- phi_interp: float32 [256, 512], replicated, may hold values from -0.375 to 0.375
- child_shift: float32 [4, 2, 256, 512], P(None, None, 'theta'), may hold values from -4 to 4
- translators: float32 [40, 2, 256, 512], P(None, None, ('theta', 'clus')), may hold values from -1.5 to 1.5
- far_source: int32 [32, 32], replicated, may hold values from 0 to 31
- far_offset: int32 [32, 32], replicated, may hold values from 0 to 39
- far_count: int32 [32], replicated, may hold values from 4 to 32, as said below
Outputs:
- incoming: float32 [128, 2, 2, 128, 256], P('clus', None, None, 'theta')
The draws below stay inside these ranges and needn't reach their ends.
Inputs may be any that keep to these rules, and one draw needn't show every extreme that they name: The first far_count[p] slots of row p of far_source and far_offset are valid; the remaining slots are padding and carry no interaction. A list is full in every draw.
All inputs are finite; a program needn't handle non-finite values.
Results may differ from the reference program's by a relative error of at most 0.0003.
Values sent between devices are 32-bit elements; how exact they have to be, the bound alone decides.
No kernel may reach another device: no remote copies, remote signals or barrier semaphores. Data moves between devices by JAX's collectives and lax.ppermute only.
A program may use at most 128 MiB of HBM per device.

```python
import jax
import jax.numpy as jnp
from jax import lax

TC = 128
PC = 256
TP = 256
PP = 512
KIDS = 4
LIST = 32
NOFF = 40
PAR_DEV = 2
NPAR = 32
NCHILD = 128


def draw_far_count(key, part):
    first_key, second_key, third_key = jax.random.split(key, 3)
    groups = NPAR // PAR_DEV
    heavy_group = jax.random.randint(first_key, (groups,), 0, 4) == 0
    chosen = jax.random.randint(second_key, (), 0, groups)
    heavy_group = heavy_group | (jnp.arange(groups) == chosen)
    light_count = jax.random.randint(third_key, (NPAR,), LIST // 8, LIST // 2 + 1)
    return jnp.where(jnp.repeat(heavy_group, PAR_DEV), LIST, light_count).astype(jnp.int32)


def place_ends(drawn, own_key, smallest, high):
    shape = drawn.shape
    place = [jax.random.randint(jax.random.fold_in(own_key, axis), (), 0, shape[axis]) for axis in range(len(shape))]
    drawn = drawn.at[tuple(place)].set(smallest)
    longest = shape.index(max(shape))
    place[longest] = (place[longest] + 1) % shape[longest]
    return drawn.at[tuple(place)].set(high)


def shard_levels(rng, dims, shards, low, high):
    factor_of, own = 1.0, jax.random.fold_in(rng, 6)
    for axis_at, shards_of in shards:
        heights = jnp.exp(jax.random.uniform(jax.random.fold_in(own, axis_at), (shards_of,), jnp.float32, low / len(shards), high / len(shards)))
        factor_of = factor_of * jnp.repeat(heights, dims[axis_at] // shards_of).reshape([-1 if axis == axis_at else 1 for axis in range(len(dims))])
    return factor_of


def noise(own_key, shape, spread, reach, pieces=(), kind=jnp.bfloat16):
    array = jax.random.normal(own_key, shape, jnp.float32) * spread
    if len(pieces) > 0:
        array = shard_levels(own_key, shape, pieces, -0.22, 0.18) * array
    return jnp.clip(array, min=-reach, max=reach).astype(kind)


def setup_inputs(seed: int = 0) -> dict:
    streams_of = jax.random.split(jax.random.key(seed), 9)
    children = noise(streams_of[0], (NCHILD, 2, 2, TC, PC), 1.0, 6.0, ((0, 16), (3, 8)), jnp.float32)
    theta_band = noise(streams_of[1], (TP, 8), 0.35, 2.0, ((0, 8),), jnp.float32)
    phi_interp = noise(streams_of[2], (PC, PP), PC ** -0.5, 0.375, (), jnp.float32)
    child_shift = noise(streams_of[3], (KIDS, 2, TP, PP), 0.7, 4.0, ((2, 8),), jnp.float32)
    translators = noise(streams_of[4], (NOFF, 2, TP, PP), 0.25, 1.5, ((2, 128),), jnp.float32)
    far_source = place_ends(jax.random.randint(streams_of[5], (NPAR, LIST), 0, NPAR), jax.random.fold_in(streams_of[5], 1), 0, NPAR - 1).astype(jnp.int32)
    far_offset = place_ends(jax.random.randint(streams_of[6], (NPAR, LIST), 0, NOFF), jax.random.fold_in(streams_of[6], 1), 0, NOFF - 1).astype(jnp.int32)
    far_count = draw_far_count(jax.random.fold_in(streams_of[8], 71), 0)
    return dict(children=children, theta_band=theta_band, phi_interp=phi_interp, child_shift=child_shift, translators=translators, far_source=far_source, far_offset=far_offset, far_count=far_count)


highest = lax.Precision.HIGHEST


def complex_times(left_side, right_side):
    real_part = left_side[..., 0, :, :] * right_side[..., 0, :, :] - left_side[..., 1, :, :] * right_side[..., 1, :, :]
    imag_part = left_side[..., 0, :, :] * right_side[..., 1, :, :] + left_side[..., 1, :, :] * right_side[..., 0, :, :]
    return jnp.stack([real_part, imag_part], axis=-3)


def theta_spread(padded, theta_band):
    child_rows = padded.shape[-2] - 8
    result = None
    for tap_index in range(8):
        slab_rows = padded[..., tap_index + 1:tap_index + 1 + child_rows, :]
        term = theta_band[:, tap_index][:, None] * jnp.repeat(slab_rows, 2, axis=-2)
        result = term if result is None else result + term
    return result


def theta_adjoint(values, theta_band):
    child_rows = values.shape[-2] // 2
    shape = values.shape[:-2] + (child_rows + 8, values.shape[-1])
    result = jnp.zeros(shape, values.dtype)
    for tap_index in range(8):
        weighted = theta_band[:, tap_index][:, None] * values
        paired = weighted[..., 0::2, :] + weighted[..., 1::2, :]
        widths = [(0, 0)] * (values.ndim - 2) + [(tap_index + 1, 7 - tap_index), (0, 0)]
        result = result + jnp.pad(paired, widths)
    return result


def phi_forward(values, phi_interp):
    return jnp.einsum('...q,qp->...p', values, phi_interp, precision=highest)


def phi_backward(values, phi_interp):
    return jnp.einsum('...p,qp->...q', values, phi_interp, precision=highest)


def reference(children, theta_band, phi_interp, child_shift, translators, far_source, far_offset, far_count):
    kid_groups = children.reshape(NPAR, KIDS, 2, 2, TC, PC)

    def aggregate(kid_block):
        padded = jnp.pad(kid_block, ((0, 0), (0, 0), (0, 0), (4, 4), (0, 0)))
        fine_field = phi_forward(theta_spread(padded, theta_band), phi_interp)
        return jnp.sum(complex_times(child_shift[:, None], fine_field), axis=0)

    parents = lax.map(aggregate, kid_groups)

    def translate(parent_index):
        sources = jnp.take(parents, far_source[parent_index], axis=0)
        operators = jnp.take(translators, far_offset[parent_index], axis=0)[:, None]
        live_mask = (jnp.arange(LIST) < far_count[parent_index]).astype(parents.dtype)
        return jnp.sum(live_mask[:, None, None, None, None] * complex_times(operators, sources), axis=0)

    local_fields = lax.map(translate, jnp.arange(NPAR))
    conjugate = jnp.stack([child_shift[:, 0], -child_shift[:, 1]], axis=1)

    def disaggregate(sample_field):
        shifted = complex_times(conjugate[:, None], sample_field[None])
        back_phi = phi_backward(shifted, phi_interp)
        extended = theta_adjoint(back_phi, theta_band)
        return extended[..., 4:4 + TC, :]

    incoming = lax.map(disaggregate, local_fields)
    return incoming.reshape(NCHILD, 2, 2, TC, PC)
```

```python
import jax
import jax.numpy as jnp
from jax import lax
from jax.experimental import pallas as pl
from jax.experimental.pallas import tpu as pltpu
from jax.sharding import PartitionSpec as P

KIDS = 4
GROUP = 4
HIGH = lax.Precision.HIGH


def shifted_ring(value, axis, step):
    count = lax.axis_size(axis)
    return lax.ppermute(value, axis, [(i, (i + step) % count) for i in range(count)])


def complex_times(left_side, right_side):
    real_part = (
        left_side[..., 0, :, :] * right_side[..., 0, :, :]
        - left_side[..., 1, :, :] * right_side[..., 1, :, :]
    )
    imag_part = (
        left_side[..., 0, :, :] * right_side[..., 1, :, :]
        + left_side[..., 1, :, :] * right_side[..., 0, :, :]
    )
    return jnp.stack([real_part, imag_part], axis=-3)


def band_table(theta_band, child_rows):
    parent_rows = theta_band.shape[0]
    row_index = jnp.arange(parent_rows, dtype=jnp.int32)
    column_index = jnp.arange(child_rows + 8, dtype=jnp.int32)
    table = jnp.zeros((parent_rows, child_rows + 8), jnp.float32)
    for tap_index in range(8):
        target = row_index // 2 + tap_index + 1
        hits = (column_index[None, :] == target[:, None]).astype(jnp.float32)
        table = table + theta_band[:, tap_index][:, None] * hits
    return table


def translate_kernel(source_ref, offset_ref, count_ref, field_ref, operator_ref, out_ref):
    parents = out_ref.shape[0]

    def one_parent(parent, carry):
        count = count_ref[parent]

        def some_slots(step, sums):
            sums = list(sums)
            for lane in range(GROUP):
                slot = step * GROUP + lane
                source = source_ref[parent, slot]
                offset = offset_ref[parent, slot]
                live = (slot < count).astype(jnp.float32)
                real = operator_ref[offset, 0] * live
                imag = operator_ref[offset, 1] * live
                for pol in range(2):
                    a = field_ref[source, pol * 2]
                    b = field_ref[source, pol * 2 + 1]
                    sums[pol * 2] = sums[pol * 2] + (real * a - imag * b)
                    sums[pol * 2 + 1] = sums[pol * 2 + 1] + (real * b + imag * a)
            return tuple(sums)

        zero = jnp.zeros(out_ref.shape[2:], jnp.float32)
        sums = lax.fori_loop(0, (count + GROUP - 1) // GROUP, some_slots, (zero,) * 4)
        for index in range(4):
            out_ref[parent, index] = sums[index]
        return carry

    lax.fori_loop(0, parents, one_parent, 0)


def translate(field, operators, far_source, far_offset, far_count):
    smem = pl.BlockSpec(memory_space=pltpu.SMEM)
    vmem = pl.BlockSpec(memory_space=pltpu.VMEM)
    return pl.pallas_call(
        translate_kernel,
        out_shape=jax.ShapeDtypeStruct(field.shape, jnp.float32),
        in_specs=[smem, smem, smem, vmem, vmem],
        out_specs=vmem,
        name="translate",
    )(far_source, far_offset, far_count, field, operators)


def on_device(
    children, theta_band, phi_interp, child_shift, translators, far_source, far_offset, far_count
):
    child_rows = children.shape[3]
    groups = lax.axis_size("clus")
    strips = lax.axis_size("theta")
    strip = lax.axis_index("theta")
    parents_here = children.shape[0] // KIDS
    rows = translators.shape[2]
    blocks = translators.shape[3] // 128
    first = (strip > 0).astype(jnp.float32)
    last = (strip < strips - 1).astype(jnp.float32)
    table = band_table(theta_band, child_rows)
    above = shifted_ring(children[:, :, :, child_rows - 4 :], "theta", 1) * first
    below = shifted_ring(children[:, :, :, :4], "theta", -1) * last
    padded = jnp.concatenate([above, children, below], axis=3)
    spread = jnp.einsum("rj,...jq->...rq", table, padded, precision=HIGH)
    fine = jnp.einsum("...q,qp->...p", spread, phi_interp, precision=HIGH)
    grouped = fine.reshape((parents_here, KIDS) + fine.shape[1:])
    parents = jnp.sum(complex_times(child_shift[None, :, None], grouped), axis=1)
    packed = parents.reshape(parents_here, 2, 2, groups, rows, blocks, 128)
    packed = packed.transpose(3, 0, 1, 2, 5, 4, 6).reshape(groups, parents_here, 4, 8, 128)
    field = lax.all_to_all(packed, "clus", 0, 0).reshape(groups * parents_here, 4, 8, 128)
    operators = translators.reshape(-1, 2, rows, blocks, 128).transpose(0, 1, 3, 2, 4)
    operators = operators.reshape(-1, 2, 8, 128)
    summed = translate(field, operators, far_source, far_offset, far_count)
    summed = summed.reshape(groups, parents_here, 4, 8, 128)
    local = lax.all_to_all(summed, "clus", 0, 0)
    local = local.reshape(groups, parents_here, 2, 2, blocks, rows, 128)
    local = local.transpose(1, 2, 3, 0, 5, 4, 6).reshape(parents.shape)
    conjugate = jnp.stack([child_shift[:, 0], -child_shift[:, 1]], axis=1)
    shifted = complex_times(conjugate[None, :, None], local[:, None])
    shifted = shifted.reshape((parents_here * KIDS,) + shifted.shape[2:])
    back_phi = jnp.einsum("...p,qp->...q", shifted, phi_interp, precision=HIGH)
    extended = jnp.einsum("rj,...rq->...jq", table, back_phi, precision=HIGH)
    own_part = extended[..., 4 : 4 + child_rows, :]
    from_below = shifted_ring(extended[..., child_rows + 4 :, :], "theta", 1) * first
    from_above = shifted_ring(extended[..., :4, :], "theta", -1) * last
    lead = [(0, 0)] * (own_part.ndim - 2)
    result = own_part + jnp.pad(from_below, lead + [(0, child_rows - 4), (0, 0)])
    result = result + jnp.pad(from_above, lead + [(child_rows - 4, 0), (0, 0)])
    return result


def solution(mesh):
    return jax.shard_map(
        on_device,
        mesh=mesh,
        in_specs=(
            P("clus", None, None, "theta", None),
            P("theta", None),
            P(),
            P(None, None, "theta", None),
            P(None, None, ("theta", "clus"), None),
            P(),
            P(),
            P(),
        ),
        out_specs=P("clus", None, None, "theta", None),
        check_vma=False,
    )
```

```python
import jax
import jax.numpy as jnp
from jax import lax
from jax.experimental import pallas as pl
from jax.experimental.pallas import tpu as pltpu
from jax.sharding import PartitionSpec as P

KIDS = 4
LIST = 32
GROUP = 4
HIGH = lax.Precision.HIGH


def shifted_ring(value, axis, step):
    count = lax.axis_size(axis)
    return lax.ppermute(value, axis, [(i, (i + step) % count) for i in range(count)])


def complex_times(left_side, right_side):
    real_part = (
        left_side[..., 0, :, :] * right_side[..., 0, :, :]
        - left_side[..., 1, :, :] * right_side[..., 1, :, :]
    )
    imag_part = (
        left_side[..., 0, :, :] * right_side[..., 1, :, :]
        + left_side[..., 1, :, :] * right_side[..., 0, :, :]
    )
    return jnp.stack([real_part, imag_part], axis=-3)


def band_table(theta_band, child_rows):
    parent_rows = theta_band.shape[0]
    row_index = jnp.arange(parent_rows, dtype=jnp.int32)
    column_index = jnp.arange(child_rows + 8, dtype=jnp.int32)
    table = jnp.zeros((parent_rows, child_rows + 8), jnp.float32)
    for tap_index in range(8):
        target = row_index // 2 + tap_index + 1
        hits = (column_index[None, :] == target[:, None]).astype(jnp.float32)
        table = table + theta_band[:, tap_index][:, None] * hits
    return table


def translate_kernel(source_ref, offset_ref, steps_ref, field_ref, operator_ref, out_ref):
    pairs = steps_ref.shape[0]

    def one_pair(pair, carry):
        def some_slots(step, sums):
            sums = list(sums)
            for member in range(2):
                for lane in range(GROUP):
                    slot = pair * (2 * LIST) + step * GROUP + (member * LIST + lane)
                    source = pl.multiple_of(source_ref[slot], 8)
                    offset = pl.multiple_of(offset_ref[slot], 8)
                    real = operator_ref[pl.ds(offset, 8), :]
                    imag = operator_ref[pl.ds(offset + 8, 8), :]
                    for pol in range(2):
                        at = member * 4 + pol * 2
                        a = field_ref[pl.ds(source + pol * 16, 8), :]
                        b = field_ref[pl.ds(source + (pol * 16 + 8), 8), :]
                        sums[at] = sums[at] + (real * a - imag * b)
                        sums[at + 1] = sums[at + 1] + (real * b + imag * a)
            return tuple(sums)

        zero = jnp.zeros((8, 128), jnp.float32)
        sums = lax.fori_loop(0, steps_ref[pair], some_slots, (zero,) * 8)
        for index in range(8):
            out_ref[pl.ds(pl.multiple_of(pair * 64 + index * 8, 8), 8), :] = sums[index]
        return carry

    lax.fori_loop(0, pairs, one_pair, 0)


def translate(field, translators, far_source, far_offset, far_count):
    parents, slots = far_source.shape
    kinds, _, rows, samples = translators.shape
    operators = translators.reshape(kinds, 2, rows, samples // 128, 128).transpose(0, 1, 3, 2, 4)
    operators = jnp.pad(operators.reshape(kinds * 16, 128), ((0, 16), (0, 0)))
    live = jnp.arange(slots, dtype=jnp.int32)[None, :] < far_count[:, None]
    source = (far_source * 32).reshape(-1)
    offset = (jnp.where(live, far_offset, kinds) * 16).reshape(-1)
    longest = jnp.max(far_count.reshape(parents // 2, 2), axis=1)
    steps = (longest + (GROUP - 1)) // GROUP
    smem = pl.BlockSpec(memory_space=pltpu.SMEM)
    vmem = pl.BlockSpec(memory_space=pltpu.VMEM)
    return pl.pallas_call(
        translate_kernel,
        out_shape=jax.ShapeDtypeStruct((parents * 32, 128), jnp.float32),
        in_specs=[smem, smem, smem, vmem, vmem],
        out_specs=vmem,
        name="translate",
    )(source, offset, steps, field.reshape(parents * 32, 128), operators)


def on_device(
    children, theta_band, phi_interp, child_shift, translators, far_source, far_offset, far_count
):
    child_rows = children.shape[3]
    groups = lax.axis_size("clus")
    strips = lax.axis_size("theta")
    strip = lax.axis_index("theta")
    parents_here = children.shape[0] // KIDS
    rows = translators.shape[2]
    blocks = translators.shape[3] // 128
    first = (strip > 0).astype(jnp.float32)
    last = (strip < strips - 1).astype(jnp.float32)
    table = band_table(theta_band, child_rows)
    own_table = table[:, 4 : 4 + child_rows]
    edge_table = jnp.concatenate([table[:8], table[-8:]], axis=0)
    edge_table = jnp.concatenate([edge_table[:, :4], edge_table[:, -4:]], axis=1)
    edge_shift = jnp.concatenate([child_shift[:, :, :8], child_shift[:, :, -8:]], axis=2)
    above = shifted_ring(children[:, :, :, child_rows - 4 :], "theta", 1) * first
    below = shifted_ring(children[:, :, :, :4], "theta", -1) * last

    def pack(parents):
        strips_in = parents.shape[3] // rows
        packed = parents.reshape(parents_here, 2, 2, strips_in, rows, blocks, 128)
        packed = packed.transpose(3, 0, 1, 2, 5, 4, 6)
        return packed.reshape(strips_in, parents_here, 4, 8, 128)

    def unpack(packed):
        strips_in = packed.shape[0]
        local = packed.reshape(strips_in, parents_here, 2, 2, blocks, rows, 128)
        local = local.transpose(1, 2, 3, 0, 5, 4, 6)
        return local.reshape(parents_here, 2, 2, strips_in * rows, blocks * 128)

    def gathered(fine, shift):
        grouped = fine.reshape((parents_here, KIDS) + fine.shape[1:])
        return pack(jnp.sum(complex_times(shift[None, :, None], grouped), axis=1))

    def scattered(packed, shift):
        conjugate = jnp.stack([shift[:, 0], -shift[:, 1]], axis=1)
        shifted = complex_times(conjugate[None, :, None], unpack(packed)[:, None])
        return shifted.reshape((parents_here * KIDS,) + shifted.shape[2:])

    spread = jnp.einsum("rj,...jq->...rq", own_table, children, precision=HIGH)
    fine = jnp.einsum("...q,qp->...p", spread, phi_interp, precision=HIGH)
    packed = gathered(fine, child_shift)
    edge = jnp.concatenate([above, below], axis=3)
    edge_fine = jnp.einsum("...q,qp->...p", edge, phi_interp, precision=HIGH)
    edge_fine = jnp.einsum("rj,...jp->...rp", edge_table, edge_fine, precision=HIGH)
    edge_packed = gathered(edge_fine, edge_shift)
    half = edge_packed.shape[0] // 2
    packed = jnp.concatenate(
        [packed[:half] + edge_packed[:half], packed[half:-half], packed[-half:] + edge_packed[half:]]
    )
    field = lax.all_to_all(packed, "clus", 0, 0)
    summed = translate(field, translators, far_source, far_offset, far_count)
    summed = summed.reshape(groups, parents_here, 4, 8, 128)
    local = lax.all_to_all(summed, "clus", 0, 0)
    edge_local = jnp.concatenate([local[:half], local[-half:]])
    edge_shifted = scattered(edge_local, edge_shift)
    edge_back = jnp.einsum("rj,...rp->...jp", edge_table, edge_shifted, precision=HIGH)
    edge_back = jnp.einsum("...p,qp->...q", edge_back, phi_interp, precision=HIGH)
    from_below = shifted_ring(edge_back[..., 4:, :], "theta", 1) * first
    from_above = shifted_ring(edge_back[..., :4, :], "theta", -1) * last
    back_phi = jnp.einsum("...p,qp->...q", scattered(local, child_shift), phi_interp, precision=HIGH)
    own_part = jnp.einsum("rj,...rq->...jq", own_table, back_phi, precision=HIGH)
    lead = [(0, 0)] * (own_part.ndim - 2)
    result = own_part + jnp.pad(from_below, lead + [(0, child_rows - 4), (0, 0)])
    result = result + jnp.pad(from_above, lead + [(child_rows - 4, 0), (0, 0)])
    return result


def solution(mesh):
    return jax.shard_map(
        on_device,
        mesh=mesh,
        in_specs=(
            P("clus", None, None, "theta", None),
            P("theta", None),
            P(),
            P(None, None, "theta", None),
            P(None, None, ("theta", "clus"), None),
            P(),
            P(),
            P(),
        ),
        out_specs=P("clus", None, None, "theta", None),
        check_vma=False,
    )
```

```python
import jax
import jax.numpy as jnp
from jax import lax
from jax.experimental import pallas as pl
from jax.experimental.pallas import tpu as pltpu
from jax.sharding import PartitionSpec as P

KIDS = 4
LIST = 32
GROUP = 4
PLANES = 32
ROWS = 32
OWN = 16
PHI = 256
SAMPLES = 512
HALF = jnp.bfloat16
WHOLE = jnp.float32


def shifted_ring(value, axis, step):
    count = lax.axis_size(axis)
    return lax.ppermute(value, axis, [(i, (i + step) % count) for i in range(count)])


def halves(value):
    high = value.astype(HALF)
    return high, (value - high.astype(WHOLE)).astype(HALF)


def dot3(left, right, contract=0):
    dims = (((1,), (contract,)), ((), ()))
    total = None
    for a, b in ((0, 0), (0, 1), (1, 0)):
        part = lax.dot_general(left[a], right[b], dims, preferred_element_type=WHOLE)
        total = part if total is None else total + part
    return total


def swap_blocks(tiles):
    sub = lax.broadcasted_iota(jnp.int32, (8, 128), 0)
    even = (sub // 2) % 2 == 0
    low = sub < 4
    a, b, c, d = tiles

    def step(first, second, shift, mask):
        one = jnp.where(mask, first, pltpu.roll(second, shift, 0))
        two = jnp.where(mask, pltpu.roll(first, 8 - shift, 0), second)
        return one, two

    a, b = step(a, b, 2, even)
    c, d = step(c, d, 2, even)
    a, c = step(a, c, 4, low)
    b, d = step(b, d, 4, low)
    return a, b, c, d


def lane_blocks(value):
    return [value[:, 128 * i : 128 * (i + 1)] for i in range(4)]


def band_tables(bands, planes, inner, outer, edge):
    shape = (planes * inner, planes * outer)
    row = lax.broadcasted_iota(jnp.int32, shape, 0)
    column = lax.broadcasted_iota(jnp.int32, shape, 1)
    child = row % inner
    parent = column % outer
    if edge:
        child = jnp.where(child < 4, child - 4, child + 12)
        parent = jnp.where(parent < 8, parent, parent + 16)
    tap = child - parent // 2 + 3
    tap = jnp.where(row // inner == column // outer, tap, -1)
    table = jnp.zeros(shape, WHOLE)
    for t in range(8):
        table = jnp.where(tap == t, jnp.broadcast_to(bands[t : t + 1], shape), table)
    return table


def own_forward_kernel(
    bands_ref, children_ref, phi_ref, shift_ref,
    packed_ref, phi_high_ref, phi_low_ref, edge_high_ref, edge_low_ref,
    back_high_ref, back_low_ref, edge_back_high_ref, edge_back_low_ref, fine_ref,
):
    phi = halves(phi_ref[...])
    phi_high_ref[...], phi_low_ref[...] = phi
    table = band_tables(bands_ref[:, :256], 8, 16, 32, False)
    back_high_ref[...], back_low_ref[...] = halves(table)
    own = halves(table.T)
    table = band_tables(bands_ref[:, 256:], 16, 8, 16, True)
    edge_back_high_ref[...], edge_back_low_ref[...] = halves(table)
    edge_high_ref[...], edge_low_ref[...] = halves(table.T)
    for group in range(4):
        rows = slice(128 * group, 128 * (group + 1))
        mixed = dot3(halves(children_ref[rows]), phi)
        fine_ref[256 * group : 256 * (group + 1)] = dot3(own, halves(mixed))
    for parent in range(2):
        for pol in range(2):
            for block in range(4):
                rows = slice(8 * block, 8 * (block + 1))
                real, imag = gathered(fine_ref, shift_ref, parent, pol, 32, 8 * block, rows)
                for part, value in enumerate((real, imag)):
                    for pair, tile in enumerate(swap_blocks(lane_blocks(value))):
                        packed_ref[4 * block + pair, parent, 2 * pol + part] = tile


def gathered(fine_ref, shift_ref, parent, pol, per_plane, first, rows):
    real = imag = None
    for kid in range(KIDS):
        at = ((parent * KIDS + kid) * 4 + pol * 2) * per_plane + first
        a = fine_ref[at : at + 8]
        b = fine_ref[at + per_plane : at + per_plane + 8]
        c = shift_ref[kid, 0, rows]
        d = shift_ref[kid, 1, rows]
        one, two = c * a - d * b, c * b + d * a
        real = one if real is None else real + one
        imag = two if imag is None else imag + two
    return real, imag


def edge_forward_kernel(
    above_ref, below_ref, phi_high_ref, phi_low_ref, edge_high_ref, edge_low_ref, shift_ref,
    packed_ref, out_ref, halo_ref, fine_ref, edge_ref, sems,
):
    middle = pltpu.make_async_copy(packed_ref.at[4:12], out_ref.at[4:12], sems.at[0])
    middle.start()
    for plane in range(PLANES):
        halo_ref[8 * plane : 8 * plane + 4] = above_ref[plane]
        halo_ref[8 * plane + 4 : 8 * plane + 8] = below_ref[plane]
    phi = (phi_high_ref[...], phi_low_ref[...])
    edge = (edge_high_ref[...], edge_low_ref[...])
    for parent in range(2):
        mixed = dot3(halves(halo_ref[128 * parent : 128 * (parent + 1)]), phi)
        fine_ref[256 * parent : 256 * (parent + 1)] = dot3(edge, halves(mixed))
    copies = []
    for side in range(2):
        rows = slice(24 * side, 24 * side + 8)
        for parent in range(2):
            for pol in range(2):
                real, imag = gathered(fine_ref, shift_ref, parent, pol, 16, 8 * side, rows)
                for part, value in enumerate((real, imag)):
                    for pair, tile in enumerate(swap_blocks(lane_blocks(value))):
                        own = packed_ref[12 * side + pair, parent, 2 * pol + part]
                        edge_ref[4 * side + pair, parent, 2 * pol + part] = own + tile
        target = out_ref.at[12 * side : 12 * side + 4]
        copy = pltpu.make_async_copy(edge_ref.at[4 * side : 4 * side + 4], target, sems.at[1 + side])
        copy.start()
        copies.append(copy)
    middle.wait()
    for copy in copies:
        copy.wait()


def spread_back(local_ref, shift_ref, parent, pol, blocks, store):
    parts = []
    for part in range(2):
        pieces = []
        for first in blocks:
            tiles = [local_ref[first + pair, parent, 2 * pol + part] for pair in range(4)]
            pieces.append(jnp.concatenate(swap_blocks(tiles), axis=1))
        parts.append(pieces)
    for kid in range(KIDS):
        real, imag = [], []
        for index, first in enumerate(blocks):
            a, b = parts[0][index], parts[1][index]
            c = shift_ref[kid, 0, 2 * first : 2 * first + 8]
            d = shift_ref[kid, 1, 2 * first : 2 * first + 8]
            real.append(c * a + d * b)
            imag.append(c * b - d * a)
        plane = (parent * KIDS + kid) * 4 + pol * 2
        store(plane, halves(jnp.concatenate(real, axis=0)))
        store(plane + 1, halves(jnp.concatenate(imag, axis=0)))


def edge_back_kernel(
    local_ref, shift_ref, phi_high_ref, phi_low_ref, table_high_ref, table_low_ref,
    up_ref, down_ref, high_ref, low_ref,
):
    phi = (phi_high_ref[...], phi_low_ref[...])
    table = (table_high_ref[...], table_low_ref[...])

    def store(plane, value):
        high_ref[16 * plane : 16 * plane + 16], low_ref[16 * plane : 16 * plane + 16] = value

    for parent in range(2):
        for pol in range(2):
            spread_back(local_ref, shift_ref, parent, pol, (0, 12), store)
        rows = slice(256 * parent, 256 * (parent + 1))
        narrowed = dot3(table, (high_ref[rows], low_ref[rows]))
        result = dot3(halves(narrowed), phi, contract=1)
        for plane in range(16):
            up_ref[16 * parent + plane] = result[8 * plane : 8 * plane + 4]
            down_ref[16 * parent + plane] = result[8 * plane + 4 : 8 * plane + 8]


def own_back_kernel(
    local_ref, shift_ref, phi_high_ref, phi_low_ref, table_high_ref, table_low_ref,
    own_ref, high_ref, low_ref,
):
    phi = (phi_high_ref[...], phi_low_ref[...])
    table = (table_high_ref[...], table_low_ref[...])

    def store(plane, value):
        high_ref[32 * plane : 32 * plane + 32], low_ref[32 * plane : 32 * plane + 32] = value

    for parent in range(2):
        for pol in range(2):
            spread_back(local_ref, shift_ref, parent, pol, (0, 4, 8, 12), store)
        for group in (2 * parent, 2 * parent + 1):
            rows = slice(256 * group, 256 * (group + 1))
            narrowed = dot3(table, (high_ref[rows], low_ref[rows]))
            own_ref[128 * group : 128 * (group + 1)] = dot3(halves(narrowed), phi, contract=1)


def translate_kernel(source_ref, offset_ref, steps_ref, field_ref, operator_ref, out_ref):
    pairs = out_ref.shape[0] // 64
    start = pl.program_id(0) * pairs

    def one_pair(index, carry):
        pair = start + index

        def some_slots(step, sums):
            sums = list(sums)
            for member in range(2):
                for lane in range(GROUP):
                    slot = pair * (2 * LIST) + step * GROUP + (member * LIST + lane)
                    source = pl.multiple_of(source_ref[slot], 8)
                    offset = pl.multiple_of(offset_ref[slot], 8)
                    real = operator_ref[pl.ds(offset, 8), :]
                    imag = operator_ref[pl.ds(offset + 8, 8), :]
                    for pol in range(2):
                        at = member * 4 + pol * 2
                        a = field_ref[pl.ds(source + pol * 16, 8), :]
                        b = field_ref[pl.ds(source + (pol * 16 + 8), 8), :]
                        sums[at] = sums[at] + (real * a - imag * b)
                        sums[at + 1] = sums[at + 1] + (real * b + imag * a)
            return tuple(sums)

        zero = jnp.zeros((8, 128), jnp.float32)
        sums = lax.fori_loop(0, steps_ref[pair], some_slots, (zero,) * 8)
        for part in range(8):
            out_ref[pl.ds(pl.multiple_of(index * 64 + part * 8, 8), 8), :] = sums[part]
        return carry

    lax.fori_loop(0, pairs, one_pair, 0)


def in_vmem(value):
    return pltpu.with_memory_space_constraint(value, pltpu.VMEM)


def call(kernel, name, outs, scratch, *operands, out_specs=None):
    vmem = pl.BlockSpec(memory_space=pltpu.VMEM)
    return pl.pallas_call(
        kernel,
        out_shape=outs,
        in_specs=[vmem] * len(operands),
        out_specs=out_specs if out_specs is not None else jax.tree.map(lambda _: vmem, outs),
        scratch_shapes=scratch,
        name=name,
    )(*[in_vmem(operand) for operand in operands])


def translate(field, translators, far_source, far_offset, far_count):
    parents, slots = far_source.shape
    kinds, _, rows, samples = translators.shape
    operators = translators.reshape(kinds, 2, rows, samples // 128, 128).transpose(0, 1, 3, 2, 4)
    operators = jnp.pad(operators.reshape(kinds * 16, 128), ((0, 16), (0, 0)))
    live = jnp.arange(slots, dtype=jnp.int32)[None, :] < far_count[:, None]
    source = (far_source * 32).reshape(-1)
    offset = (jnp.where(live, far_offset, kinds) * 16).reshape(-1)
    longest = jnp.max(far_count.reshape(parents // 2, 2), axis=1)
    steps = (longest + (GROUP - 1)) // GROUP
    smem = pl.BlockSpec(memory_space=pltpu.SMEM)
    vmem = pl.BlockSpec(memory_space=pltpu.VMEM)
    return pl.pallas_call(
        translate_kernel,
        grid=(4,),
        out_shape=jax.ShapeDtypeStruct((parents * 32, 128), jnp.float32),
        in_specs=[smem, smem, smem, vmem, vmem],
        out_specs=pl.BlockSpec((parents * 8, 128), lambda i: (i, 0)),
        name="translate",
    )(source, offset, steps, in_vmem(field.reshape(parents * 32, 128)), in_vmem(operators))


def on_device(
    children, theta_band, phi_interp, child_shift, translators, far_source, far_offset, far_count
):
    strips = lax.axis_size("theta")
    strip = lax.axis_index("theta")
    first = (strip > 0).astype(jnp.float32)
    last = (strip < strips - 1).astype(jnp.float32)
    planes = children.reshape(PLANES, OWN, PHI)
    above = shifted_ring(planes[:, OWN - 4 :], "theta", 1)
    below = shifted_ring(planes[:, :4], "theta", -1)
    taps = theta_band.T
    edge_taps = jnp.concatenate([taps[:, :8] * first, taps[:, -8:] * last], axis=1)
    bands = jnp.concatenate([jnp.tile(taps, (1, 8)), jnp.tile(edge_taps, (1, 16))], axis=1)
    half = lambda *shape: pltpu.VMEM(shape, HALF)
    whole = lambda *shape: pltpu.VMEM(shape, WHOLE)
    tables = (half(256, 512),) * 2 + (half(256, 128),) * 2 + (half(128, 256),) * 4
    packed, phi_high, phi_low, edge_high, edge_low, *backs = call(
        own_forward_kernel, "own_forward", (whole(16, 2, 4, 8, 128),) + tables,
        [whole(1024, SAMPLES)], bands, planes.reshape(-1, PHI), phi_interp, child_shift,
    )
    packed = call(
        edge_forward_kernel, "edge_forward", jax.ShapeDtypeStruct((16, 2, 4, 8, 128), WHOLE),
        [whole(256, PHI), whole(512, SAMPLES), whole(8, 2, 4, 8, 128), pltpu.SemaphoreType.DMA((3,))],
        above, below, phi_high, phi_low, edge_high, edge_low, child_shift, packed,
        out_specs=pl.BlockSpec(memory_space=pl.ANY),
    )
    field = lax.all_to_all(packed, "clus", 0, 0)
    summed = translate(field, translators, far_source, far_offset, far_count)
    local = lax.all_to_all(summed.reshape(packed.shape), "clus", 0, 0)
    up, down = call(
        edge_back_kernel, "edge_back", (whole(PLANES, 4, PHI),) * 2,
        [half(512, SAMPLES)] * 2, local, child_shift, phi_high, phi_low, backs[2], backs[3],
    )
    from_below = shifted_ring(down, "theta", 1)
    from_above = shifted_ring(up, "theta", -1)
    own = call(
        own_back_kernel, "own_back", whole(PLANES * OWN, PHI),
        [half(1024, SAMPLES)] * 2, local, child_shift, phi_high, phi_low, backs[0], backs[1],
    ).reshape(planes.shape)
    result = own + jnp.pad(from_below, ((0, 0), (0, OWN - 4), (0, 0)))
    result = result + jnp.pad(from_above, ((0, 0), (OWN - 4, 0), (0, 0)))
    return result.reshape(children.shape)


def solution(mesh):
    return jax.shard_map(
        on_device,
        mesh=mesh,
        in_specs=(
            P("clus", None, None, "theta", None),
            P("theta", None),
            P(),
            P(None, None, "theta", None),
            P(None, None, ("theta", "clus"), None),
            P(),
            P(),
            P(),
        ),
        out_specs=P("clus", None, None, "theta", None),
        check_vma=False,
    )
```

```python
import jax
import jax.numpy as jnp
from jax import lax
from jax.experimental import pallas as pl
from jax.experimental.pallas import tpu as pltpu
from jax.sharding import PartitionSpec as P

KIDS = 4
LIST = 32
GROUP = 4
PLANES = 32
ROWS = 32
OWN = 16
PHI = 256
SAMPLES = 512
GRANT = 12 * 2**20
HALF = jnp.bfloat16
WHOLE = jnp.float32


def shifted_ring(value, axis, step):
    count = lax.axis_size(axis)
    return lax.ppermute(value, axis, [(i, (i + step) % count) for i in range(count)])


def halves(value):
    high = value.astype(HALF)
    return high, (value - high.astype(WHOLE)).astype(HALF)


def dot3(left, right, contract=0):
    dims = (((1,), (contract,)), ((), ()))
    total = None
    for a, b in ((0, 0), (0, 1), (1, 0)):
        part = lax.dot_general(left[a], right[b], dims, preferred_element_type=WHOLE)
        total = part if total is None else total + part
    return total


def swap_blocks(tiles):
    sub = lax.broadcasted_iota(jnp.int32, (8, 128), 0)
    even = (sub // 2) % 2 == 0
    low = sub < 4
    a, b, c, d = tiles

    def step(first, second, shift, mask):
        one = jnp.where(mask, first, pltpu.roll(second, shift, 0))
        two = jnp.where(mask, pltpu.roll(first, 8 - shift, 0), second)
        return one, two

    a, b = step(a, b, 2, even)
    c, d = step(c, d, 2, even)
    a, c = step(a, c, 4, low)
    b, d = step(b, d, 4, low)
    return a, b, c, d


def lane_blocks(value):
    return [value[:, 128 * i : 128 * (i + 1)] for i in range(4)]


def tiled(bands, outer):
    row = lax.broadcasted_iota(jnp.int32, (outer, 256), 0)
    column = lax.broadcasted_iota(jnp.int32, (outer, 256), 1)
    pick = (row == column % outer).astype(HALF)
    return [jnp.dot(part, pick, preferred_element_type=WHOLE) for part in halves(bands)]


def band_tables(bands, planes, inner, outer, edge):
    shape = (planes * inner, planes * outer)
    row = lax.broadcasted_iota(jnp.int32, shape, 0)
    column = lax.broadcasted_iota(jnp.int32, shape, 1)
    child = row % inner
    parent = column % outer
    if edge:
        child = jnp.where(child < 4, child - 4, child + 12)
        parent = jnp.where(parent < 8, parent, parent + 16)
    tap = child - parent // 2 + 3
    tap = jnp.where(row // inner == column // outer, tap, -1)
    tables = []
    for part in tiled(bands, outer):
        table = jnp.zeros(shape, WHOLE)
        for t in range(8):
            table = jnp.where(tap == t, jnp.broadcast_to(part[t : t + 1], shape), table)
        tables.append(table)
    return tables


def own_forward_kernel(
    taps_hbm, children_hbm, phi_hbm, shift_ref,
    packed_ref, phi_high_ref, phi_low_ref, edge_high_ref, edge_low_ref,
    back_high_ref, back_low_ref, edge_back_high_ref, edge_back_low_ref,
    fine_ref, taps_ref, phi_ref, children_ref, sems,
):
    pairs = ((taps_hbm, taps_ref), (phi_hbm, phi_ref), (children_hbm, children_ref))
    copies = [pltpu.make_async_copy(*pair, sems.at[i]) for i, pair in enumerate(pairs)]
    for copy in copies:
        copy.start()
    strip = lax.axis_index("theta")
    first = (strip > 0).astype(WHOLE)
    last = (strip < lax.axis_size("theta") - 1).astype(WHOLE)
    copies[0].wait()
    taps = taps_ref[...]
    table = band_tables(taps, 8, 16, 32, False)
    own = []
    for part, ref in zip(table, (back_high_ref, back_low_ref)):
        ref[...] = part.astype(HALF)
        own.append(part.T.astype(HALF))
    taps = jnp.concatenate([taps[:, :8] * first, taps[:, ROWS - 8 :] * last], axis=1)
    table = band_tables(taps, 16, 8, 16, True)
    refs = ((edge_back_high_ref, edge_high_ref), (edge_back_low_ref, edge_low_ref))
    for part, (back_ref, ref) in zip(table, refs):
        back_ref[...] = part.astype(HALF)
        ref[...] = part.T.astype(HALF)
    copies[1].wait()
    phi = halves(phi_ref[...])
    phi_high_ref[...], phi_low_ref[...] = phi
    copies[2].wait()
    for group in range(4):
        rows = slice(128 * group, 128 * (group + 1))
        mixed = dot3(halves(children_ref[rows]), phi)
        fine_ref[256 * group : 256 * (group + 1)] = dot3(own, halves(mixed))
    for parent in range(2):
        for pol in range(2):
            for block in range(4):
                rows = slice(8 * block, 8 * (block + 1))
                real, imag = gathered(fine_ref, shift_ref, parent, pol, 32, 8 * block, rows)
                for part, value in enumerate((real, imag)):
                    for pair, tile in enumerate(swap_blocks(lane_blocks(value))):
                        packed_ref[4 * block + pair, parent, 2 * pol + part] = tile


def gathered(fine_ref, shift_ref, parent, pol, per_plane, first, rows):
    real = imag = None
    for kid in range(KIDS):
        at = ((parent * KIDS + kid) * 4 + pol * 2) * per_plane + first
        a = fine_ref[at : at + 8]
        b = fine_ref[at + per_plane : at + per_plane + 8]
        c = shift_ref[kid, 0, rows]
        d = shift_ref[kid, 1, rows]
        one, two = c * a - d * b, c * b + d * a
        real = one if real is None else real + one
        imag = two if imag is None else imag + two
    return real, imag


def edge_forward_kernel(
    above_ref, below_ref, phi_high_ref, phi_low_ref, edge_high_ref, edge_low_ref, shift_ref,
    packed_ref, out_ref, halo_ref, fine_ref, edge_ref, sems,
):
    middle = pltpu.make_async_copy(packed_ref.at[4:12], out_ref.at[4:12], sems.at[0])
    middle.start()
    for plane in range(PLANES):
        halo_ref[8 * plane : 8 * plane + 4] = above_ref[plane]
        halo_ref[8 * plane + 4 : 8 * plane + 8] = below_ref[plane]
    phi = (phi_high_ref[...], phi_low_ref[...])
    edge = (edge_high_ref[...], edge_low_ref[...])
    for parent in range(2):
        mixed = dot3(halves(halo_ref[128 * parent : 128 * (parent + 1)]), phi)
        fine_ref[256 * parent : 256 * (parent + 1)] = dot3(edge, halves(mixed))
    copies = []
    for side in range(2):
        rows = slice(24 * side, 24 * side + 8)
        for parent in range(2):
            for pol in range(2):
                real, imag = gathered(fine_ref, shift_ref, parent, pol, 16, 8 * side, rows)
                for part, value in enumerate((real, imag)):
                    for pair, tile in enumerate(swap_blocks(lane_blocks(value))):
                        own = packed_ref[12 * side + pair, parent, 2 * pol + part]
                        edge_ref[4 * side + pair, parent, 2 * pol + part] = own + tile
        target = out_ref.at[12 * side : 12 * side + 4]
        copy = pltpu.make_async_copy(edge_ref.at[4 * side : 4 * side + 4], target, sems.at[1 + side])
        copy.start()
        copies.append(copy)
    middle.wait()
    for copy in copies:
        copy.wait()


def spread_back(local_ref, shift_ref, parent, pol, blocks, store):
    parts = []
    for part in range(2):
        pieces = []
        for first in blocks:
            tiles = [local_ref[first + pair, parent, 2 * pol + part] for pair in range(4)]
            pieces.append(jnp.concatenate(swap_blocks(tiles), axis=1))
        parts.append(pieces)
    for kid in range(KIDS):
        real, imag = [], []
        for index, first in enumerate(blocks):
            a, b = parts[0][index], parts[1][index]
            c = shift_ref[kid, 0, 2 * first : 2 * first + 8]
            d = shift_ref[kid, 1, 2 * first : 2 * first + 8]
            real.append(c * a + d * b)
            imag.append(c * b - d * a)
        plane = (parent * KIDS + kid) * 4 + pol * 2
        store(plane, halves(jnp.concatenate(real, axis=0)))
        store(plane + 1, halves(jnp.concatenate(imag, axis=0)))


def edge_back_kernel(
    local_ref, shift_ref, phi_high_ref, phi_low_ref, table_high_ref, table_low_ref,
    up_ref, down_ref, high_ref, low_ref,
):
    phi = (phi_high_ref[...], phi_low_ref[...])
    table = (table_high_ref[...], table_low_ref[...])

    def store(plane, value):
        high_ref[16 * plane : 16 * plane + 16], low_ref[16 * plane : 16 * plane + 16] = value

    for parent in range(2):
        for pol in range(2):
            spread_back(local_ref, shift_ref, parent, pol, (0, 12), store)
        rows = slice(256 * parent, 256 * (parent + 1))
        narrowed = dot3(table, (high_ref[rows], low_ref[rows]))
        result = dot3(halves(narrowed), phi, contract=1)
        for plane in range(16):
            up_ref[16 * parent + plane] = result[8 * plane : 8 * plane + 4]
            down_ref[16 * parent + plane] = result[8 * plane + 4 : 8 * plane + 8]


def own_back_kernel(
    local_ref, shift_ref, phi_high_ref, phi_low_ref, table_high_ref, table_low_ref,
    own_ref, high_ref, low_ref,
):
    phi = (phi_high_ref[...], phi_low_ref[...])
    table = (table_high_ref[...], table_low_ref[...])

    def store(plane, value):
        high_ref[32 * plane : 32 * plane + 32], low_ref[32 * plane : 32 * plane + 32] = value

    for parent in range(2):
        for pol in range(2):
            spread_back(local_ref, shift_ref, parent, pol, (0, 4, 8, 12), store)
        for group in (2 * parent, 2 * parent + 1):
            rows = slice(256 * group, 256 * (group + 1))
            narrowed = dot3(table, (high_ref[rows], low_ref[rows]))
            own_ref[128 * group : 128 * (group + 1)] = dot3(halves(narrowed), phi, contract=1)


def translate_kernel(source_ref, offset_ref, steps_ref, field_ref, operator_ref, out_ref):
    pairs = out_ref.shape[0] // 64
    start = pl.program_id(0) * pairs

    def one_pair(index, carry):
        pair = start + index

        def some_slots(step, sums):
            sums = list(sums)
            for member in range(2):
                for lane in range(GROUP):
                    slot = pair * (2 * LIST) + step * GROUP + (member * LIST + lane)
                    source = pl.multiple_of(source_ref[slot], 8)
                    offset = pl.multiple_of(offset_ref[slot], 8)
                    real = operator_ref[pl.ds(offset, 8), :]
                    imag = operator_ref[pl.ds(offset + 8, 8), :]
                    for pol in range(2):
                        at = member * 4 + pol * 2
                        a = field_ref[pl.ds(source + pol * 16, 8), :]
                        b = field_ref[pl.ds(source + (pol * 16 + 8), 8), :]
                        sums[at] = sums[at] + (real * a - imag * b)
                        sums[at + 1] = sums[at + 1] + (real * b + imag * a)
            return tuple(sums)

        zero = jnp.zeros((8, 128), jnp.float32)
        sums = lax.fori_loop(0, steps_ref[pair], some_slots, (zero,) * 8)
        for part in range(8):
            out_ref[pl.ds(pl.multiple_of(index * 64 + part * 8, 8), 8), :] = sums[part]
        return carry

    lax.fori_loop(0, pairs, one_pair, 0)


def in_vmem(value):
    return pltpu.with_memory_space_constraint(value, pltpu.VMEM)


def in_hbm(value):
    return pltpu.with_memory_space_constraint(value, pltpu.HBM)


def call(kernel, name, outs, scratch, *operands, raw=0, out_specs=None):
    vmem = pl.BlockSpec(memory_space=pltpu.VMEM)
    hbm = pl.BlockSpec(memory_space=pltpu.HBM)
    return pl.pallas_call(
        kernel,
        out_shape=outs,
        in_specs=[hbm] * raw + [vmem] * (len(operands) - raw),
        out_specs=out_specs if out_specs is not None else jax.tree.map(lambda _: vmem, outs),
        scratch_shapes=scratch,
        compiler_params=pltpu.CompilerParams(vmem_limit_bytes=GRANT),
        name=name,
    )(*map(in_hbm, operands[:raw]), *map(in_vmem, operands[raw:]))


def translate(field, translators, far_source, far_offset, far_count):
    parents, slots = far_source.shape
    kinds, _, rows, samples = translators.shape
    operators = translators.reshape(kinds, 2, rows, samples // 128, 128).transpose(0, 1, 3, 2, 4)
    operators = jnp.pad(operators.reshape(kinds * 16, 128), ((0, 16), (0, 0)))
    live = jnp.arange(slots, dtype=jnp.int32)[None, :] < far_count[:, None]
    source = (far_source * 32).reshape(-1)
    offset = (jnp.where(live, far_offset, kinds) * 16).reshape(-1)
    longest = jnp.max(far_count.reshape(parents // 2, 2), axis=1)
    steps = (longest + (GROUP - 1)) // GROUP
    smem = pl.BlockSpec(memory_space=pltpu.SMEM)
    vmem = pl.BlockSpec(memory_space=pltpu.VMEM)
    return pl.pallas_call(
        translate_kernel,
        grid=(4,),
        out_shape=jax.ShapeDtypeStruct((parents * 32, 128), jnp.float32),
        in_specs=[smem, smem, smem, vmem, vmem],
        out_specs=pl.BlockSpec((parents * 8, 128), lambda i: (i, 0)),
        compiler_params=pltpu.CompilerParams(vmem_limit_bytes=GRANT),
        name="translate",
    )(source, offset, steps, in_vmem(field.reshape(parents * 32, 128)), in_vmem(operators))


def on_device(
    children, theta_band, phi_interp, child_shift, translators, far_source, far_offset, far_count
):
    planes = children.reshape(PLANES, OWN, PHI)
    above = shifted_ring(planes[:, OWN - 4 :], "theta", 1)
    below = shifted_ring(planes[:, :4], "theta", -1)
    half = lambda *shape: pltpu.VMEM(shape, HALF)
    whole = lambda *shape: pltpu.VMEM(shape, WHOLE)
    tables = (half(256, 512),) * 2 + (half(256, 128),) * 2 + (half(128, 256),) * 4
    packed, phi_high, phi_low, edge_high, edge_low, *backs = call(
        own_forward_kernel, "own_forward", (whole(16, 2, 4, 8, 128),) + tables,
        [
            whole(1024, SAMPLES), whole(8, ROWS), whole(PHI, SAMPLES), whole(PLANES * OWN, PHI),
            pltpu.SemaphoreType.DMA((3,)),
        ],
        theta_band.T, planes.reshape(-1, PHI), phi_interp, child_shift, raw=3,
    )
    packed = call(
        edge_forward_kernel, "edge_forward", jax.ShapeDtypeStruct((16, 2, 4, 8, 128), WHOLE),
        [whole(256, PHI), whole(512, SAMPLES), whole(8, 2, 4, 8, 128), pltpu.SemaphoreType.DMA((3,))],
        above, below, phi_high, phi_low, edge_high, edge_low, child_shift, packed,
        out_specs=pl.BlockSpec(memory_space=pl.ANY),
    )
    field = lax.all_to_all(packed, "clus", 0, 0)
    summed = translate(field, translators, far_source, far_offset, far_count)
    local = lax.all_to_all(summed.reshape(packed.shape), "clus", 0, 0)
    up, down = call(
        edge_back_kernel, "edge_back", (whole(PLANES, 4, PHI),) * 2,
        [half(512, SAMPLES)] * 2, local, child_shift, phi_high, phi_low, backs[2], backs[3],
    )
    from_below = shifted_ring(down, "theta", 1)
    from_above = shifted_ring(up, "theta", -1)
    own = call(
        own_back_kernel, "own_back", whole(PLANES * OWN, PHI),
        [half(1024, SAMPLES)] * 2, local, child_shift, phi_high, phi_low, backs[0], backs[1],
    ).reshape(planes.shape)
    result = own + jnp.pad(from_below, ((0, 0), (0, OWN - 4), (0, 0)))
    result = result + jnp.pad(from_above, ((0, 0), (OWN - 4, 0), (0, 0)))
    return result.reshape(children.shape)


def solution(mesh):
    return jax.shard_map(
        on_device,
        mesh=mesh,
        in_specs=(
            P("clus", None, None, "theta", None),
            P("theta", None),
            P(),
            P(None, None, "theta", None),
            P(None, None, ("theta", "clus"), None),
            P(),
            P(),
            P(),
        ),
        out_specs=P("clus", None, None, "theta", None),
        check_vma=False,
    )
```

```python
import jax
import jax.numpy as jnp
from jax import lax
from jax.experimental import pallas as pl
from jax.experimental.pallas import tpu as pltpu
from jax.sharding import PartitionSpec as P

KIDS = 4
LIST = 32
GROUP = 4
QUAD = 4
PLANES = 32
ROWS = 32
OWN = 16
PHI = 256
SAMPLES = 512
GRANT = 12 * 2**20
HALF = jnp.bfloat16
WHOLE = jnp.float32


def shifted_ring(value, axis, step):
    count = lax.axis_size(axis)
    return lax.ppermute(value, axis, [(i, (i + step) % count) for i in range(count)])


def halves(value):
    high = value.astype(HALF)
    return high, (value - high.astype(WHOLE)).astype(HALF)


def dot3(left, right, contract=0):
    dims = (((1,), (contract,)), ((), ()))
    total = None
    for a, b in ((0, 0), (0, 1), (1, 0)):
        part = lax.dot_general(left[a], right[b], dims, preferred_element_type=WHOLE)
        total = part if total is None else total + part
    return total


def swap_blocks(tiles):
    sub = lax.broadcasted_iota(jnp.int32, (8, 128), 0)
    even = (sub // 2) % 2 == 0
    low = sub < 4
    a, b, c, d = tiles

    def step(first, second, shift, mask):
        one = jnp.where(mask, first, pltpu.roll(second, shift, 0))
        two = jnp.where(mask, pltpu.roll(first, 8 - shift, 0), second)
        return one, two

    a, b = step(a, b, 2, even)
    c, d = step(c, d, 2, even)
    a, c = step(a, c, 4, low)
    b, d = step(b, d, 4, low)
    return a, b, c, d


def lane_blocks(value):
    return [value[:, 128 * i : 128 * (i + 1)] for i in range(4)]


def tiled(bands, outer):
    row = lax.broadcasted_iota(jnp.int32, (outer, 256), 0)
    column = lax.broadcasted_iota(jnp.int32, (outer, 256), 1)
    pick = (row == column % outer).astype(HALF)
    return [jnp.dot(part, pick, preferred_element_type=WHOLE) for part in halves(bands)]


def band_tables(bands, planes, inner, outer, edge):
    shape = (planes * inner, planes * outer)
    row = lax.broadcasted_iota(jnp.int32, shape, 0)
    column = lax.broadcasted_iota(jnp.int32, shape, 1)
    child = row % inner
    parent = column % outer
    if edge:
        child = jnp.where(child < 4, child - 4, child + 12)
        parent = jnp.where(parent < 8, parent, parent + 16)
    tap = child - parent // 2 + 3
    tap = jnp.where(row // inner == column // outer, tap, -1)
    tables = []
    for part in tiled(bands, outer):
        table = jnp.zeros(shape, WHOLE)
        for t in range(8):
            table = jnp.where(tap == t, jnp.broadcast_to(part[t : t + 1], shape), table)
        tables.append(table)
    return tables


def cut_kernel(children_hbm, children_ref, upper_ref, lower_ref, sems):
    chunks = [slice(8 * i, 8 * i + 8) for i in range(4)]
    copies = [
        pltpu.make_async_copy(children_hbm.at[chunk], children_ref.at[chunk], sems.at[i])
        for i, chunk in enumerate(chunks)
    ]
    for copy in copies:
        copy.start()
    for copy, chunk in zip(copies, chunks):
        copy.wait()
        upper_ref[chunk] = children_ref[chunk, :4]
        lower_ref[chunk] = children_ref[chunk, OWN - 4 :]


def own_forward_kernel(
    taps_hbm, phi_hbm, children_ref, shift_ref,
    packed_ref, phi_high_ref, phi_low_ref, edge_high_ref, edge_low_ref,
    back_high_ref, back_low_ref, edge_back_high_ref, edge_back_low_ref,
    fine_ref, taps_ref, phi_ref, sems,
):
    pairs = ((taps_hbm, taps_ref), (phi_hbm, phi_ref))
    copies = [pltpu.make_async_copy(*pair, sems.at[i]) for i, pair in enumerate(pairs)]
    for copy in copies:
        copy.start()
    strip = lax.axis_index("theta")
    first = (strip > 0).astype(WHOLE)
    last = (strip < lax.axis_size("theta") - 1).astype(WHOLE)
    copies[0].wait()
    taps = taps_ref[...]
    table = band_tables(taps, 8, 16, 32, False)
    own = []
    for part, ref in zip(table, (back_high_ref, back_low_ref)):
        ref[...] = part.astype(HALF)
        own.append(part.T.astype(HALF))
    taps = jnp.concatenate([taps[:, :8] * first, taps[:, ROWS - 8 :] * last], axis=1)
    table = band_tables(taps, 16, 8, 16, True)
    refs = ((edge_back_high_ref, edge_high_ref), (edge_back_low_ref, edge_low_ref))
    for part, (back_ref, ref) in zip(table, refs):
        back_ref[...] = part.astype(HALF)
        ref[...] = part.T.astype(HALF)
    copies[1].wait()
    phi = halves(phi_ref[...])
    phi_high_ref[...], phi_low_ref[...] = phi
    for group in range(4):
        own_rows = children_ref[8 * group : 8 * group + 8].reshape(8 * OWN, PHI)
        mixed = dot3(halves(own_rows), phi)
        fine_ref[256 * group : 256 * (group + 1)] = dot3(own, halves(mixed))
    for parent in range(2):
        for pol in range(2):
            for block in range(4):
                rows = slice(8 * block, 8 * (block + 1))
                real, imag = gathered(fine_ref, shift_ref, parent, pol, 32, 8 * block, rows)
                for part, value in enumerate((real, imag)):
                    for pair, tile in enumerate(swap_blocks(lane_blocks(value))):
                        packed_ref[4 * block + pair, parent, 2 * pol + part] = tile


def gathered(fine_ref, shift_ref, parent, pol, per_plane, first, rows):
    real = imag = None
    for kid in range(KIDS):
        at = ((parent * KIDS + kid) * 4 + pol * 2) * per_plane + first
        a = fine_ref[at : at + 8]
        b = fine_ref[at + per_plane : at + per_plane + 8]
        c = shift_ref[kid, 0, rows]
        d = shift_ref[kid, 1, rows]
        one, two = c * a - d * b, c * b + d * a
        real = one if real is None else real + one
        imag = two if imag is None else imag + two
    return real, imag


def edge_forward_kernel(
    codes_hbm, above_ref, below_ref, phi_high_ref, phi_low_ref, edge_high_ref, edge_low_ref,
    shift_ref, packed_ref, out_ref, codes_ref, halo_ref, fine_ref, sem,
):
    copy = pltpu.make_async_copy(codes_hbm, codes_ref, sem)
    copy.start()
    for plane in range(PLANES):
        halo_ref[8 * plane : 8 * plane + 4] = above_ref[plane]
        halo_ref[8 * plane + 4 : 8 * plane + 8] = below_ref[plane]
    phi = (phi_high_ref[...], phi_low_ref[...])
    edge = (edge_high_ref[...], edge_low_ref[...])
    for parent in range(2):
        mixed = dot3(halves(halo_ref[128 * parent : 128 * (parent + 1)]), phi)
        fine_ref[256 * parent : 256 * (parent + 1)] = dot3(edge, halves(mixed))
    out_ref[4:12] = packed_ref[4:12]
    for side in range(2):
        rows = slice(24 * side, 24 * side + 8)
        for parent in range(2):
            for pol in range(2):
                real, imag = gathered(fine_ref, shift_ref, parent, pol, 16, 8 * side, rows)
                for part, value in enumerate((real, imag)):
                    for pair, tile in enumerate(swap_blocks(lane_blocks(value))):
                        at = (12 * side + pair, parent, 2 * pol + part)
                        out_ref[at] = packed_ref[at] + tile
    copy.wait()


def spread_back(local_ref, shift_ref, parent, pol, blocks, store):
    parts = []
    for part in range(2):
        pieces = []
        for first in blocks:
            tiles = [local_ref[first + pair, parent, 2 * pol + part] for pair in range(4)]
            pieces.append(jnp.concatenate(swap_blocks(tiles), axis=1))
        parts.append(pieces)
    for kid in range(KIDS):
        real, imag = [], []
        for index, first in enumerate(blocks):
            a, b = parts[0][index], parts[1][index]
            c = shift_ref[kid, 0, 2 * first : 2 * first + 8]
            d = shift_ref[kid, 1, 2 * first : 2 * first + 8]
            real.append(c * a + d * b)
            imag.append(c * b - d * a)
        plane = (parent * KIDS + kid) * 4 + pol * 2
        store(plane, halves(jnp.concatenate(real, axis=0)))
        store(plane + 1, halves(jnp.concatenate(imag, axis=0)))


def edge_back_kernel(
    local_ref, shift_ref, phi_high_ref, phi_low_ref, table_high_ref, table_low_ref,
    up_ref, down_ref, high_ref, low_ref,
):
    phi = (phi_high_ref[...], phi_low_ref[...])
    table = (table_high_ref[...], table_low_ref[...])

    def store(plane, value):
        high_ref[16 * plane : 16 * plane + 16], low_ref[16 * plane : 16 * plane + 16] = value

    for parent in range(2):
        for pol in range(2):
            spread_back(local_ref, shift_ref, parent, pol, (0, 12), store)
        rows = slice(256 * parent, 256 * (parent + 1))
        narrowed = dot3(table, (high_ref[rows], low_ref[rows]))
        result = dot3(halves(narrowed), phi, contract=1)
        for plane in range(16):
            up_ref[16 * parent + plane] = result[8 * plane : 8 * plane + 4]
            down_ref[16 * parent + plane] = result[8 * plane + 4 : 8 * plane + 8]


def own_back_kernel(
    local_ref, shift_ref, phi_high_ref, phi_low_ref, table_high_ref, table_low_ref,
    own_ref, high_ref, low_ref,
):
    phi = (phi_high_ref[...], phi_low_ref[...])
    table = (table_high_ref[...], table_low_ref[...])

    def store(plane, value):
        high_ref[32 * plane : 32 * plane + 32], low_ref[32 * plane : 32 * plane + 32] = value

    for parent in range(2):
        for pol in range(2):
            spread_back(local_ref, shift_ref, parent, pol, (0, 4, 8, 12), store)
        for group in (2 * parent, 2 * parent + 1):
            rows = slice(256 * group, 256 * (group + 1))
            narrowed = dot3(table, (high_ref[rows], low_ref[rows]))
            own_ref[128 * group : 128 * (group + 1)] = dot3(halves(narrowed), phi, contract=1)


def translate_kernel(codes_ref, field_ref, operator_ref, out_ref):
    parents = out_ref.shape[0] // 32
    slots = parents * LIST

    def one_quad(quad, carry):
        bases = [codes_ref[2 * slots + quad * QUAD + member] for member in range(QUAD)]

        def some_slots(step, sums):
            sums = list(sums)
            for member in range(QUAD):
                slot = bases[member] + step * GROUP
                for lane in range(GROUP):
                    source = pl.multiple_of(codes_ref[slot + lane], 8)
                    offset = pl.multiple_of(codes_ref[slot + (slots + lane)], 8)
                    c = operator_ref[pl.ds(offset, 8), :]
                    less = operator_ref[pl.ds(offset + 8, 8), :]
                    more = operator_ref[pl.ds(offset + 16, 8), :]
                    for pol in range(2):
                        at = member * 6 + pol * 3
                        a = field_ref[pl.ds(source + pol * 16, 8), :]
                        b = field_ref[pl.ds(source + (pol * 16 + 8), 8), :]
                        sums[at] = sums[at] + c * (a + b)
                        sums[at + 1] = sums[at + 1] + a * less
                        sums[at + 2] = sums[at + 2] + b * more
            return tuple(sums)

        zero = jnp.zeros((8, 128), jnp.float32)
        steps = codes_ref[2 * slots + parents + quad]
        sums = lax.fori_loop(0, steps, some_slots, (zero,) * (6 * QUAD))
        for member in range(QUAD):
            for pol in range(2):
                both, less, more = sums[member * 6 + pol * 3 : member * 6 + pol * 3 + 3]
                at = pl.multiple_of(bases[member] + pol * 16, 8)
                out_ref[pl.ds(at, 8), :] = both - more
                out_ref[pl.ds(at + 8, 8), :] = both + less
        return carry

    lax.fori_loop(0, parents // QUAD, one_quad, 0)


def in_vmem(value):
    return pltpu.with_memory_space_constraint(value, pltpu.VMEM)


def in_smem(value):
    return pltpu.with_memory_space_constraint(value, pltpu.SMEM)


def in_hbm(value):
    return pltpu.with_memory_space_constraint(value, pltpu.HBM)


def call(kernel, name, outs, scratch, *operands, raw=0, out_specs=None):
    vmem = pl.BlockSpec(memory_space=pltpu.VMEM)
    hbm = pl.BlockSpec(memory_space=pltpu.HBM)
    return pl.pallas_call(
        kernel,
        out_shape=outs,
        in_specs=[hbm] * raw + [vmem] * (len(operands) - raw),
        out_specs=out_specs if out_specs is not None else jax.tree.map(lambda _: vmem, outs),
        scratch_shapes=scratch,
        compiler_params=pltpu.CompilerParams(vmem_limit_bytes=GRANT),
        name=name,
    )(*map(in_hbm, operands[:raw]), *map(in_vmem, operands[raw:]))


def slot_codes(far_source, far_offset, far_count, kinds):
    parents, slots = far_source.shape
    live = jnp.arange(slots, dtype=jnp.int32)[None, :] < far_count[:, None]
    source = (far_source * 32).reshape(-1)
    offset = (jnp.where(live, far_offset, kinds) * 24).reshape(-1)
    index = jnp.arange(parents, dtype=jnp.int32)
    key = far_count * parents - index
    rank = jnp.sum((key[None, :] > key[:, None]).astype(jnp.int32), axis=1)
    chosen = rank[None, :] == index[:, None]
    order = jnp.sum(jnp.where(chosen, index[None, :] * LIST, 0), axis=1)
    counts = jnp.sum(jnp.where(chosen[::QUAD], far_count[None, :], 0), axis=1)
    return jnp.concatenate([source, offset, order, (counts + (GROUP - 1)) // GROUP])


def operator_table(translators):
    kinds, _, rows, samples = translators.shape
    table = translators.reshape(kinds, 2, rows, samples // 128, 128).transpose(0, 1, 3, 2, 4)
    real, imag = table[:, 0], table[:, 1]
    table = jnp.stack([real, imag - real, imag + real], axis=1)
    return jnp.pad(table.reshape(kinds * 24, 128), ((0, 24), (0, 0)))


def translate(field, codes, operators):
    smem = pl.BlockSpec(memory_space=pltpu.SMEM)
    vmem = pl.BlockSpec(memory_space=pltpu.VMEM)
    field = field.reshape(-1, 128)
    return pl.pallas_call(
        translate_kernel,
        out_shape=jax.ShapeDtypeStruct(field.shape, jnp.float32),
        in_specs=[smem, vmem, vmem],
        out_specs=vmem,
        compiler_params=pltpu.CompilerParams(vmem_limit_bytes=GRANT),
        name="translate",
    )(in_smem(codes), in_vmem(field), in_vmem(operators))


def merge_kernel(own_ref, top_ref, bottom_ref, out_hbm, out_ref, sems):
    copies = []
    for i in range(4):
        chunk = slice(8 * i, 8 * i + 8)
        own = own_ref[chunk]
        middle = own[:, 4 : OWN - 4]
        top = own[:, :4] + top_ref[chunk]
        bottom = own[:, OWN - 4 :] + bottom_ref[chunk]
        out_ref[chunk] = jnp.concatenate([top, middle, bottom], axis=1)
        copies.append(pltpu.make_async_copy(out_ref.at[chunk], out_hbm.at[chunk], sems.at[i]))
        copies[-1].start()
    for copy in copies:
        copy.wait()


def on_device(
    children, theta_band, phi_interp, child_shift, translators, far_source, far_offset, far_count
):
    planes = children.reshape(PLANES, OWN, PHI)
    half = lambda *shape: pltpu.VMEM(shape, HALF)
    whole = lambda *shape: pltpu.VMEM(shape, WHOLE)
    hbm = pl.BlockSpec(memory_space=pl.ANY)
    vmem = pl.BlockSpec(memory_space=pltpu.VMEM)
    smem = pl.BlockSpec(memory_space=pltpu.SMEM)
    planes, upper, lower = call(
        cut_kernel, "cut", (whole(PLANES, OWN, PHI),) + (whole(PLANES, 4, PHI),) * 2,
        [pltpu.SemaphoreType.DMA((4,))], planes, raw=1,
    )
    above = shifted_ring(lower, "theta", 1)
    below = shifted_ring(upper, "theta", -1)
    tables = (half(256, 512),) * 2 + (half(256, 128),) * 2 + (half(128, 256),) * 4
    packed, phi_high, phi_low, edge_high, edge_low, *backs = call(
        own_forward_kernel, "own_forward", (whole(16, 2, 4, 8, 128),) + tables,
        [
            whole(1024, SAMPLES), whole(8, ROWS), whole(PHI, SAMPLES),
            pltpu.SemaphoreType.DMA((2,)),
        ],
        theta_band.T, phi_interp, planes, child_shift, raw=2,
    )
    codes = slot_codes(far_source, far_offset, far_count, translators.shape[0])
    operators = operator_table(translators)
    packed, codes = call(
        edge_forward_kernel, "edge_forward",
        (whole(16, 2, 4, 8, 128), pltpu.SMEM(codes.shape, jnp.int32)),
        [whole(256, PHI), whole(512, SAMPLES), pltpu.SemaphoreType.DMA],
        codes, above, below, phi_high, phi_low, edge_high, edge_low, child_shift, packed,
        raw=1, out_specs=(vmem, smem),
    )
    packed, operators = lax.optimization_barrier((packed, operators))
    field = lax.all_to_all(packed, "clus", 0, 0)
    summed = translate(field, codes, operators)
    local = lax.all_to_all(summed.reshape(packed.shape), "clus", 0, 0)
    up, down = call(
        edge_back_kernel, "edge_back", (whole(PLANES, 4, PHI),) * 2,
        [half(512, SAMPLES)] * 2, local, child_shift, phi_high, phi_low, backs[2], backs[3],
    )
    from_below = shifted_ring(down, "theta", 1)
    from_above = shifted_ring(up, "theta", -1)
    own = call(
        own_back_kernel, "own_back", whole(PLANES * OWN, PHI),
        [half(1024, SAMPLES)] * 2, local, child_shift, phi_high, phi_low, backs[0], backs[1],
    ).reshape(planes.shape)
    result = call(
        merge_kernel, "merge", jax.ShapeDtypeStruct(planes.shape, WHOLE),
        [whole(PLANES, OWN, PHI), pltpu.SemaphoreType.DMA((4,))],
        own, from_below, from_above, out_specs=hbm,
    )
    return result.reshape(children.shape)


def solution(mesh):
    return jax.shard_map(
        on_device,
        mesh=mesh,
        in_specs=(
            P("clus", None, None, "theta", None),
            P("theta", None),
            P(),
            P(None, None, "theta", None),
            P(None, None, ("theta", "clus"), None),
            P(),
            P(),
            P(),
        ),
        out_specs=P("clus", None, None, "theta", None),
        check_vma=False,
    )
```

```python
import functools

import jax
import jax.numpy as jnp
from jax import lax
from jax.experimental import pallas as pl
from jax.experimental.pallas import tpu as pltpu
from jax.sharding import PartitionSpec as P

KIDS = 4
LIST = 32
GROUP = 8
PAIR = 2
PLANES = 32
ROWS = 32
OWN = 16
PHI = 256
SAMPLES = 512
GRANT = 12 * 2**20
HALF = jnp.bfloat16
WHOLE = jnp.float32


def shifted_ring(value, axis, step):
    count = lax.axis_size(axis)
    return lax.ppermute(value, axis, [(i, (i + step) % count) for i in range(count)])


def halves(value):
    high = value.astype(HALF)
    return high, (value - high.astype(WHOLE)).astype(HALF)


def dot3(left, right, contract=0):
    dims = (((1,), (contract,)), ((), ()))
    total = None
    for a, b in ((0, 0), (0, 1), (1, 0)):
        part = lax.dot_general(left[a], right[b], dims, preferred_element_type=WHOLE)
        total = part if total is None else total + part
    return total


def swap_blocks(tiles):
    sub = lax.broadcasted_iota(jnp.int32, (8, 128), 0)
    even = (sub // 2) % 2 == 0
    low = sub < 4
    a, b, c, d = tiles

    def step(first, second, shift, mask):
        one = jnp.where(mask, first, pltpu.roll(second, shift, 0))
        two = jnp.where(mask, pltpu.roll(first, 8 - shift, 0), second)
        return one, two

    a, b = step(a, b, 2, even)
    c, d = step(c, d, 2, even)
    a, c = step(a, c, 4, low)
    b, d = step(b, d, 4, low)
    return a, b, c, d


def lane_blocks(value):
    return [value[:, 128 * i : 128 * (i + 1)] for i in range(4)]


def tiled(bands, outer, width):
    row = lax.broadcasted_iota(jnp.int32, (outer, width), 0)
    column = lax.broadcasted_iota(jnp.int32, (outer, width), 1)
    pick = (row == column % outer).astype(HALF)
    return [jnp.dot(part, pick, preferred_element_type=WHOLE) for part in halves(bands)]


def band_tables(bands, planes, inner, outer, place):
    shape = (planes * inner, planes * outer)
    row = lax.broadcasted_iota(jnp.int32, shape, 0)
    column = lax.broadcasted_iota(jnp.int32, shape, 1)
    child, parent = place(row % inner, column % outer)
    tap = child - parent // 2 + 3
    tap = jnp.where(row // inner == column // outer, tap, -1)
    tables = []
    for part in tiled(bands, outer, shape[1]):
        table = jnp.zeros(shape, WHOLE)
        for t in range(8):
            table = jnp.where(tap == t, jnp.broadcast_to(part[t : t + 1], shape), table)
        tables.append(table)
    return tables


def edge_rows(child, parent):
    child = jnp.where(child < 4, child - 4, child + 12)
    return child, jnp.where(parent < 8, parent, parent + 16)


def cut_kernel(children_hbm, taps_hbm, children_ref, taps_ref, upper_ref, lower_ref, sems):
    chunks = [slice(128 * i, 128 * i + 128) for i in range(4)]
    copies = [
        pltpu.make_async_copy(
            children_hbm.at[chunk, 128 * side : 128 * side + 128],
            children_ref.at[side, chunk],
            sems.at[2 * i + side],
        )
        for i, chunk in enumerate(chunks)
        for side in range(2)
    ]
    for copy in copies:
        copy.start()
    taps = pltpu.make_async_copy(taps_hbm, taps_ref, sems.at[8])
    taps.start()
    for at, copy in enumerate(copies):
        copy.wait()
        i, side = divmod(at, 2)
        for ref, first, count in ((upper_ref, 0, 4), (lower_ref, OWN - 3, 3)):
            for row in range(count):
                rows = pl.ds(128 * i + first + row, 8, stride=OWN)
                value = children_ref[side, rows, :]
                ref[row, 8 * i : 8 * i + 8, 128 * side : 128 * side + 128] = value
    taps.wait()


def both_sides(ref, first, count):
    return jnp.concatenate([ref[side, first : first + count] for side in range(2)], axis=1)


def own_forward_kernel(
    phi_hbm, source_hbm, offset_hbm, counts_hbm, taps_ref, children_ref, shift_ref,
    packed_ref, phi_high_ref, phi_low_ref, edge_high_ref, edge_low_ref, back_high_ref, back_low_ref,
    up_high_ref, up_low_ref, down_high_ref, down_low_ref, codes_ref, counts_ref,
    fine_ref, phi_ref, source_ref, offset_ref, sems, *, kinds,
):
    pairs = (
        (phi_hbm, phi_ref), (source_hbm, source_ref), (offset_hbm, offset_ref),
        (counts_hbm, counts_ref),
    )
    copies = [pltpu.make_async_copy(*pair, sems.at[i]) for i, pair in enumerate(pairs)]
    for copy in copies:
        copy.start()
    strip = lax.axis_index("theta")
    first = (strip > 0).astype(WHOLE)
    last = (strip < lax.axis_size("theta") - 1).astype(WHOLE)
    taps = taps_ref[...]
    table = band_tables(taps, 8, 16, 32, lambda child, parent: (child, parent))
    own = []
    for part, ref in zip(table, (back_high_ref, back_low_ref)):
        ref[...] = part.astype(HALF)
        own.append(part.T.astype(HALF))
    for copy in copies:
        copy.wait()
    phi = halves(phi_ref[...])
    phi_high_ref[...], phi_low_ref[...] = phi
    lane = lax.broadcasted_iota(jnp.int32, (1, LIST), 1)
    for parent in range(source_ref.shape[0]):
        live = lane < counts_ref[parent]
        offset = jnp.where(live, offset_ref[parent : parent + 1], kinds)
        codes_ref[parent : parent + 1] = source_ref[parent : parent + 1] * 32 + offset * (24 * 65536)
    for group in range(4):
        mixed = dot3(halves(both_sides(children_ref, 128 * group, 128)), phi)
        fine_ref[256 * group : 256 * (group + 1)] = dot3(own, halves(mixed))
    upper, lower = taps[:, :8] * first, taps[:, ROWS - 8 :] * last
    table = band_tables(jnp.concatenate([upper, lower], axis=1), 16, 8, 16, edge_rows)
    for part, ref in zip(table, (edge_high_ref, edge_low_ref)):
        ref[...] = part.T.astype(HALF)
    table = band_tables(upper, 16, 4, 8, lambda child, parent: (child - 4, parent))
    for part, ref in zip(table, (up_high_ref, up_low_ref)):
        ref[...] = part.astype(HALF)
    table = band_tables(lower, 16, 4, 8, lambda child, parent: (child + 16, parent + 24))
    for part, ref in zip(table, (down_high_ref, down_low_ref)):
        ref[...] = part.astype(HALF)
    for parent in range(2):
        for pol in range(2):
            for block in range(4):
                rows = slice(8 * block, 8 * (block + 1))
                real, imag = gathered(fine_ref, shift_ref, parent, pol, 32, 8 * block, rows)
                for part, value in enumerate((real, imag)):
                    for pair, tile in enumerate(swap_blocks(lane_blocks(value))):
                        packed_ref[4 * block + pair, parent, 2 * pol + part] = tile


def gathered(fine_ref, shift_ref, parent, pol, per_plane, first, rows):
    real = imag = None
    for kid in range(KIDS):
        at = ((parent * KIDS + kid) * 4 + pol * 2) * per_plane + first
        a = fine_ref[at : at + 8]
        b = fine_ref[at + per_plane : at + per_plane + 8]
        c = shift_ref[kid, 0, rows]
        d = shift_ref[kid, 1, rows]
        one, two = c * a - d * b, c * b + d * a
        real = one if real is None else real + one
        imag = two if imag is None else imag + two
    return real, imag


def edge_forward_kernel(
    codes_src, above_ref, below_ref, phi_high_ref, phi_low_ref, edge_high_ref, edge_low_ref,
    shift_ref, packed_ref, out_ref, codes_ref, halo_ref, fine_ref, sem,
):
    codes = pltpu.make_async_copy(codes_src, codes_ref, sem)
    codes.start()
    for side in range(2):
        lanes = slice(128 * side, 128 * side + 128)
        halo_ref[side, pl.ds(0, PLANES, stride=8), :] = jnp.zeros((PLANES, 128), WHOLE)
        for row in range(3):
            halo_ref[side, pl.ds(row + 1, PLANES, stride=8), :] = above_ref[row, :, lanes]
        for row in range(4):
            halo_ref[side, pl.ds(row + 4, PLANES, stride=8), :] = below_ref[row, :, lanes]
    phi = (phi_high_ref[...], phi_low_ref[...])
    edge = (edge_high_ref[...], edge_low_ref[...])
    for parent in range(2):
        mixed = dot3(halves(both_sides(halo_ref, 128 * parent, 128)), phi)
        fine_ref[256 * parent : 256 * (parent + 1)] = dot3(edge, halves(mixed))
    out_ref[4:12] = packed_ref[4:12]
    for side in range(2):
        rows = slice(24 * side, 24 * side + 8)
        for parent in range(2):
            for pol in range(2):
                real, imag = gathered(fine_ref, shift_ref, parent, pol, 16, 8 * side, rows)
                for part, value in enumerate((real, imag)):
                    for pair, tile in enumerate(swap_blocks(lane_blocks(value))):
                        at = (12 * side + pair, parent, 2 * pol + part)
                        out_ref[at] = packed_ref[at] + tile
    codes.wait()


def spread_back(local_ref, shift_ref, parent, pol, blocks, high_ref, low_ref):
    parts = []
    for part in range(2):
        pieces = []
        for first in blocks:
            tiles = [local_ref[first + pair, parent, 2 * pol + part] for pair in range(4)]
            pieces.append(jnp.concatenate(swap_blocks(tiles), axis=1))
        parts.append(pieces)
    for kid in range(KIDS):
        real, imag = [], []
        for index, first in enumerate(blocks):
            a, b = parts[0][index], parts[1][index]
            c = shift_ref[kid, 0, 2 * first : 2 * first + 8]
            d = shift_ref[kid, 1, 2 * first : 2 * first + 8]
            real.append(c * a + d * b)
            imag.append(c * b - d * a)
        height = 16 * len(blocks)
        at = ((parent * KIDS + kid) * 2 + pol) * height
        value = halves(jnp.concatenate(real + imag, axis=0))
        high_ref[at : at + height], low_ref[at : at + height] = value


def edge_back_kernel(first, skipped):
    def kernel(
        local_ref, shift_ref, phi_high_ref, phi_low_ref, table_high_ref, table_low_ref,
        out_ref, high_ref, low_ref, narrow_ref, result_ref,
    ):
        phi = (phi_high_ref[...], phi_low_ref[...])
        table = (table_high_ref[...], table_low_ref[...])
        for parent in range(2):
            for pol in range(2):
                spread_back(local_ref, shift_ref, parent, pol, (first,), high_ref, low_ref)
            rows = slice(128 * parent, 128 * (parent + 1))
            narrow = dot3(table, (high_ref[rows], low_ref[rows]))
            narrow_ref[64 * parent : 64 * (parent + 1)] = narrow
        result = dot3(halves(narrow_ref[...]), phi, contract=1)
        for side in range(2):
            lanes = slice(128 * side, 128 * side + 128)
            result_ref[side] = result[:, lanes]
            for row in range(4 - skipped):
                rows = pl.ds(row + skipped, PLANES, stride=4)
                out_ref[row, :, lanes] = result_ref[side, rows, :]

    return kernel


def own_back_kernel(
    local_ref, shift_ref, phi_high_ref, phi_low_ref, table_high_ref, table_low_ref,
    own_ref, high_ref, low_ref,
):
    phi = (phi_high_ref[...], phi_low_ref[...])
    table = (table_high_ref[...], table_low_ref[...])

    for parent in range(2):
        for pol in range(2):
            spread_back(local_ref, shift_ref, parent, pol, (0, 4, 8, 12), high_ref, low_ref)
        for group in (2 * parent, 2 * parent + 1):
            rows = slice(256 * group, 256 * (group + 1))
            narrowed = dot3(table, (high_ref[rows], low_ref[rows]))
            result = dot3(halves(narrowed), phi, contract=1)
            for side in range(2):
                lanes = slice(128 * side, 128 * side + 128)
                own_ref[side, 128 * group : 128 * (group + 1)] = result[:, lanes]


def translate_kernel(codes_ref, counts_ref, field_ref, operator_ref, out_ref, table_ref):
    parents = counts_ref.shape[0]
    kinds = operator_ref.shape[0] // 16
    for kind in range(kinds):
        c = operator_ref[16 * kind : 16 * kind + 8]
        d = operator_ref[16 * kind + 8 : 16 * kind + 16]
        for at, value in enumerate((c, d - c, c + d)):
            table_ref[24 * kind + 8 * at : 24 * kind + 8 * at + 8] = value
    table_ref[24 * kinds : 24 * kinds + 24] = jnp.zeros((24, 128), WHOLE)

    def one_pair(pair, carry):
        def some_slots(step, sums):
            sums = list(sums)
            for member in range(PAIR):
                for lane in range(GROUP):
                    slot = pair * (PAIR * LIST) + step * GROUP + (member * LIST + lane)
                    code = codes_ref[slot]
                    source = pl.multiple_of(code & 0xFFFF, 8)
                    offset = pl.multiple_of(code >> 16, 8)
                    c = table_ref[pl.ds(offset, 8), :]
                    less = table_ref[pl.ds(offset + 8, 8), :]
                    more = table_ref[pl.ds(offset + 16, 8), :]
                    for pol in range(2):
                        at = member * 6 + pol * 3
                        a = field_ref[pl.ds(source + pol * 16, 8), :]
                        b = field_ref[pl.ds(source + (pol * 16 + 8), 8), :]
                        sums[at] = sums[at] + c * (a + b)
                        sums[at + 1] = sums[at + 1] + a * less
                        sums[at + 2] = sums[at + 2] + b * more
            return tuple(sums)

        zero = jnp.zeros((8, 128), WHOLE)
        longest = jnp.maximum(counts_ref[pair * PAIR], counts_ref[pair * PAIR + 1])
        steps = lax.shift_right_logical(longest + (GROUP - 1), 3)
        sums = lax.fori_loop(0, steps, some_slots, (zero,) * (6 * PAIR))
        for member in range(PAIR):
            for pol in range(2):
                both, less, more = sums[member * 6 + pol * 3 : member * 6 + pol * 3 + 3]
                at = pl.multiple_of(pair * 64 + member * 32 + pol * 16, 8)
                out_ref[pl.ds(at, 8), :] = both - more
                out_ref[pl.ds(at + 8, 8), :] = both + less
        return carry

    lax.fori_loop(0, parents // PAIR, one_pair, 0)


def in_vmem(value):
    return pltpu.with_memory_space_constraint(value, pltpu.VMEM)


def in_smem(value):
    return pltpu.with_memory_space_constraint(value, pltpu.SMEM)


def in_hbm(value):
    return pltpu.with_memory_space_constraint(value, pltpu.HBM)


def call(kernel, name, outs, scratch, *operands, raw=0, out_specs=None):
    vmem = pl.BlockSpec(memory_space=pltpu.VMEM)
    hbm = pl.BlockSpec(memory_space=pltpu.HBM)
    return pl.pallas_call(
        kernel,
        out_shape=outs,
        in_specs=[hbm] * raw + [vmem] * (len(operands) - raw),
        out_specs=out_specs if out_specs is not None else jax.tree.map(lambda _: vmem, outs),
        scratch_shapes=scratch,
        compiler_params=pltpu.CompilerParams(vmem_limit_bytes=GRANT),
        name=name,
    )(*map(in_hbm, operands[:raw]), *map(in_vmem, operands[raw:]))


def operator_rows(translators):
    kinds, _, rows, samples = translators.shape
    table = translators.reshape(kinds, 2, rows, samples // 128, 128).transpose(0, 1, 3, 2, 4)
    return table.reshape(kinds * 16, 128)


def translate(field, codes, counts, operators):
    smem = pl.BlockSpec(memory_space=pltpu.SMEM)
    vmem = pl.BlockSpec(memory_space=pltpu.VMEM)
    field = field.reshape(-1, 128)
    return pl.pallas_call(
        translate_kernel,
        out_shape=jax.ShapeDtypeStruct(field.shape, WHOLE),
        in_specs=[smem, smem, vmem, vmem],
        out_specs=vmem,
        scratch_shapes=[pltpu.VMEM((operators.shape[0] * 3 // 2 + 24, 128), WHOLE)],
        compiler_params=pltpu.CompilerParams(vmem_limit_bytes=GRANT),
        name="translate",
    )(in_smem(codes), in_smem(counts), in_vmem(field), in_vmem(operators))


def merge_kernel(own_ref, top_ref, bottom_ref, out_hbm, out_ref, sems):
    copies = []
    for i in range(4):
        chunk = slice(128 * i, 128 * i + 128)
        for side in range(2):
            lanes = slice(128 * side, 128 * side + 128)
            out_ref[side, chunk] = own_ref[side, chunk]
            for ref, first, count in ((top_ref, 0, 4), (bottom_ref, OWN - 3, 3)):
                for row in range(count):
                    rows = pl.ds(128 * i + first + row, 8, stride=OWN)
                    value = own_ref[side, rows, :] + ref[row, 8 * i : 8 * i + 8, lanes]
                    out_ref[side, rows, :] = value
            target = out_hbm.at[chunk, lanes]
            copy = pltpu.make_async_copy(out_ref.at[side, chunk], target, sems.at[2 * i + side])
            copy.start()
            copies.append(copy)
    for copy in copies:
        copy.wait()


def on_device(
    children, theta_band, phi_interp, child_shift, translators, far_source, far_offset, far_count
):
    half = lambda *shape: pltpu.VMEM(shape, HALF)
    whole = lambda *shape: pltpu.VMEM(shape, WHOLE)
    hbm = pl.BlockSpec(memory_space=pl.ANY)
    vmem = pl.BlockSpec(memory_space=pltpu.VMEM)
    smem = pl.BlockSpec(memory_space=pltpu.SMEM)
    dma = pltpu.SemaphoreType.DMA
    planes, taps, upper, lower = call(
        cut_kernel, "cut",
        (whole(2, PLANES * OWN, 128), whole(8, ROWS), whole(4, PLANES, PHI), whole(3, PLANES, PHI)),
        [dma((9,))], children.reshape(-1, PHI), theta_band.T, raw=2,
    )
    below = shifted_ring(upper, "theta", -1)
    above = shifted_ring(lower, "theta", 1)
    tables = (half(256, 512),) * 2 + (half(256, 128),) * 2 + (half(128, 256),) * 2
    packed, *tables, codes, counts = call(
        functools.partial(own_forward_kernel, kinds=translators.shape[0]), "own_forward",
        (whole(16, 2, 4, 8, 128),) + tables + (half(64, 128),) * 4
        + (pltpu.VMEM(far_source.shape, jnp.int32), pltpu.SMEM(far_count.shape, jnp.int32)),
        [
            whole(1024, SAMPLES), whole(PHI, SAMPLES), pltpu.VMEM(far_source.shape, jnp.int32),
            pltpu.VMEM(far_source.shape, jnp.int32), dma((4,)),
        ],
        phi_interp, far_source, far_offset, far_count, taps, planes, child_shift,
        raw=4, out_specs=(vmem,) * 12 + (smem,),
    )
    phi, edge, back, up_table, down_table = (tables[i : i + 2] for i in range(0, 10, 2))
    operators = in_vmem(operator_rows(translators))
    packed, codes = call(
        edge_forward_kernel, "edge_forward",
        (whole(16, 2, 4, 8, 128), pltpu.SMEM((codes.size,), jnp.int32)),
        [whole(2, 256, 128), whole(512, SAMPLES), dma],
        codes.reshape(-1), above, below, *phi, *edge, child_shift, packed, out_specs=(vmem, smem),
    )
    packed, operators = lax.optimization_barrier((packed, operators))
    field = lax.all_to_all(packed, "clus", 0, 0)
    summed = translate(field, codes, counts, operators)
    local = lax.all_to_all(summed.reshape(packed.shape), "clus", 0, 0)
    scratch = [half(256, SAMPLES)] * 2 + [whole(128, SAMPLES), whole(2, 128, 128)]
    down = call(
        edge_back_kernel(12, 0), "down_back", whole(4, PLANES, PHI), scratch,
        local, child_shift, *phi, *down_table,
    )
    from_below = shifted_ring(down, "theta", 1)
    up = call(
        edge_back_kernel(0, 1), "up_back", whole(3, PLANES, PHI), scratch,
        local, child_shift, *phi, *up_table,
    )
    from_above = shifted_ring(up, "theta", -1)
    own = call(
        own_back_kernel, "own_back", whole(2, PLANES * OWN, 128), [half(1024, SAMPLES)] * 2,
        local, child_shift, *phi, *back,
    )
    result = call(
        merge_kernel, "merge", jax.ShapeDtypeStruct((PLANES * OWN, PHI), WHOLE),
        [whole(2, PLANES * OWN, 128), dma((8,))], own, from_below, from_above, out_specs=hbm,
    )
    return result.reshape(children.shape)


def solution(mesh):
    return jax.shard_map(
        on_device,
        mesh=mesh,
        in_specs=(
            P("clus", None, None, "theta", None),
            P("theta", None),
            P(),
            P(None, None, "theta", None),
            P(None, None, ("theta", "clus"), None),
            P(),
            P(),
            P(),
        ),
        out_specs=P("clus", None, None, "theta", None),
        check_vma=False,
    )
```

```python
import functools

import jax
import jax.numpy as jnp
from jax import lax
from jax.experimental import pallas as pl
from jax.experimental.pallas import tpu as pltpu
from jax.sharding import PartitionSpec as P

KIDS = 4
LIST = 32
GROUP = 8
PAIR = 2
PLANES = 32
ROWS = 32
OWN = 16
PHI = 256
SAMPLES = 512
GRANT = 12 * 2**20
HALF = jnp.bfloat16
WHOLE = jnp.float32


def swapped(value, far):
    count = lax.axis_size("theta")
    pairs = [(i, (i - 1 if (i % 2 == 0) == far else i + 1) % count) for i in range(count)]
    return lax.ppermute(value, "theta", pairs)


def even_strip():
    return lax.rem(lax.axis_index("theta"), 2) == 0


def halves(value):
    high = value.astype(HALF)
    return high, (value - high.astype(WHOLE)).astype(HALF)


def dot3(left, right, contract=0):
    dims = (((1,), (contract,)), ((), ()))
    total = None
    for a, b in ((0, 0), (0, 1), (1, 0)):
        part = lax.dot_general(left[a], right[b], dims, preferred_element_type=WHOLE)
        total = part if total is None else total + part
    return total


def swap_blocks(tiles):
    sub = lax.broadcasted_iota(jnp.int32, (8, 128), 0)
    even = (sub // 2) % 2 == 0
    low = sub < 4
    a, b, c, d = tiles

    def step(first, second, shift, mask):
        one = jnp.where(mask, first, pltpu.roll(second, shift, 0))
        two = jnp.where(mask, pltpu.roll(first, 8 - shift, 0), second)
        return one, two

    a, b = step(a, b, 2, even)
    c, d = step(c, d, 2, even)
    a, c = step(a, c, 4, low)
    b, d = step(b, d, 4, low)
    return a, b, c, d


def lane_blocks(value):
    return [value[:, 128 * i : 128 * (i + 1)] for i in range(4)]


def tiled(bands, outer, width):
    row = lax.broadcasted_iota(jnp.int32, (outer, width), 0)
    column = lax.broadcasted_iota(jnp.int32, (outer, width), 1)
    pick = (row == column % outer).astype(HALF)
    return [jnp.dot(part, pick, preferred_element_type=WHOLE) for part in halves(bands)]


def band_tables(bands, planes, inner, outer, place):
    shape = (planes * inner, planes * outer)
    row = lax.broadcasted_iota(jnp.int32, shape, 0)
    column = lax.broadcasted_iota(jnp.int32, shape, 1)
    child, parent = place(row % inner, column % outer)
    tap = child - parent // 2 + 3
    tap = jnp.where(row // inner == column // outer, tap, -1)
    tables = []
    for part in tiled(bands, outer, shape[1]):
        table = jnp.zeros(shape, WHOLE)
        for t in range(8):
            table = jnp.where(tap == t, jnp.broadcast_to(part[t : t + 1], shape), table)
        tables.append(table)
    return tables


def edge_rows(child, parent):
    child = jnp.where(child < 4, child - 4, child + 12)
    return child, jnp.where(parent < 8, parent, parent + 16)


def cut_kernel(children_hbm, taps_hbm, children_ref, taps_ref, far_ref, near_ref, sems):
    even = even_strip()
    chunks = [slice(128 * i, 128 * i + 128) for i in range(4)]
    copies = [
        pltpu.make_async_copy(
            children_hbm.at[chunk, 128 * side : 128 * side + 128],
            children_ref.at[side, chunk],
            sems.at[2 * i + side],
        )
        for i, chunk in enumerate(chunks)
        for side in range(2)
    ]
    for copy in copies:
        copy.start()
    taps = pltpu.make_async_copy(taps_hbm, taps_ref, sems.at[8])
    taps.start()
    for at, copy in enumerate(copies):
        copy.wait()
        i, side = divmod(at, 2)
        lanes = slice(128 * side, 128 * side + 128)
        for row in range(4):
            upper = children_ref[side, pl.ds(128 * i + row, 8, stride=OWN), :]
            lower = children_ref[side, pl.ds(128 * i + OWN - 4 + row, 8, stride=OWN), :]
            far_ref[row, 8 * i : 8 * i + 8, lanes] = jnp.where(even, upper, lower)
            near_ref[row, 8 * i : 8 * i + 8, lanes] = jnp.where(even, lower, upper)
    taps.wait()


def both_sides(ref, first, count):
    return jnp.concatenate([ref[side, first : first + count] for side in range(2)], axis=1)


def own_forward_kernel(
    phi_hbm, source_hbm, offset_hbm, counts_hbm, taps_ref, children_ref, shift_ref,
    packed_ref, phi_high_ref, phi_low_ref, edge_high_ref, edge_low_ref, back_high_ref, back_low_ref,
    side_high_ref, side_low_ref, codes_ref, counts_ref,
    fine_ref, phi_ref, source_ref, offset_ref, sems, *, kinds,
):
    pairs = (
        (phi_hbm, phi_ref), (source_hbm, source_ref), (offset_hbm, offset_ref),
        (counts_hbm, counts_ref),
    )
    copies = [pltpu.make_async_copy(*pair, sems.at[i]) for i, pair in enumerate(pairs)]
    for copy in copies:
        copy.start()
    strip = lax.axis_index("theta")
    first = (strip > 0).astype(WHOLE)
    last = (strip < lax.axis_size("theta") - 1).astype(WHOLE)
    taps = taps_ref[...]
    table = band_tables(taps, 8, 16, 32, lambda child, parent: (child, parent))
    own = []
    for part, ref in zip(table, (back_high_ref, back_low_ref)):
        ref[...] = part.astype(HALF)
        own.append(part.T.astype(HALF))
    for copy in copies:
        copy.wait()
    phi = halves(phi_ref[...])
    phi_high_ref[...], phi_low_ref[...] = phi
    lane = lax.broadcasted_iota(jnp.int32, (1, LIST), 1)
    for parent in range(source_ref.shape[0]):
        live = lane < counts_ref[parent]
        offset = jnp.where(live, offset_ref[parent : parent + 1], kinds)
        codes_ref[parent : parent + 1] = source_ref[parent : parent + 1] * 32 + offset * (24 * 65536)
    for group in range(4):
        mixed = dot3(halves(both_sides(children_ref, 128 * group, 128)), phi)
        fine_ref[256 * group : 256 * (group + 1)] = dot3(own, halves(mixed))
    upper, lower = taps[:, :8] * first, taps[:, ROWS - 8 :] * last
    table = band_tables(jnp.concatenate([upper, lower], axis=1), 16, 8, 16, edge_rows)
    for part, ref in zip(table, (edge_high_ref, edge_low_ref)):
        ref[...] = part.T.astype(HALF)
    table = band_tables(upper, 16, 4, 8, lambda child, parent: (child - 4, parent))
    for part, ref in zip(table, (side_high_ref, side_low_ref)):
        ref[0] = part.astype(HALF)
    table = band_tables(lower, 16, 4, 8, lambda child, parent: (child + 16, parent + 24))
    for part, ref in zip(table, (side_high_ref, side_low_ref)):
        ref[1] = part.astype(HALF)
    for parent in range(2):
        for pol in range(2):
            for block in range(4):
                rows = slice(8 * block, 8 * (block + 1))
                real, imag = gathered(fine_ref, shift_ref, parent, pol, 32, 8 * block, rows)
                for part, value in enumerate((real, imag)):
                    for pair, tile in enumerate(swap_blocks(lane_blocks(value))):
                        packed_ref[4 * block + pair, parent, 2 * pol + part] = tile


def gathered(fine_ref, shift_ref, parent, pol, per_plane, first, rows):
    real = imag = None
    for kid in range(KIDS):
        at = ((parent * KIDS + kid) * 4 + pol * 2) * per_plane + first
        a = fine_ref[at : at + 8]
        b = fine_ref[at + per_plane : at + per_plane + 8]
        c = shift_ref[kid, 0, rows]
        d = shift_ref[kid, 1, rows]
        one, two = c * a - d * b, c * b + d * a
        real = one if real is None else real + one
        imag = two if imag is None else imag + two
    return real, imag


def edge_forward_kernel(
    codes_src, far_ref, near_ref, phi_high_ref, phi_low_ref, edge_high_ref, edge_low_ref,
    shift_ref, packed_ref, out_ref, codes_ref, halo_ref, fine_ref, sem,
):
    codes = pltpu.make_async_copy(codes_src, codes_ref, sem)
    codes.start()
    even = even_strip()
    for side in range(2):
        lanes = slice(128 * side, 128 * side + 128)
        for row in range(4):
            far, near = far_ref[row, :, lanes], near_ref[row, :, lanes]
            halo_ref[side, pl.ds(row, PLANES, stride=8), :] = jnp.where(even, far, near)
            halo_ref[side, pl.ds(row + 4, PLANES, stride=8), :] = jnp.where(even, near, far)
    phi = (phi_high_ref[...], phi_low_ref[...])
    edge = (edge_high_ref[...], edge_low_ref[...])
    for parent in range(2):
        mixed = dot3(halves(both_sides(halo_ref, 128 * parent, 128)), phi)
        fine_ref[256 * parent : 256 * (parent + 1)] = dot3(edge, halves(mixed))
    out_ref[4:12] = packed_ref[4:12]
    for side in range(2):
        rows = slice(24 * side, 24 * side + 8)
        for parent in range(2):
            for pol in range(2):
                real, imag = gathered(fine_ref, shift_ref, parent, pol, 16, 8 * side, rows)
                for part, value in enumerate((real, imag)):
                    for pair, tile in enumerate(swap_blocks(lane_blocks(value))):
                        at = (12 * side + pair, parent, 2 * pol + part)
                        out_ref[at] = packed_ref[at] + tile
    codes.wait()


def spread_back(local_ref, shift_ref, parent, pol, blocks, high_ref, low_ref):
    parts = []
    for part in range(2):
        pieces = []
        for first in blocks:
            tiles = [local_ref[first + pair, parent, 2 * pol + part] for pair in range(4)]
            pieces.append(jnp.concatenate(swap_blocks(tiles), axis=1))
        parts.append(pieces)
    for kid in range(KIDS):
        real, imag = [], []
        for index, first in enumerate(blocks):
            a, b = parts[0][index], parts[1][index]
            rows = pl.ds(pl.multiple_of(2 * first, 8), 8)
            c, d = shift_ref[kid, 0, rows], shift_ref[kid, 1, rows]
            real.append(c * a + d * b)
            imag.append(c * b - d * a)
        height = 16 * len(blocks)
        at = ((parent * KIDS + kid) * 2 + pol) * height
        value = halves(jnp.concatenate(real + imag, axis=0))
        high_ref[at : at + height], low_ref[at : at + height] = value


def edge_back_kernel(far):
    def kernel(
        local_ref, shift_ref, phi_high_ref, phi_low_ref, table_high_ref, table_low_ref,
        out_ref, high_ref, low_ref, narrow_ref, result_ref,
    ):
        phi = (phi_high_ref[...], phi_low_ref[...])
        side = lax.rem(lax.axis_index("theta") + (0 if far else 1), 2)
        table = (table_high_ref[side], table_low_ref[side])
        first = side * 12
        for parent in range(2):
            for pol in range(2):
                spread_back(local_ref, shift_ref, parent, pol, (first,), high_ref, low_ref)
            rows = slice(128 * parent, 128 * (parent + 1))
            narrow = dot3(table, (high_ref[rows], low_ref[rows]))
            narrow_ref[64 * parent : 64 * (parent + 1)] = narrow
        result = dot3(halves(narrow_ref[...]), phi, contract=1)
        for half in range(2):
            lanes = slice(128 * half, 128 * half + 128)
            result_ref[half] = result[:, lanes]
            for row in range(4):
                rows = pl.ds(row, PLANES, stride=4)
                out_ref[row, :, lanes] = result_ref[half, rows, :]

    return kernel


def own_back_kernel(
    local_ref, shift_ref, phi_high_ref, phi_low_ref, table_high_ref, table_low_ref,
    own_ref, high_ref, low_ref,
):
    phi = (phi_high_ref[...], phi_low_ref[...])
    table = (table_high_ref[...], table_low_ref[...])

    for parent in range(2):
        for pol in range(2):
            spread_back(local_ref, shift_ref, parent, pol, (0, 4, 8, 12), high_ref, low_ref)
        for group in (2 * parent, 2 * parent + 1):
            rows = slice(256 * group, 256 * (group + 1))
            narrowed = dot3(table, (high_ref[rows], low_ref[rows]))
            result = dot3(halves(narrowed), phi, contract=1)
            for side in range(2):
                lanes = slice(128 * side, 128 * side + 128)
                own_ref[side, 128 * group : 128 * (group + 1)] = result[:, lanes]


def translate_kernel(codes_ref, counts_ref, field_ref, operator_ref, out_ref, table_ref):
    parents = counts_ref.shape[0]
    kinds = operator_ref.shape[0] // 16
    for kind in range(kinds):
        c = operator_ref[16 * kind : 16 * kind + 8]
        d = operator_ref[16 * kind + 8 : 16 * kind + 16]
        for at, value in enumerate((c, d - c, c + d)):
            table_ref[24 * kind + 8 * at : 24 * kind + 8 * at + 8] = value
    table_ref[24 * kinds : 24 * kinds + 24] = jnp.zeros((24, 128), WHOLE)

    def one_pair(pair, carry):
        def some_slots(step, sums):
            sums = list(sums)
            for member in range(PAIR):
                for lane in range(GROUP):
                    slot = pair * (PAIR * LIST) + step * GROUP + (member * LIST + lane)
                    code = codes_ref[slot]
                    source = pl.multiple_of(code & 0xFFFF, 8)
                    offset = pl.multiple_of(code >> 16, 8)
                    c = table_ref[pl.ds(offset, 8), :]
                    less = table_ref[pl.ds(offset + 8, 8), :]
                    more = table_ref[pl.ds(offset + 16, 8), :]
                    for pol in range(2):
                        at = member * 6 + pol * 3
                        a = field_ref[pl.ds(source + pol * 16, 8), :]
                        b = field_ref[pl.ds(source + (pol * 16 + 8), 8), :]
                        sums[at] = sums[at] + c * (a + b)
                        sums[at + 1] = sums[at + 1] + a * less
                        sums[at + 2] = sums[at + 2] + b * more
            return tuple(sums)

        zero = jnp.zeros((8, 128), WHOLE)
        longest = jnp.maximum(counts_ref[pair * PAIR], counts_ref[pair * PAIR + 1])
        steps = lax.shift_right_logical(longest + (GROUP - 1), 3)
        sums = lax.fori_loop(0, steps, some_slots, (zero,) * (6 * PAIR))
        for member in range(PAIR):
            for pol in range(2):
                both, less, more = sums[member * 6 + pol * 3 : member * 6 + pol * 3 + 3]
                at = pl.multiple_of(pair * 64 + member * 32 + pol * 16, 8)
                out_ref[pl.ds(at, 8), :] = both - more
                out_ref[pl.ds(at + 8, 8), :] = both + less
        return carry

    lax.fori_loop(0, parents // PAIR, one_pair, 0)


def in_vmem(value):
    return pltpu.with_memory_space_constraint(value, pltpu.VMEM)


def in_smem(value):
    return pltpu.with_memory_space_constraint(value, pltpu.SMEM)


def in_hbm(value):
    return pltpu.with_memory_space_constraint(value, pltpu.HBM)


def call(kernel, name, outs, scratch, *operands, raw=0, out_specs=None):
    vmem = pl.BlockSpec(memory_space=pltpu.VMEM)
    hbm = pl.BlockSpec(memory_space=pltpu.HBM)
    return pl.pallas_call(
        kernel,
        out_shape=outs,
        in_specs=[hbm] * raw + [vmem] * (len(operands) - raw),
        out_specs=out_specs if out_specs is not None else jax.tree.map(lambda _: vmem, outs),
        scratch_shapes=scratch,
        compiler_params=pltpu.CompilerParams(vmem_limit_bytes=GRANT),
        name=name,
    )(*map(in_hbm, operands[:raw]), *map(in_vmem, operands[raw:]))


def operator_rows(translators):
    kinds, _, rows, samples = translators.shape
    table = translators.reshape(kinds, 2, rows, samples // 128, 128).transpose(0, 1, 3, 2, 4)
    return table.reshape(kinds * 16, 128)


def translate(field, codes, counts, operators):
    smem = pl.BlockSpec(memory_space=pltpu.SMEM)
    vmem = pl.BlockSpec(memory_space=pltpu.VMEM)
    field = field.reshape(-1, 128)
    return pl.pallas_call(
        translate_kernel,
        out_shape=jax.ShapeDtypeStruct(field.shape, WHOLE),
        in_specs=[smem, smem, vmem, vmem],
        out_specs=vmem,
        scratch_shapes=[pltpu.VMEM((operators.shape[0] * 3 // 2 + 24, 128), WHOLE)],
        compiler_params=pltpu.CompilerParams(vmem_limit_bytes=GRANT),
        name="translate",
    )(in_smem(codes), in_smem(counts), in_vmem(field), in_vmem(operators))


def merge_kernel(own_ref, far_ref, near_ref, out_hbm, out_ref, sems):
    even = even_strip()
    copies = []
    for i in range(4):
        chunk = slice(128 * i, 128 * i + 128)
        for side in range(2):
            lanes = slice(128 * side, 128 * side + 128)
            out_ref[side, chunk] = own_ref[side, chunk]
            for row in range(4):
                far = far_ref[row, 8 * i : 8 * i + 8, lanes]
                near = near_ref[row, 8 * i : 8 * i + 8, lanes]
                top = pl.ds(128 * i + row, 8, stride=OWN)
                bottom = pl.ds(128 * i + OWN - 4 + row, 8, stride=OWN)
                out_ref[side, top, :] = own_ref[side, top, :] + jnp.where(even, far, near)
                out_ref[side, bottom, :] = own_ref[side, bottom, :] + jnp.where(even, near, far)
            target = out_hbm.at[chunk, lanes]
            copy = pltpu.make_async_copy(out_ref.at[side, chunk], target, sems.at[2 * i + side])
            copy.start()
            copies.append(copy)
    for copy in copies:
        copy.wait()


def on_device(
    children, theta_band, phi_interp, child_shift, translators, far_source, far_offset, far_count
):
    half = lambda *shape: pltpu.VMEM(shape, HALF)
    whole = lambda *shape: pltpu.VMEM(shape, WHOLE)
    hbm = pl.BlockSpec(memory_space=pl.ANY)
    vmem = pl.BlockSpec(memory_space=pltpu.VMEM)
    smem = pl.BlockSpec(memory_space=pltpu.SMEM)
    dma = pltpu.SemaphoreType.DMA
    planes, taps, far, near = call(
        cut_kernel, "cut",
        (whole(2, PLANES * OWN, 128), whole(8, ROWS)) + (whole(4, PLANES, PHI),) * 2,
        [dma((9,))], children.reshape(-1, PHI), theta_band.T, raw=2,
    )
    far = swapped(far, True)
    near = swapped(near, False)
    tables = (half(256, 512),) * 2 + (half(256, 128),) * 2 + (half(128, 256),) * 2
    packed, *tables, codes, counts = call(
        functools.partial(own_forward_kernel, kinds=translators.shape[0]), "own_forward",
        (whole(16, 2, 4, 8, 128),) + tables + (half(2, 64, 128),) * 2
        + (pltpu.VMEM(far_source.shape, jnp.int32), pltpu.SMEM(far_count.shape, jnp.int32)),
        [
            whole(1024, SAMPLES), whole(PHI, SAMPLES), pltpu.VMEM(far_source.shape, jnp.int32),
            pltpu.VMEM(far_source.shape, jnp.int32), dma((4,)),
        ],
        phi_interp, far_source, far_offset, far_count, taps, planes, child_shift,
        raw=4, out_specs=(vmem,) * 10 + (smem,),
    )
    phi, edge, back, sides = (tables[i : i + 2] for i in range(0, 8, 2))
    operators = in_vmem(operator_rows(translators))
    packed, codes = call(
        edge_forward_kernel, "edge_forward",
        (whole(16, 2, 4, 8, 128), pltpu.SMEM((codes.size,), jnp.int32)),
        [whole(2, 256, 128), whole(512, SAMPLES), dma],
        codes.reshape(-1), far, near, *phi, *edge, child_shift, packed, out_specs=(vmem, smem),
    )
    packed, operators = lax.optimization_barrier((packed, operators))
    field = lax.all_to_all(packed, "clus", 0, 0)
    summed = translate(field, codes, counts, operators)
    local = lax.all_to_all(summed.reshape(packed.shape), "clus", 0, 0)
    scratch = [half(256, SAMPLES)] * 2 + [whole(128, SAMPLES), whole(2, 128, 128)]
    far, near = (
        swapped(
            call(
                edge_back_kernel(side), "edge_back", whole(4, PLANES, PHI), scratch,
                local, child_shift, *phi, *sides,
            ),
            side,
        )
        for side in (True, False)
    )
    own = call(
        own_back_kernel, "own_back", whole(2, PLANES * OWN, 128), [half(1024, SAMPLES)] * 2,
        local, child_shift, *phi, *back,
    )
    result = call(
        merge_kernel, "merge", jax.ShapeDtypeStruct((PLANES * OWN, PHI), WHOLE),
        [whole(2, PLANES * OWN, 128), dma((8,))], own, far, near, out_specs=hbm,
    )
    return result.reshape(children.shape)


def solution(mesh):
    return jax.shard_map(
        on_device,
        mesh=mesh,
        in_specs=(
            P("clus", None, None, "theta", None),
            P("theta", None),
            P(),
            P(None, None, "theta", None),
            P(None, None, ("theta", "clus"), None),
            P(),
            P(),
            P(),
        ),
        out_specs=P("clus", None, None, "theta", None),
        check_vma=False,
    )
```

```python
import functools

import jax
import jax.numpy as jnp
from jax import lax
from jax.experimental import pallas as pl
from jax.experimental.pallas import tpu as pltpu
from jax.sharding import PartitionSpec as P


KIDS = 4
LIST = 32
GROUP = 8
PAIR = 2
PLANES = 32
ROWS = 32
OWN = 16
PHI = 256
SAMPLES = 512
GRANT = 12 * 2**20
HALF = jnp.bfloat16
WHOLE = jnp.float32


def shifted_ring(value, axis, step):
    count = lax.axis_size(axis)
    return lax.ppermute(value, axis, [(i, (i + step) % count) for i in range(count)])


def halves(value):
    high = value.astype(HALF)
    return high, (value - high.astype(WHOLE)).astype(HALF)


def dot3(left, right, contract=0):
    dims = (((1,), (contract,)), ((), ()))
    total = None
    for a, b in ((0, 0), (0, 1), (1, 0)):
        part = lax.dot_general(left[a], right[b], dims, preferred_element_type=WHOLE)
        total = part if total is None else total + part
    return total


def swap_blocks(tiles):
    sub = lax.broadcasted_iota(jnp.int32, (8, 128), 0)
    even = (sub // 2) % 2 == 0
    low = sub < 4
    a, b, c, d = tiles

    def step(first, second, shift, mask):
        one = jnp.where(mask, first, pltpu.roll(second, shift, 0))
        two = jnp.where(mask, pltpu.roll(first, 8 - shift, 0), second)
        return one, two

    a, b = step(a, b, 2, even)
    c, d = step(c, d, 2, even)
    a, c = step(a, c, 4, low)
    b, d = step(b, d, 4, low)
    return a, b, c, d


def lane_blocks(value):
    return [value[:, 128 * i : 128 * (i + 1)] for i in range(4)]


def tiled(bands, outer, width):
    row = lax.broadcasted_iota(jnp.int32, (outer, width), 0)
    column = lax.broadcasted_iota(jnp.int32, (outer, width), 1)
    pick = (row == column % outer).astype(HALF)
    return [jnp.dot(part, pick, preferred_element_type=WHOLE) for part in halves(bands)]


def band_tables(bands, planes, inner, outer, place):
    shape = (planes * inner, planes * outer)
    row = lax.broadcasted_iota(jnp.int32, shape, 0)
    column = lax.broadcasted_iota(jnp.int32, shape, 1)
    child, parent = place(row % inner, column % outer)
    tap = child - parent // 2 + 3
    tap = jnp.where(row // inner == column // outer, tap, -1)
    tables = []
    for part in tiled(bands, outer, shape[1]):
        table = jnp.zeros(shape, WHOLE)
        for t in range(8):
            table = jnp.where(tap == t, jnp.broadcast_to(part[t : t + 1], shape), table)
        tables.append(table)
    return tables


def edge_rows(child, parent):
    child = jnp.where(child < 4, child - 4, child + 12)
    return child, jnp.where(parent < 8, parent, parent + 16)


def cut_kernel(
    children_hbm, taps_hbm, phi_hbm, children_ref, taps_ref, phi_ref, upper_ref, lower_ref, sems
):
    chunks = [slice(128 * i, 128 * i + 128) for i in range(4)]
    copies = [
        pltpu.make_async_copy(
            children_hbm.at[chunk, 128 * side : 128 * side + 128],
            children_ref.at[side, chunk],
            sems.at[2 * i + side],
        )
        for i, chunk in enumerate(chunks)
        for side in range(2)
    ]
    for copy in copies:
        copy.start()
    taps = pltpu.make_async_copy(taps_hbm, taps_ref, sems.at[8])
    taps.start()
    phi = pltpu.make_async_copy(phi_hbm, phi_ref, sems.at[9])
    phi.start()
    for at, copy in enumerate(copies):
        copy.wait()
        i, side = divmod(at, 2)
        for ref, first, count in ((upper_ref, 0, 4), (lower_ref, OWN - 3, 3)):
            for row in range(count):
                rows = pl.ds(128 * i + first + row, 8, stride=OWN)
                value = children_ref[side, rows, :]
                ref[row, 8 * i : 8 * i + 8, 128 * side : 128 * side + 128] = value
    taps.wait()
    phi.wait()


def both_sides(ref, first, count):
    return jnp.concatenate([ref[side, first : first + count] for side in range(2)], axis=1)


def own_forward_kernel(
    source_hbm, offset_hbm, counts_hbm, phi_ref, taps_ref, children_ref, shift_ref,
    packed_ref, phi_high_ref, phi_low_ref, edge_high_ref, edge_low_ref, back_high_ref, back_low_ref,
    up_high_ref, up_low_ref, down_high_ref, down_low_ref, codes_ref, counts_ref,
    fine_ref, source_ref, offset_ref, sems, *, kinds,
):
    pairs = ((source_hbm, source_ref), (offset_hbm, offset_ref), (counts_hbm, counts_ref))
    copies = [pltpu.make_async_copy(*pair, sems.at[i]) for i, pair in enumerate(pairs)]
    for copy in copies:
        copy.start()
    strip = lax.axis_index("theta")
    first = (strip > 0).astype(WHOLE)
    last = (strip < lax.axis_size("theta") - 1).astype(WHOLE)
    taps = taps_ref[...]
    table = band_tables(taps, 8, 16, 32, lambda child, parent: (child, parent))
    own = []
    for part, ref in zip(table, (back_high_ref, back_low_ref)):
        ref[...] = part.astype(HALF)
        own.append(part.T.astype(HALF))
    phi = halves(phi_ref[...])
    phi_high_ref[...], phi_low_ref[...] = phi
    for group in range(4):
        mixed = dot3(halves(both_sides(children_ref, 128 * group, 128)), phi)
        fine_ref[256 * group : 256 * (group + 1)] = dot3(own, halves(mixed))
    for copy in copies:
        copy.wait()
    lane = lax.broadcasted_iota(jnp.int32, (1, LIST), 1)
    for parent in range(source_ref.shape[0]):
        live = lane < counts_ref[parent]
        offset = jnp.where(live, offset_ref[parent : parent + 1], kinds)
        codes_ref[parent : parent + 1] = source_ref[parent : parent + 1] * 32 + offset * (24 * 65536)
    upper, lower = taps[:, :8] * first, taps[:, ROWS - 8 :] * last
    table = band_tables(jnp.concatenate([upper, lower], axis=1), 16, 8, 16, edge_rows)
    for part, ref in zip(table, (edge_high_ref, edge_low_ref)):
        ref[...] = part.T.astype(HALF)
    table = band_tables(upper, 16, 4, 8, lambda child, parent: (child - 4, parent))
    for part, ref in zip(table, (up_high_ref, up_low_ref)):
        ref[...] = part.astype(HALF)
    table = band_tables(lower, 16, 4, 8, lambda child, parent: (child + 16, parent + 24))
    for part, ref in zip(table, (down_high_ref, down_low_ref)):
        ref[...] = part.astype(HALF)
    for parent in range(2):
        for pol in range(2):
            for block in range(4):
                rows = slice(8 * block, 8 * (block + 1))
                real, imag = gathered(fine_ref, shift_ref, parent, pol, 32, 8 * block, rows)
                for part, value in enumerate((real, imag)):
                    for pair, tile in enumerate(swap_blocks(lane_blocks(value))):
                        packed_ref[4 * block + pair, parent, 2 * pol + part] = tile


def gathered(fine_ref, shift_ref, parent, pol, per_plane, first, rows):
    real = imag = None
    for kid in range(KIDS):
        at = ((parent * KIDS + kid) * 4 + pol * 2) * per_plane + first
        a = fine_ref[at : at + 8]
        b = fine_ref[at + per_plane : at + per_plane + 8]
        c = shift_ref[kid, 0, rows]
        d = shift_ref[kid, 1, rows]
        one, two = c * a - d * b, c * b + d * a
        real = one if real is None else real + one
        imag = two if imag is None else imag + two
    return real, imag


def edge_forward_kernel(
    codes_src, above_ref, below_ref, phi_high_ref, phi_low_ref, edge_high_ref, edge_low_ref,
    shift_ref, packed_ref, out_ref, codes_ref, halo_ref, fine_ref, sem,
):
    codes = pltpu.make_async_copy(codes_src, codes_ref, sem)
    codes.start()
    for side in range(2):
        lanes = slice(128 * side, 128 * side + 128)
        halo_ref[side, pl.ds(0, PLANES, stride=8), :] = jnp.zeros((PLANES, 128), WHOLE)
        for row in range(3):
            halo_ref[side, pl.ds(row + 1, PLANES, stride=8), :] = above_ref[row, :, lanes]
        for row in range(4):
            halo_ref[side, pl.ds(row + 4, PLANES, stride=8), :] = below_ref[row, :, lanes]
    phi = (phi_high_ref[...], phi_low_ref[...])
    edge = (edge_high_ref[...], edge_low_ref[...])
    for parent in range(2):
        mixed = dot3(halves(both_sides(halo_ref, 128 * parent, 128)), phi)
        fine_ref[256 * parent : 256 * (parent + 1)] = dot3(edge, halves(mixed))
    out_ref[4:12] = packed_ref[4:12]
    for side in range(2):
        rows = slice(24 * side, 24 * side + 8)
        for parent in range(2):
            for pol in range(2):
                real, imag = gathered(fine_ref, shift_ref, parent, pol, 16, 8 * side, rows)
                for part, value in enumerate((real, imag)):
                    for pair, tile in enumerate(swap_blocks(lane_blocks(value))):
                        at = (12 * side + pair, parent, 2 * pol + part)
                        out_ref[at] = packed_ref[at] + tile
    codes.wait()


def spread_back(local_ref, shift_ref, parent, pol, blocks, high_ref, low_ref):
    parts = []
    for part in range(2):
        pieces = []
        for first in blocks:
            tiles = [local_ref[first + pair, parent, 2 * pol + part] for pair in range(4)]
            pieces.append(jnp.concatenate(swap_blocks(tiles), axis=1))
        parts.append(pieces)
    for kid in range(KIDS):
        real, imag = [], []
        for index, first in enumerate(blocks):
            a, b = parts[0][index], parts[1][index]
            c = shift_ref[kid, 0, 2 * first : 2 * first + 8]
            d = shift_ref[kid, 1, 2 * first : 2 * first + 8]
            real.append(c * a + d * b)
            imag.append(c * b - d * a)
        height = 16 * len(blocks)
        at = ((parent * KIDS + kid) * 2 + pol) * height
        value = halves(jnp.concatenate(real + imag, axis=0))
        high_ref[at : at + height], low_ref[at : at + height] = value


def edge_back_kernel(first, skipped):
    def kernel(
        local_ref, shift_ref, phi_high_ref, phi_low_ref, table_high_ref, table_low_ref,
        out_ref, high_ref, low_ref, narrow_ref, result_ref,
    ):
        phi = (phi_high_ref[...], phi_low_ref[...])
        table = (table_high_ref[...], table_low_ref[...])
        for parent in range(2):
            for pol in range(2):
                spread_back(local_ref, shift_ref, parent, pol, (first,), high_ref, low_ref)
            rows = slice(128 * parent, 128 * (parent + 1))
            narrow = dot3(table, (high_ref[rows], low_ref[rows]))
            narrow_ref[64 * parent : 64 * (parent + 1)] = narrow
        result = dot3(halves(narrow_ref[...]), phi, contract=1)
        for side in range(2):
            lanes = slice(128 * side, 128 * side + 128)
            result_ref[side] = result[:, lanes]
            for row in range(4 - skipped):
                rows = pl.ds(row + skipped, PLANES, stride=4)
                out_ref[row, :, lanes] = result_ref[side, rows, :]

    return kernel


def own_back_kernel(
    local_ref, shift_ref, phi_high_ref, phi_low_ref, table_high_ref, table_low_ref,
    own_ref, high_ref, low_ref,
):
    phi = (phi_high_ref[...], phi_low_ref[...])
    table = (table_high_ref[...], table_low_ref[...])

    for parent in range(2):
        for pol in range(2):
            spread_back(local_ref, shift_ref, parent, pol, (0, 4, 8, 12), high_ref, low_ref)
        for group in (2 * parent, 2 * parent + 1):
            rows = slice(256 * group, 256 * (group + 1))
            narrowed = dot3(table, (high_ref[rows], low_ref[rows]))
            result = dot3(halves(narrowed), phi, contract=1)
            for side in range(2):
                lanes = slice(128 * side, 128 * side + 128)
                own_ref[side, 128 * group : 128 * (group + 1)] = result[:, lanes]


def translate_kernel(codes_ref, counts_ref, field_ref, operator_ref, out_ref, table_ref):
    parents = counts_ref.shape[0]
    kinds = operator_ref.shape[0] // 16
    for kind in range(kinds):
        c = operator_ref[16 * kind : 16 * kind + 8]
        d = operator_ref[16 * kind + 8 : 16 * kind + 16]
        for at, value in enumerate((c, d - c, c + d)):
            table_ref[24 * kind + 8 * at : 24 * kind + 8 * at + 8] = value
    table_ref[24 * kinds : 24 * kinds + 24] = jnp.zeros((24, 128), WHOLE)

    def one_pair(pair, carry):
        def some_slots(step, sums):
            sums = list(sums)
            for member in range(PAIR):
                for lane in range(GROUP):
                    slot = pair * (PAIR * LIST) + step * GROUP + (member * LIST + lane)
                    code = codes_ref[slot]
                    source = pl.multiple_of(code & 0xFFFF, 8)
                    offset = pl.multiple_of(code >> 16, 8)
                    c = table_ref[pl.ds(offset, 8), :]
                    less = table_ref[pl.ds(offset + 8, 8), :]
                    more = table_ref[pl.ds(offset + 16, 8), :]
                    for pol in range(2):
                        at = member * 6 + pol * 3
                        a = field_ref[pl.ds(source + pol * 16, 8), :]
                        b = field_ref[pl.ds(source + (pol * 16 + 8), 8), :]
                        sums[at] = sums[at] + c * (a + b)
                        sums[at + 1] = sums[at + 1] + a * less
                        sums[at + 2] = sums[at + 2] + b * more
            return tuple(sums)

        zero = jnp.zeros((8, 128), WHOLE)
        longest = jnp.maximum(counts_ref[pair * PAIR], counts_ref[pair * PAIR + 1])
        steps = lax.shift_right_logical(longest + (GROUP - 1), 3)
        sums = lax.fori_loop(0, steps, some_slots, (zero,) * (6 * PAIR))
        for member in range(PAIR):
            for pol in range(2):
                both, less, more = sums[member * 6 + pol * 3 : member * 6 + pol * 3 + 3]
                at = pl.multiple_of(pair * 64 + member * 32 + pol * 16, 8)
                out_ref[pl.ds(at, 8), :] = both - more
                out_ref[pl.ds(at + 8, 8), :] = both + less
        return carry

    lax.fori_loop(0, parents // PAIR, one_pair, 0)


def in_vmem(value):
    return pltpu.with_memory_space_constraint(value, pltpu.VMEM)


def in_smem(value):
    return pltpu.with_memory_space_constraint(value, pltpu.SMEM)


def in_hbm(value):
    return pltpu.with_memory_space_constraint(value, pltpu.HBM)


def call(kernel, outs, scratch, *operands, raw=0, out_specs=None):
    vmem = pl.BlockSpec(memory_space=pltpu.VMEM)
    hbm = pl.BlockSpec(memory_space=pltpu.HBM)
    return pl.pallas_call(
        kernel,
        out_shape=outs,
        in_specs=[hbm] * raw + [vmem] * (len(operands) - raw),
        out_specs=out_specs if out_specs is not None else jax.tree.map(lambda _: vmem, outs),
        scratch_shapes=scratch,
        compiler_params=pltpu.CompilerParams(vmem_limit_bytes=GRANT),
    )(*map(in_hbm, operands[:raw]), *map(in_vmem, operands[raw:]))


def operator_rows(translators):
    kinds, _, rows, samples = translators.shape
    table = translators.reshape(kinds, 2, rows, samples // 128, 128).transpose(0, 1, 3, 2, 4)
    return table.reshape(kinds * 16, 128)


def translate(field, codes, counts, operators):
    smem = pl.BlockSpec(memory_space=pltpu.SMEM)
    vmem = pl.BlockSpec(memory_space=pltpu.VMEM)
    field = field.reshape(-1, 128)
    return pl.pallas_call(
        translate_kernel,
        out_shape=jax.ShapeDtypeStruct(field.shape, WHOLE),
        in_specs=[smem, smem, vmem, vmem],
        out_specs=vmem,
        scratch_shapes=[pltpu.VMEM((operators.shape[0] * 3 // 2 + 24, 128), WHOLE)],
        compiler_params=pltpu.CompilerParams(vmem_limit_bytes=GRANT),
        name="translate",
    )(in_smem(codes), in_smem(counts), in_vmem(field), in_vmem(operators))


def merge_kernel(own_ref, top_ref, bottom_ref, out_hbm, out_ref, sems):
    copies = []
    for i in range(4):
        chunk = slice(128 * i, 128 * i + 128)
        for side in range(2):
            lanes = slice(128 * side, 128 * side + 128)
            out_ref[side, chunk] = own_ref[side, chunk]
            for ref, first, count in ((top_ref, 0, 4), (bottom_ref, OWN - 3, 3)):
                for row in range(count):
                    rows = pl.ds(128 * i + first + row, 8, stride=OWN)
                    value = own_ref[side, rows, :] + ref[row, 8 * i : 8 * i + 8, lanes]
                    out_ref[side, rows, :] = value
            target = out_hbm.at[chunk, lanes]
            copy = pltpu.make_async_copy(out_ref.at[side, chunk], target, sems.at[2 * i + side])
            copy.start()
            copies.append(copy)
    for copy in copies:
        copy.wait()


def on_device(
    children, theta_band, phi_interp, child_shift, translators, far_source, far_offset, far_count
):
    half = lambda *shape: pltpu.VMEM(shape, HALF)
    whole = lambda *shape: pltpu.VMEM(shape, WHOLE)
    hbm = pl.BlockSpec(memory_space=pl.ANY)
    vmem = pl.BlockSpec(memory_space=pltpu.VMEM)
    smem = pl.BlockSpec(memory_space=pltpu.SMEM)
    dma = pltpu.SemaphoreType.DMA
    planes, taps, phi, upper, lower = call(
        cut_kernel,
        (
            whole(2, PLANES * OWN, 128), whole(8, ROWS), whole(*phi_interp.shape),
            whole(4, PLANES, PHI), whole(3, PLANES, PHI),
        ),
        [dma((10,))], children.reshape(-1, PHI), theta_band.T, phi_interp, raw=3,
    )
    above = shifted_ring(lower, "theta", 1)
    below = shifted_ring(upper, "theta", -1)
    tables = (half(256, 512),) * 2 + (half(256, 128),) * 2 + (half(128, 256),) * 2
    packed, *tables, codes, counts = call(
        functools.partial(own_forward_kernel, kinds=translators.shape[0]),
        (whole(16, 2, 4, 8, 128),) + tables + (half(64, 128),) * 4
        + (pltpu.VMEM(far_source.shape, jnp.int32), pltpu.SMEM(far_count.shape, jnp.int32)),
        [
            whole(1024, SAMPLES), pltpu.VMEM(far_source.shape, jnp.int32),
            pltpu.VMEM(far_source.shape, jnp.int32), dma((3,)),
        ],
        far_source, far_offset, far_count, phi, taps, planes, child_shift,
        raw=3, out_specs=(vmem,) * 12 + (smem,),
    )
    phi, edge, back, up_table, down_table = (tables[i : i + 2] for i in range(0, 10, 2))
    operators = in_vmem(operator_rows(translators))
    packed, codes = call(
        edge_forward_kernel,
        (whole(16, 2, 4, 8, 128), pltpu.SMEM((codes.size,), jnp.int32)),
        [whole(2, 256, 128), whole(512, SAMPLES), dma],
        codes.reshape(-1), above, below, *phi, *edge, child_shift, packed, out_specs=(vmem, smem),
    )
    packed, operators = lax.optimization_barrier((packed, operators))
    field = lax.all_to_all(packed, "clus", 0, 0)
    summed = translate(field, codes, counts, operators)
    local = lax.all_to_all(summed.reshape(packed.shape), "clus", 0, 0)
    scratch = [half(256, SAMPLES)] * 2 + [whole(128, SAMPLES), whole(2, 128, 128)]
    down = call(
        edge_back_kernel(12, 0), whole(4, PLANES, PHI), scratch,
        local, child_shift, *phi, *down_table,
    )
    from_below = shifted_ring(down, "theta", 1)
    up = call(
        edge_back_kernel(0, 1), whole(3, PLANES, PHI), scratch,
        local, child_shift, *phi, *up_table,
    )
    from_above = shifted_ring(up, "theta", -1)
    own = call(
        own_back_kernel, whole(2, PLANES * OWN, 128), [half(1024, SAMPLES)] * 2,
        local, child_shift, *phi, *back,
    )
    result = call(
        merge_kernel, jax.ShapeDtypeStruct((PLANES * OWN, PHI), WHOLE),
        [whole(2, PLANES * OWN, 128), dma((8,))], own, from_below, from_above, out_specs=hbm,
    )
    return result.reshape(children.shape)


def solution(mesh):
    return jax.shard_map(
        on_device,
        mesh=mesh,
        in_specs=(
            P("clus", None, None, "theta", None),
            P("theta", None),
            P(),
            P(None, None, "theta", None),
            P(None, None, ("theta", "clus"), None),
            P(),
            P(),
            P(),
        ),
        out_specs=P("clus", None, None, "theta", None),
        check_vma=False,
    )
```

```python
import functools

import jax
import jax.numpy as jnp
from jax import lax
from jax.experimental import pallas as pl
from jax.experimental.pallas import tpu as pltpu
from jax.sharding import PartitionSpec as P


KIDS = 4
LIST = 32
GROUP = 8
PAIR = 2
PLANES = 32
ROWS = 32
OWN = 16
PHI = 256
SAMPLES = 512
GRANT = 12 * 2**20
HALF = jnp.bfloat16
WHOLE = jnp.float32


def shifted_ring(value, axis, step):
    count = lax.axis_size(axis)
    return lax.ppermute(value, axis, [(i, (i + step) % count) for i in range(count)])


def halves(value):
    high = value.astype(HALF)
    return high, (value - high.astype(WHOLE)).astype(HALF)


def dot3(left, right, contract=0):
    dims = (((1,), (contract,)), ((), ()))
    total = None
    for a, b in ((0, 0), (0, 1), (1, 0)):
        part = lax.dot_general(left[a], right[b], dims, preferred_element_type=WHOLE)
        total = part if total is None else total + part
    return total


def swap_blocks(tiles):
    sub = lax.broadcasted_iota(jnp.int32, (8, 128), 0)
    even = (sub // 2) % 2 == 0
    low = sub < 4
    a, b, c, d = tiles

    def step(first, second, shift, mask):
        one = jnp.where(mask, first, pltpu.roll(second, shift, 0))
        two = jnp.where(mask, pltpu.roll(first, 8 - shift, 0), second)
        return one, two

    a, b = step(a, b, 2, even)
    c, d = step(c, d, 2, even)
    a, c = step(a, c, 4, low)
    b, d = step(b, d, 4, low)
    return a, b, c, d


def lane_blocks(value):
    return [value[:, 128 * i : 128 * (i + 1)] for i in range(4)]


def table_times(table, value):
    wide = jnp.dot(table, jnp.concatenate([value[0], value[0]], axis=0), preferred_element_type=WHOLE)
    depth = table.shape[1] // 2
    return wide + jnp.dot(table[:, :depth], value[1], preferred_element_type=WHOLE)


def same(child, parent):
    return child, parent


def edge_rows(child, parent):
    child = jnp.where(child < 4, child - 4, child + 12)
    return child, jnp.where(parent < 8, parent, parent + 16)


def tap_of(child, parent, place):
    child, parent = place(child, parent)
    return child - parent // 2 + 3


def forward_table(bands, planes, inner, place):
    outer = bands.shape[0]
    width = planes * inner
    row = lax.broadcasted_iota(jnp.int32, (outer, width), 0)
    column = lax.broadcasted_iota(jnp.int32, (outer, width), 1)
    tap = tap_of(column % inner, row, place)
    block = jnp.zeros((outer, width), WHOLE)
    for t in range(8):
        block = jnp.where(tap == t, jnp.broadcast_to(bands[:, t : t + 1], block.shape), block)
    owner = column // inner
    blocks = [jnp.where(owner == plane, block, 0.0) for plane in range(planes)]
    return jnp.concatenate(blocks, axis=0)


def backward_table(bands, planes, inner, place):
    outer = bands.shape[1]
    width = planes * outer
    high = max(inner, 8)
    pick = lax.broadcasted_iota(jnp.int32, (outer, width), 1) % outer
    pick = (lax.broadcasted_iota(jnp.int32, (outer, width), 0) == pick).astype(HALF)
    row = lax.broadcasted_iota(jnp.int32, (high, width), 0)
    column = lax.broadcasted_iota(jnp.int32, (high, width), 1)
    tap = tap_of(row % inner, column % outer, place)
    tables = []
    for part in halves(bands):
        tiled = jnp.dot(part, pick, preferred_element_type=WHOLE)
        block = jnp.zeros((high, width), WHOLE)
        for t in range(8):
            block = jnp.where(tap == t, jnp.broadcast_to(tiled[t : t + 1], block.shape), block)
        owner = column // outer - row // inner
        step = high // inner
        blocks = [jnp.where(owner == plane, block, 0.0) for plane in range(0, planes, step)]
        tables.append(jnp.concatenate(blocks, axis=0).astype(HALF))
    return tables


def cut_kernel(
    children_hbm, taps_hbm, phi_hbm, children_ref, taps_ref, phi_ref, upper_ref, lower_ref, sems
):
    chunks = [slice(128 * i, 128 * i + 128) for i in range(4)]
    copies = [
        pltpu.make_async_copy(
            children_hbm.at[chunk, 128 * side : 128 * side + 128],
            children_ref.at[side, chunk],
            sems.at[2 * i + side],
        )
        for i, chunk in enumerate(chunks)
        for side in range(2)
    ]
    for copy in copies:
        copy.start()
    taps = pltpu.make_async_copy(taps_hbm, taps_ref, sems.at[8])
    taps.start()
    phi = pltpu.make_async_copy(phi_hbm, phi_ref, sems.at[9])
    phi.start()
    for at, copy in enumerate(copies):
        copy.wait()
        i, side = divmod(at, 2)
        for ref, first, count in ((upper_ref, 0, 4), (lower_ref, OWN - 3, 3)):
            for row in range(count):
                rows = pl.ds(128 * i + first + row, 8, stride=OWN)
                value = children_ref[side, rows, :]
                ref[row, 8 * i : 8 * i + 8, 128 * side : 128 * side + 128] = value
    taps.wait()
    phi.wait()


def both_sides(ref, first, count):
    return jnp.concatenate([ref[side, first : first + count] for side in range(2)], axis=1)


def own_forward_kernel(
    source_hbm, offset_hbm, counts_hbm, phi_ref, taps_ref, children_ref, shift_ref,
    packed_ref, phi_high_ref, phi_low_ref, edge_ref, back_high_ref, back_low_ref,
    up_ref, down_ref, codes_ref, counts_ref,
    fine_ref, source_ref, offset_ref, sems, *, kinds,
):
    pairs = ((source_hbm, source_ref), (offset_hbm, offset_ref), (counts_hbm, counts_ref))
    copies = [pltpu.make_async_copy(*pair, sems.at[i]) for i, pair in enumerate(pairs)]
    for copy in copies:
        copy.start()
    strip = lax.axis_index("theta")
    first = (strip > 0).astype(WHOLE)
    last = (strip < lax.axis_size("theta") - 1).astype(WHOLE)
    taps = taps_ref[...]
    bands = jnp.concatenate([taps] * 16, axis=0).T[:, :8]
    own = jnp.concatenate(halves(forward_table(bands, 8, 16, same)), axis=1)
    phi = halves(phi_ref[...])
    phi_high_ref[...], phi_low_ref[...] = phi

    def spread(group):
        mixed = dot3(halves(both_sides(children_ref, 128 * group, 128)), phi)
        fine_ref[256 * group : 256 * (group + 1)] = table_times(own, halves(mixed))

    def collect(parent):
        for pol in range(2):
            for block in range(4):
                rows = slice(8 * block, 8 * (block + 1))
                real, imag = gathered(fine_ref, shift_ref, parent, pol, 32, 8 * block, rows)
                for part, value in enumerate((real, imag)):
                    for pair, tile in enumerate(swap_blocks(lane_blocks(value))):
                        packed_ref[4 * block + pair, parent, 2 * pol + part] = tile

    for group in range(4):
        spread(group)
        if group == 2:
            collect(0)
    edge = jnp.concatenate([bands[:8] * first, bands[ROWS - 8 :] * last], axis=0)
    edge_ref[...] = jnp.concatenate(halves(forward_table(edge, 16, 8, edge_rows)), axis=1)
    back_high_ref[...], back_low_ref[...] = backward_table(taps, 8, 16, same)
    upper, lower = taps[:, :8] * first, taps[:, ROWS - 8 :] * last
    table = backward_table(upper, 16, 4, lambda child, parent: (child - 4, parent))
    up_ref[...] = jnp.concatenate(table, axis=1)
    table = backward_table(lower, 16, 4, lambda child, parent: (child + 16, parent + 24))
    down_ref[...] = jnp.concatenate(table, axis=1)
    for copy in copies:
        copy.wait()
    lane = lax.broadcasted_iota(jnp.int32, (1, LIST), 1)
    for parent in range(source_ref.shape[0]):
        live = lane < counts_ref[parent]
        offset = jnp.where(live, offset_ref[parent : parent + 1], kinds)
        codes_ref[parent : parent + 1] = source_ref[parent : parent + 1] * 32 + offset * (24 * 65536)
    collect(1)


def gathered(fine_ref, shift_ref, parent, pol, per_plane, first, rows):
    real = imag = None
    for kid in range(KIDS):
        at = ((parent * KIDS + kid) * 4 + pol * 2) * per_plane + first
        a = fine_ref[at : at + 8]
        b = fine_ref[at + per_plane : at + per_plane + 8]
        c = shift_ref[kid, 0, rows]
        d = shift_ref[kid, 1, rows]
        one, two = c * a - d * b, c * b + d * a
        real = one if real is None else real + one
        imag = two if imag is None else imag + two
    return real, imag


def edge_forward_kernel(
    codes_src, above_ref, below_ref, phi_high_ref, phi_low_ref, edge_ref,
    shift_ref, packed_ref, out_ref, codes_ref, halo_ref, fine_ref, sem,
):
    codes = pltpu.make_async_copy(codes_src, codes_ref, sem)
    codes.start()
    for side in range(2):
        lanes = slice(128 * side, 128 * side + 128)
        halo_ref[side, pl.ds(0, PLANES, stride=8), :] = jnp.zeros((PLANES, 128), WHOLE)
        for row in range(3):
            halo_ref[side, pl.ds(row + 1, PLANES, stride=8), :] = above_ref[row, :, lanes]
        for row in range(4):
            halo_ref[side, pl.ds(row + 4, PLANES, stride=8), :] = below_ref[row, :, lanes]
    phi = (phi_high_ref[...], phi_low_ref[...])
    edge = edge_ref[...]
    for parent in range(2):
        mixed = dot3(halves(both_sides(halo_ref, 128 * parent, 128)), phi)
        fine_ref[256 * parent : 256 * (parent + 1)] = table_times(edge, halves(mixed))
    out_ref[4:12] = packed_ref[4:12]
    for side in range(2):
        rows = slice(24 * side, 24 * side + 8)
        for parent in range(2):
            for pol in range(2):
                real, imag = gathered(fine_ref, shift_ref, parent, pol, 16, 8 * side, rows)
                for part, value in enumerate((real, imag)):
                    for pair, tile in enumerate(swap_blocks(lane_blocks(value))):
                        at = (12 * side + pair, parent, 2 * pol + part)
                        out_ref[at] = packed_ref[at] + tile
    codes.wait()


def spread_back(local_ref, shift_ref, parent, pol, blocks, high_ref, low_ref):
    parts = []
    for part in range(2):
        pieces = []
        for first in blocks:
            tiles = [local_ref[first + pair, parent, 2 * pol + part] for pair in range(4)]
            pieces.append(jnp.concatenate(swap_blocks(tiles), axis=1))
        parts.append(pieces)
    for kid in range(KIDS):
        real, imag = [], []
        for index, first in enumerate(blocks):
            a, b = parts[0][index], parts[1][index]
            c = shift_ref[kid, 0, 2 * first : 2 * first + 8]
            d = shift_ref[kid, 1, 2 * first : 2 * first + 8]
            real.append(c * a + d * b)
            imag.append(c * b - d * a)
        height = 16 * len(blocks)
        at = ((parent * KIDS + kid) * 2 + pol) * height
        value = halves(jnp.concatenate(real + imag, axis=0))
        high_ref[at : at + height], low_ref[at : at + height] = value


def edge_back_kernel(first, skipped):
    def kernel(
        local_ref, shift_ref, phi_high_ref, phi_low_ref, table_ref,
        out_ref, high_ref, low_ref, narrow_ref, result_ref,
    ):
        phi = (phi_high_ref[...], phi_low_ref[...])
        table = table_ref[...]
        for parent in range(2):
            for pol in range(2):
                spread_back(local_ref, shift_ref, parent, pol, (first,), high_ref, low_ref)
            rows = slice(128 * parent, 128 * (parent + 1))
            narrow = table_times(table, (high_ref[rows], low_ref[rows]))
            narrow_ref[64 * parent : 64 * (parent + 1)] = narrow
        result = dot3(halves(narrow_ref[...]), phi, contract=1)
        for side in range(2):
            lanes = slice(128 * side, 128 * side + 128)
            result_ref[side] = result[:, lanes]
            for row in range(4 - skipped):
                rows = pl.ds(row + skipped, PLANES, stride=4)
                out_ref[row, :, lanes] = result_ref[side, rows, :]

    return kernel


def own_back_kernel(
    local_ref, shift_ref, phi_high_ref, phi_low_ref, table_high_ref, table_low_ref,
    own_ref, high_ref, low_ref,
):
    phi = (phi_high_ref[...], phi_low_ref[...])
    table = (table_high_ref[...], table_low_ref[...])

    for parent in range(2):
        for pol in range(2):
            spread_back(local_ref, shift_ref, parent, pol, (0, 4, 8, 12), high_ref, low_ref)
        for group in (2 * parent, 2 * parent + 1):
            rows = slice(256 * group, 256 * (group + 1))
            narrowed = dot3(table, (high_ref[rows], low_ref[rows]))
            result = dot3(halves(narrowed), phi, contract=1)
            for side in range(2):
                lanes = slice(128 * side, 128 * side + 128)
                own_ref[side, 128 * group : 128 * (group + 1)] = result[:, lanes]


def translate_kernel(codes_ref, counts_ref, field_ref, operator_ref, out_ref, table_ref):
    parents = counts_ref.shape[0]
    kinds = operator_ref.shape[0] // 16
    for kind in range(kinds):
        c = operator_ref[16 * kind : 16 * kind + 8]
        d = operator_ref[16 * kind + 8 : 16 * kind + 16]
        for at, value in enumerate((c, d - c, c + d)):
            table_ref[24 * kind + 8 * at : 24 * kind + 8 * at + 8] = value
    table_ref[24 * kinds : 24 * kinds + 24] = jnp.zeros((24, 128), WHOLE)

    def one_pair(pair, carry):
        def some_slots(step, sums):
            sums = list(sums)
            for member in range(PAIR):
                for lane in range(GROUP):
                    slot = pair * (PAIR * LIST) + step * GROUP + (member * LIST + lane)
                    code = codes_ref[slot]
                    source = pl.multiple_of(code & 0xFFFF, 8)
                    offset = pl.multiple_of(code >> 16, 8)
                    c = table_ref[pl.ds(offset, 8), :]
                    less = table_ref[pl.ds(offset + 8, 8), :]
                    more = table_ref[pl.ds(offset + 16, 8), :]
                    for pol in range(2):
                        at = member * 6 + pol * 3
                        a = field_ref[pl.ds(source + pol * 16, 8), :]
                        b = field_ref[pl.ds(source + (pol * 16 + 8), 8), :]
                        sums[at] = sums[at] + c * (a + b)
                        sums[at + 1] = sums[at + 1] + a * less
                        sums[at + 2] = sums[at + 2] + b * more
            return tuple(sums)

        zero = jnp.zeros((8, 128), WHOLE)
        longest = jnp.maximum(counts_ref[pair * PAIR], counts_ref[pair * PAIR + 1])
        steps = lax.shift_right_logical(longest + (GROUP - 1), 3)
        sums = lax.fori_loop(0, steps, some_slots, (zero,) * (6 * PAIR))
        for member in range(PAIR):
            for pol in range(2):
                both, less, more = sums[member * 6 + pol * 3 : member * 6 + pol * 3 + 3]
                at = pl.multiple_of(pair * 64 + member * 32 + pol * 16, 8)
                out_ref[pl.ds(at, 8), :] = both - more
                out_ref[pl.ds(at + 8, 8), :] = both + less
        return carry

    lax.fori_loop(0, parents // PAIR, one_pair, 0)


def in_vmem(value):
    return pltpu.with_memory_space_constraint(value, pltpu.VMEM)


def in_smem(value):
    return pltpu.with_memory_space_constraint(value, pltpu.SMEM)


def in_hbm(value):
    return pltpu.with_memory_space_constraint(value, pltpu.HBM)


def call(kernel, outs, scratch, *operands, raw=0, out_specs=None):
    vmem = pl.BlockSpec(memory_space=pltpu.VMEM)
    hbm = pl.BlockSpec(memory_space=pltpu.HBM)
    return pl.pallas_call(
        kernel,
        out_shape=outs,
        in_specs=[hbm] * raw + [vmem] * (len(operands) - raw),
        out_specs=out_specs if out_specs is not None else jax.tree.map(lambda _: vmem, outs),
        scratch_shapes=scratch,
        compiler_params=pltpu.CompilerParams(vmem_limit_bytes=GRANT),
    )(*map(in_hbm, operands[:raw]), *map(in_vmem, operands[raw:]))


def operator_rows(translators):
    kinds, _, rows, samples = translators.shape
    table = translators.reshape(kinds, 2, rows, samples // 128, 128).transpose(0, 1, 3, 2, 4)
    return table.reshape(kinds * 16, 128)


def translate(field, codes, counts, operators):
    smem = pl.BlockSpec(memory_space=pltpu.SMEM)
    vmem = pl.BlockSpec(memory_space=pltpu.VMEM)
    field = field.reshape(-1, 128)
    return pl.pallas_call(
        translate_kernel,
        out_shape=jax.ShapeDtypeStruct(field.shape, WHOLE),
        in_specs=[smem, smem, vmem, vmem],
        out_specs=vmem,
        scratch_shapes=[pltpu.VMEM((operators.shape[0] * 3 // 2 + 24, 128), WHOLE)],
        compiler_params=pltpu.CompilerParams(vmem_limit_bytes=GRANT),
        name="translate",
    )(in_smem(codes), in_smem(counts), in_vmem(field), in_vmem(operators))


def merge_kernel(own_ref, top_ref, bottom_ref, out_hbm, out_ref, sems):
    copies = []
    for i in range(4):
        chunk = slice(128 * i, 128 * i + 128)
        for side in range(2):
            lanes = slice(128 * side, 128 * side + 128)
            out_ref[side, chunk] = own_ref[side, chunk]
            for ref, first, count in ((top_ref, 0, 4), (bottom_ref, OWN - 3, 3)):
                for row in range(count):
                    rows = pl.ds(128 * i + first + row, 8, stride=OWN)
                    value = own_ref[side, rows, :] + ref[row, 8 * i : 8 * i + 8, lanes]
                    out_ref[side, rows, :] = value
            target = out_hbm.at[chunk, lanes]
            copy = pltpu.make_async_copy(out_ref.at[side, chunk], target, sems.at[2 * i + side])
            copy.start()
            copies.append(copy)
    for copy in copies:
        copy.wait()


def on_device(
    children, theta_band, phi_interp, child_shift, translators, far_source, far_offset, far_count
):
    half = lambda *shape: pltpu.VMEM(shape, HALF)
    whole = lambda *shape: pltpu.VMEM(shape, WHOLE)
    hbm = pl.BlockSpec(memory_space=pl.ANY)
    vmem = pl.BlockSpec(memory_space=pltpu.VMEM)
    smem = pl.BlockSpec(memory_space=pltpu.SMEM)
    dma = pltpu.SemaphoreType.DMA
    planes, taps, phi, upper, lower = call(
        cut_kernel,
        (
            whole(2, PLANES * OWN, 128), whole(8, ROWS), whole(*phi_interp.shape),
            whole(4, PLANES, PHI), whole(3, PLANES, PHI),
        ),
        [dma((10,))], children.reshape(-1, PHI), theta_band.T, phi_interp, raw=3,
    )
    above = shifted_ring(lower, "theta", 1)
    below = shifted_ring(upper, "theta", -1)
    tables = (half(256, 512),) * 2 + (half(256, 256),) + (half(128, 256),) * 2
    packed, *tables, codes, counts = call(
        functools.partial(own_forward_kernel, kinds=translators.shape[0]),
        (whole(16, 2, 4, 8, 128),) + tables + (half(64, 256),) * 2
        + (pltpu.VMEM(far_source.shape, jnp.int32), pltpu.SMEM(far_count.shape, jnp.int32)),
        [
            whole(1024, SAMPLES), pltpu.VMEM(far_source.shape, jnp.int32),
            pltpu.VMEM(far_source.shape, jnp.int32), dma((3,)),
        ],
        far_source, far_offset, far_count, phi, taps, planes, child_shift,
        raw=3, out_specs=(vmem,) * 9 + (smem,),
    )
    *phi, edge, back_high, back_low, up_table, down_table = tables
    operators = in_vmem(operator_rows(translators))
    packed, codes = call(
        edge_forward_kernel,
        (whole(16, 2, 4, 8, 128), pltpu.SMEM((codes.size,), jnp.int32)),
        [whole(2, 256, 128), whole(512, SAMPLES), dma],
        codes.reshape(-1), above, below, *phi, edge, child_shift, packed, out_specs=(vmem, smem),
    )
    packed, operators = lax.optimization_barrier((packed, operators))
    field = lax.all_to_all(packed, "clus", 0, 0)
    summed = translate(field, codes, counts, operators)
    local = lax.all_to_all(summed.reshape(packed.shape), "clus", 0, 0)
    scratch = [half(256, SAMPLES)] * 2 + [whole(128, SAMPLES), whole(2, 128, 128)]
    down = call(
        edge_back_kernel(12, 0), whole(4, PLANES, PHI), scratch,
        local, child_shift, *phi, down_table,
    )
    from_below = shifted_ring(down, "theta", 1)
    up = call(
        edge_back_kernel(0, 1), whole(3, PLANES, PHI), scratch,
        local, child_shift, *phi, up_table,
    )
    from_above = shifted_ring(up, "theta", -1)
    own = call(
        own_back_kernel, whole(2, PLANES * OWN, 128), [half(1024, SAMPLES)] * 2,
        local, child_shift, *phi, back_high, back_low,
    )
    result = call(
        merge_kernel, jax.ShapeDtypeStruct((PLANES * OWN, PHI), WHOLE),
        [whole(2, PLANES * OWN, 128), dma((8,))], own, from_below, from_above, out_specs=hbm,
    )
    return result.reshape(children.shape)


def solution(mesh):
    return jax.shard_map(
        on_device,
        mesh=mesh,
        in_specs=(
            P("clus", None, None, "theta", None),
            P("theta", None),
            P(),
            P(None, None, "theta", None),
            P(None, None, ("theta", "clus"), None),
            P(),
            P(),
            P(),
        ),
        out_specs=P("clus", None, None, "theta", None),
        check_vma=False,
    )
```

```python
import functools

import jax
import jax.numpy as jnp
from jax import lax
from jax.experimental import pallas as pl
from jax.experimental.pallas import tpu as pltpu
from jax.sharding import PartitionSpec as P


KIDS = 4
LIST = 32
GROUP = 8
PAIR = 2
PLANES = 32
ROWS = 32
OWN = 16
PHI = 256
SAMPLES = 512
GRANT = 12 * 2**20
HALF = jnp.bfloat16
WHOLE = jnp.float32


def shifted_ring(value, axis, step):
    count = lax.axis_size(axis)
    return lax.ppermute(value, axis, [(i, (i + step) % count) for i in range(count)])


def halves(value):
    high = value.astype(HALF)
    return high, (value - high.astype(WHOLE)).astype(HALF)


def dot3(left, right, contract=0):
    dims = (((1,), (contract,)), ((), ()))
    total = None
    for a, b in ((0, 0), (0, 1), (1, 0)):
        part = lax.dot_general(left[a], right[b], dims, preferred_element_type=WHOLE)
        total = part if total is None else total + part
    return total


def swap_blocks(tiles):
    sub = lax.broadcasted_iota(jnp.int32, (8, 128), 0)
    even = (sub // 2) % 2 == 0
    low = sub < 4
    a, b, c, d = tiles

    def step(first, second, shift, mask):
        one = jnp.where(mask, first, pltpu.roll(second, shift, 0))
        two = jnp.where(mask, pltpu.roll(first, 8 - shift, 0), second)
        return one, two

    a, b = step(a, b, 2, even)
    c, d = step(c, d, 2, even)
    a, c = step(a, c, 4, low)
    b, d = step(b, d, 4, low)
    return a, b, c, d


def lane_blocks(value):
    return [value[:, 128 * i : 128 * (i + 1)] for i in range(4)]


def table_times(table, value):
    wide = jnp.dot(table, jnp.concatenate([value[0], value[0]], axis=0), preferred_element_type=WHOLE)
    depth = table.shape[1] // 2
    return wide + jnp.dot(table[:, :depth], value[1], preferred_element_type=WHOLE)


def same(child, parent):
    return child, parent


def above_rows(child, parent):
    return child - 4, parent


def below_rows(child, parent):
    return child + OWN, parent + ROWS - 8


def side_table(bands, place):
    row = lax.broadcasted_iota(jnp.int32, (8, 256), 0)
    column = lax.broadcasted_iota(jnp.int32, (8, 256), 1)
    tap = tap_of(column % 4, row, place)
    part = column // 64
    high, low = (value.astype(WHOLE) for value in halves(bands))
    block = jnp.zeros((8, 256), WHOLE)
    for t in range(8):
        value = jnp.where(part == 1, low[:, t : t + 1], high[:, t : t + 1])
        block = jnp.where(jnp.logical_and(tap == t, part < 3), value, block)
    owner = (column % 64) // 4
    blocks = [jnp.where(owner == plane, block, 0.0) for plane in range(16)]
    return jnp.concatenate(blocks, axis=0).astype(HALF)


def tap_of(child, parent, place):
    child, parent = place(child, parent)
    return child - parent // 2 + 3


def forward_table(bands, planes, inner, place):
    outer = bands.shape[0]
    width = planes * inner
    row = lax.broadcasted_iota(jnp.int32, (outer, width), 0)
    column = lax.broadcasted_iota(jnp.int32, (outer, width), 1)
    tap = tap_of(column % inner, row, place)
    block = jnp.zeros((outer, width), WHOLE)
    for t in range(8):
        block = jnp.where(tap == t, jnp.broadcast_to(bands[:, t : t + 1], block.shape), block)
    owner = column // inner
    blocks = [jnp.where(owner == plane, block, 0.0) for plane in range(planes)]
    return jnp.concatenate(blocks, axis=0)


def backward_table(bands, planes, inner, place):
    outer = bands.shape[1]
    width = planes * outer
    high = max(inner, 8)
    pick = lax.broadcasted_iota(jnp.int32, (outer, width), 1) % outer
    pick = (lax.broadcasted_iota(jnp.int32, (outer, width), 0) == pick).astype(HALF)
    row = lax.broadcasted_iota(jnp.int32, (high, width), 0)
    column = lax.broadcasted_iota(jnp.int32, (high, width), 1)
    tap = tap_of(row % inner, column % outer, place)
    tables = []
    for part in halves(bands):
        tiled = jnp.dot(part, pick, preferred_element_type=WHOLE)
        block = jnp.zeros((high, width), WHOLE)
        for t in range(8):
            block = jnp.where(tap == t, jnp.broadcast_to(tiled[t : t + 1], block.shape), block)
        owner = column // outer - row // inner
        step = high // inner
        blocks = [jnp.where(owner == plane, block, 0.0) for plane in range(0, planes, step)]
        tables.append(jnp.concatenate(blocks, axis=0).astype(HALF))
    return tables


def cut_kernel(
    children_hbm, taps_hbm, phi_hbm, children_ref, taps_ref, phi_ref, upper_ref, lower_ref, sems
):
    chunks = [slice(128 * i, 128 * i + 128) for i in range(4)]
    copies = [
        pltpu.make_async_copy(
            children_hbm.at[chunk, 128 * side : 128 * side + 128],
            children_ref.at[side, chunk],
            sems.at[2 * i + side],
        )
        for i, chunk in enumerate(chunks)
        for side in range(2)
    ]
    for copy in copies:
        copy.start()
    taps = pltpu.make_async_copy(taps_hbm, taps_ref, sems.at[8])
    taps.start()
    phi = pltpu.make_async_copy(phi_hbm, phi_ref, sems.at[9])
    phi.start()
    for at, copy in enumerate(copies):
        copy.wait()
        i, side = divmod(at, 2)
        for ref, first, count in ((upper_ref, 0, 4), (lower_ref, OWN - 3, 3)):
            for row in range(count):
                rows = pl.ds(128 * i + first + row, 8, stride=OWN)
                value = children_ref[side, rows, :]
                ref[row, 8 * i : 8 * i + 8, 128 * side : 128 * side + 128] = value
    taps.wait()
    phi.wait()


def both_sides(ref, first, count):
    return jnp.concatenate([ref[side, first : first + count] for side in range(2)], axis=1)


def own_forward_kernel(
    source_hbm, offset_hbm, counts_hbm, phi_ref, taps_ref, children_ref, shift_ref,
    packed_ref, phi_high_ref, phi_low_ref, above_ref, below_ref, back_high_ref, back_low_ref,
    up_ref, down_ref, codes_ref, counts_ref,
    fine_ref, source_ref, offset_ref, sems, *, kinds,
):
    pairs = ((source_hbm, source_ref), (offset_hbm, offset_ref), (counts_hbm, counts_ref))
    copies = [pltpu.make_async_copy(*pair, sems.at[i]) for i, pair in enumerate(pairs)]
    for copy in copies:
        copy.start()
    strip = lax.axis_index("theta")
    first = (strip > 0).astype(WHOLE)
    last = (strip < lax.axis_size("theta") - 1).astype(WHOLE)
    taps = taps_ref[...]
    bands = jnp.concatenate([taps] * 16, axis=0).T[:, :8]
    own = jnp.concatenate(halves(forward_table(bands, 8, 16, same)), axis=1)
    phi = halves(phi_ref[...])
    phi_high_ref[...], phi_low_ref[...] = phi

    def spread(group):
        mixed = dot3(halves(both_sides(children_ref, 128 * group, 128)), phi)
        fine_ref[256 * group : 256 * (group + 1)] = table_times(own, halves(mixed))

    def collect(parent):
        for pol in range(2):
            for block in range(4):
                rows = slice(8 * block, 8 * (block + 1))
                real, imag = gathered(fine_ref, shift_ref, parent, pol, 32, 8 * block, rows)
                for part, value in enumerate((real, imag)):
                    for pair, tile in enumerate(swap_blocks(lane_blocks(value))):
                        packed_ref[4 * block + pair, parent, 2 * pol + part] = tile

    for group in range(4):
        spread(group)
        if group == 2:
            collect(0)
    above_ref[...] = side_table(bands[:8] * first, above_rows)
    below_ref[...] = side_table(bands[ROWS - 8 :] * last, below_rows)
    back_high_ref[...], back_low_ref[...] = backward_table(taps, 8, 16, same)
    upper, lower = taps[:, :8] * first, taps[:, ROWS - 8 :] * last
    table = backward_table(upper, 16, 4, above_rows)
    up_ref[...] = jnp.concatenate(table, axis=1)
    table = backward_table(lower, 16, 4, below_rows)
    down_ref[...] = jnp.concatenate(table, axis=1)
    for copy in copies:
        copy.wait()
    lane = lax.broadcasted_iota(jnp.int32, (1, LIST), 1)
    for parent in range(source_ref.shape[0]):
        live = lane < counts_ref[parent]
        offset = jnp.where(live, offset_ref[parent : parent + 1], kinds)
        codes_ref[parent : parent + 1] = source_ref[parent : parent + 1] * 32 + offset * (24 * 65536)
    collect(1)


def gathered(fine_ref, shift_ref, parent, pol, per_plane, first, rows):
    real = imag = None
    for kid in range(KIDS):
        at = ((parent * KIDS + kid) * 4 + pol * 2) * per_plane + first
        a = fine_ref[at : at + 8]
        b = fine_ref[at + per_plane : at + per_plane + 8]
        c = shift_ref[kid, 0, rows]
        d = shift_ref[kid, 1, rows]
        one, two = c * a - d * b, c * b + d * a
        real = one if real is None else real + one
        imag = two if imag is None else imag + two
    return real, imag


def edge_forward_kernel(side):
    first, count = 12 * side, 3 + side

    def kernel(*refs):
        if side == 0:
            codes_src, halo_in, phi_high_ref, phi_low_ref, table_ref, shift_ref = refs[:6]
            _, out_ref, codes_ref, halo_ref, fine_ref, sem = refs[6:]
            codes = pltpu.make_async_copy(codes_src, codes_ref, sem)
            codes.start()
        else:
            halo_in, phi_high_ref, phi_low_ref, table_ref, shift_ref = refs[:5]
            _, out_ref, halo_ref, fine_ref = refs[5:]
        for half in range(2):
            lanes = slice(128 * half, 128 * half + 128)
            if side == 0:
                halo_ref[half, pl.ds(0, PLANES, stride=4), :] = jnp.zeros((PLANES, 128), WHOLE)
            for row in range(count):
                rows = pl.ds(row + 4 - count, PLANES, stride=4)
                halo_ref[half, rows, :] = halo_in[row, :, lanes]
        phi = (phi_high_ref[...], phi_low_ref[...])
        high, low = halves(dot3(halves(both_sides(halo_ref, 0, 128)), phi))
        table = table_ref[...]
        for parent in range(2):
            rows = slice(64 * parent, 64 * parent + 64)
            value = jnp.concatenate([high[rows], high[rows], low[rows], high[rows]], axis=0)
            fine = jnp.dot(table, value, preferred_element_type=WHOLE)
            fine_ref[128 * parent : 128 * parent + 128] = fine
        rows = slice(24 * side, 24 * side + 8)
        for parent in range(2):
            for pol in range(2):
                real, imag = gathered(fine_ref, shift_ref, parent, pol, 8, 0, rows)
                for part, value in enumerate((real, imag)):
                    for pair, tile in enumerate(swap_blocks(lane_blocks(value))):
                        at = (first + pair, parent, 2 * pol + part)
                        out_ref[at] = out_ref[at] + tile
        if side == 0:
            codes.wait()

    return kernel


def spread_back(local_ref, shift_ref, parent, pol, blocks, high_ref, low_ref):
    parts = []
    for part in range(2):
        pieces = []
        for first in blocks:
            tiles = [local_ref[first + pair, parent, 2 * pol + part] for pair in range(4)]
            pieces.append(jnp.concatenate(swap_blocks(tiles), axis=1))
        parts.append(pieces)
    for kid in range(KIDS):
        real, imag = [], []
        for index, first in enumerate(blocks):
            a, b = parts[0][index], parts[1][index]
            c = shift_ref[kid, 0, 2 * first : 2 * first + 8]
            d = shift_ref[kid, 1, 2 * first : 2 * first + 8]
            real.append(c * a + d * b)
            imag.append(c * b - d * a)
        height = 16 * len(blocks)
        at = ((parent * KIDS + kid) * 2 + pol) * height
        value = halves(jnp.concatenate(real + imag, axis=0))
        high_ref[at : at + height], low_ref[at : at + height] = value


def edge_back_kernel(first, skipped):
    def kernel(
        local_ref, shift_ref, phi_high_ref, phi_low_ref, table_ref,
        out_ref, high_ref, low_ref, narrow_ref, result_ref,
    ):
        phi = (phi_high_ref[...], phi_low_ref[...])
        table = table_ref[...]
        for parent in range(2):
            for pol in range(2):
                spread_back(local_ref, shift_ref, parent, pol, (first,), high_ref, low_ref)
            rows = slice(128 * parent, 128 * (parent + 1))
            narrow = table_times(table, (high_ref[rows], low_ref[rows]))
            narrow_ref[64 * parent : 64 * (parent + 1)] = narrow
        result = dot3(halves(narrow_ref[...]), phi, contract=1)
        for side in range(2):
            lanes = slice(128 * side, 128 * side + 128)
            result_ref[side] = result[:, lanes]
            for row in range(4 - skipped):
                rows = pl.ds(row + skipped, PLANES, stride=4)
                out_ref[row, :, lanes] = result_ref[side, rows, :]

    return kernel


def own_back_kernel(
    local_ref, shift_ref, phi_high_ref, phi_low_ref, table_high_ref, table_low_ref,
    own_ref, high_ref, low_ref,
):
    phi = (phi_high_ref[...], phi_low_ref[...])
    table = (table_high_ref[...], table_low_ref[...])

    for parent in range(2):
        for pol in range(2):
            spread_back(local_ref, shift_ref, parent, pol, (0, 4, 8, 12), high_ref, low_ref)
        for group in (2 * parent, 2 * parent + 1):
            rows = slice(256 * group, 256 * (group + 1))
            narrowed = dot3(table, (high_ref[rows], low_ref[rows]))
            result = dot3(halves(narrowed), phi, contract=1)
            for side in range(2):
                lanes = slice(128 * side, 128 * side + 128)
                own_ref[side, 128 * group : 128 * (group + 1)] = result[:, lanes]


def translate_kernel(codes_ref, counts_ref, field_ref, operator_ref, out_ref, table_ref, sum_ref):
    parents = counts_ref.shape[0]
    kinds = operator_ref.shape[0] // 16
    for kind in range(kinds):
        c = operator_ref[16 * kind : 16 * kind + 8]
        d = operator_ref[16 * kind + 8 : 16 * kind + 16]
        for at, value in enumerate((c, d - c, c + d)):
            table_ref[24 * kind + 8 * at : 24 * kind + 8 * at + 8] = value
    table_ref[24 * kinds : 24 * kinds + 24] = jnp.zeros((24, 128), WHOLE)
    for at in range(2 * parents):
        rows = slice(16 * at, 16 * at + 8)
        sum_ref[8 * at : 8 * at + 8] = field_ref[rows] + field_ref[16 * at + 8 : 16 * at + 16]

    def one_pair(pair, carry):
        def some_slots(step, sums):
            sums = list(sums)
            for member in range(PAIR):
                for lane in range(GROUP):
                    slot = pair * (PAIR * LIST) + step * GROUP + (member * LIST + lane)
                    code = codes_ref[slot]
                    source = pl.multiple_of(code & 0xFFFF, 8)
                    offset = pl.multiple_of(code >> 16, 8)
                    half = pl.multiple_of((code & 0xFFFF) >> 1, 8)
                    c = table_ref[pl.ds(offset, 8), :]
                    less = table_ref[pl.ds(offset + 8, 8), :]
                    more = table_ref[pl.ds(offset + 16, 8), :]
                    for pol in range(2):
                        at = member * 6 + pol * 3
                        a = field_ref[pl.ds(source + pol * 16, 8), :]
                        b = field_ref[pl.ds(source + (pol * 16 + 8), 8), :]
                        sums[at] = sums[at] + c * sum_ref[pl.ds(half + pol * 8, 8), :]
                        sums[at + 1] = sums[at + 1] + a * less
                        sums[at + 2] = sums[at + 2] + b * more
            return tuple(sums)

        zero = jnp.zeros((8, 128), WHOLE)
        longest = jnp.maximum(counts_ref[pair * PAIR], counts_ref[pair * PAIR + 1])
        steps = lax.shift_right_logical(longest + (GROUP - 1), 3)
        sums = lax.fori_loop(0, steps, some_slots, (zero,) * (6 * PAIR))
        for member in range(PAIR):
            for pol in range(2):
                both, less, more = sums[member * 6 + pol * 3 : member * 6 + pol * 3 + 3]
                at = pl.multiple_of(pair * 64 + member * 32 + pol * 16, 8)
                out_ref[pl.ds(at, 8), :] = both - more
                out_ref[pl.ds(at + 8, 8), :] = both + less
        return carry

    lax.fori_loop(0, parents // PAIR, one_pair, 0)


def in_vmem(value):
    return pltpu.with_memory_space_constraint(value, pltpu.VMEM)


def in_smem(value):
    return pltpu.with_memory_space_constraint(value, pltpu.SMEM)


def in_hbm(value):
    return pltpu.with_memory_space_constraint(value, pltpu.HBM)


def call(kernel, outs, scratch, *operands, raw=0, out_specs=None, aliases={}):
    vmem = pl.BlockSpec(memory_space=pltpu.VMEM)
    hbm = pl.BlockSpec(memory_space=pltpu.HBM)
    return pl.pallas_call(
        kernel,
        out_shape=outs,
        in_specs=[hbm] * raw + [vmem] * (len(operands) - raw),
        out_specs=out_specs if out_specs is not None else jax.tree.map(lambda _: vmem, outs),
        scratch_shapes=scratch,
        input_output_aliases=aliases,
        compiler_params=pltpu.CompilerParams(vmem_limit_bytes=GRANT),
    )(*map(in_hbm, operands[:raw]), *map(in_vmem, operands[raw:]))


def operator_rows(translators):
    kinds, _, rows, samples = translators.shape
    table = translators.reshape(kinds, 2, rows, samples // 128, 128).transpose(0, 1, 3, 2, 4)
    return table.reshape(kinds * 16, 128)


def translate(field, codes, counts, operators):
    smem = pl.BlockSpec(memory_space=pltpu.SMEM)
    vmem = pl.BlockSpec(memory_space=pltpu.VMEM)
    field = field.reshape(-1, 128)
    return pl.pallas_call(
        translate_kernel,
        out_shape=jax.ShapeDtypeStruct(field.shape, WHOLE),
        in_specs=[smem, smem, vmem, vmem],
        out_specs=vmem,
        scratch_shapes=[
            pltpu.VMEM((operators.shape[0] * 3 // 2 + 24, 128), WHOLE),
            pltpu.VMEM((field.shape[0] // 2, 128), WHOLE),
        ],
        compiler_params=pltpu.CompilerParams(vmem_limit_bytes=GRANT),
        name="translate",
    )(in_smem(codes), in_smem(counts), in_vmem(field), in_vmem(operators))


def merge_kernel(own_ref, top_ref, bottom_ref, out_hbm, out_ref, sems):
    copies = []
    for i in range(4):
        chunk = slice(128 * i, 128 * i + 128)
        for side in range(2):
            lanes = slice(128 * side, 128 * side + 128)
            out_ref[side, chunk] = own_ref[side, chunk]
            for ref, first, count in ((top_ref, 0, 4), (bottom_ref, OWN - 3, 3)):
                for row in range(count):
                    rows = pl.ds(128 * i + first + row, 8, stride=OWN)
                    value = own_ref[side, rows, :] + ref[row, 8 * i : 8 * i + 8, lanes]
                    out_ref[side, rows, :] = value
            target = out_hbm.at[chunk, lanes]
            copy = pltpu.make_async_copy(out_ref.at[side, chunk], target, sems.at[2 * i + side])
            copy.start()
            copies.append(copy)
    for copy in copies:
        copy.wait()


def on_device(
    children, theta_band, phi_interp, child_shift, translators, far_source, far_offset, far_count
):
    half = lambda *shape: pltpu.VMEM(shape, HALF)
    whole = lambda *shape: pltpu.VMEM(shape, WHOLE)
    hbm = pl.BlockSpec(memory_space=pl.ANY)
    vmem = pl.BlockSpec(memory_space=pltpu.VMEM)
    smem = pl.BlockSpec(memory_space=pltpu.SMEM)
    dma = pltpu.SemaphoreType.DMA
    planes, taps, phi, upper, lower = call(
        cut_kernel,
        (
            whole(2, PLANES * OWN, 128), whole(8, ROWS), whole(*phi_interp.shape),
            whole(4, PLANES, PHI), whole(3, PLANES, PHI),
        ),
        [dma((10,))], children.reshape(-1, PHI), theta_band.T, phi_interp, raw=3,
    )
    above = shifted_ring(lower, "theta", 1)
    below = shifted_ring(upper, "theta", -1)
    tables = (half(256, 512),) * 2 + (half(128, 256),) * 4
    packed, *tables, codes, counts = call(
        functools.partial(own_forward_kernel, kinds=translators.shape[0]),
        (whole(16, 2, 4, 8, 128),) + tables + (half(64, 256),) * 2
        + (pltpu.VMEM(far_source.shape, jnp.int32), pltpu.SMEM(far_count.shape, jnp.int32)),
        [
            whole(1024, SAMPLES), pltpu.VMEM(far_source.shape, jnp.int32),
            pltpu.VMEM(far_source.shape, jnp.int32), dma((3,)),
        ],
        far_source, far_offset, far_count, phi, taps, planes, child_shift,
        raw=3, out_specs=(vmem,) * 10 + (smem,),
    )
    *phi, above_table, below_table, back_high, back_low, up_table, down_table = tables
    operators = in_vmem(operator_rows(translators))
    scratch = [whole(2, 128, 128), whole(256, SAMPLES)]
    packed, codes = call(
        edge_forward_kernel(0),
        (whole(16, 2, 4, 8, 128), pltpu.SMEM((codes.size,), jnp.int32)), scratch + [dma],
        codes.reshape(-1), above, *phi, above_table, child_shift, packed,
        out_specs=(vmem, smem), aliases={6: 0},
    )
    packed = call(
        edge_forward_kernel(1), whole(16, 2, 4, 8, 128), scratch,
        below, *phi, below_table, child_shift, packed, aliases={5: 0},
    )
    packed, operators = lax.optimization_barrier((packed, operators))
    field = lax.all_to_all(packed, "clus", 0, 0)
    summed = translate(field, codes, counts, operators)
    local = lax.all_to_all(summed.reshape(packed.shape), "clus", 0, 0)
    scratch = [half(256, SAMPLES)] * 2 + [whole(128, SAMPLES), whole(2, 128, 128)]
    down = call(
        edge_back_kernel(12, 0), whole(4, PLANES, PHI), scratch,
        local, child_shift, *phi, down_table,
    )
    from_below = shifted_ring(down, "theta", 1)
    up = call(
        edge_back_kernel(0, 1), whole(3, PLANES, PHI), scratch,
        local, child_shift, *phi, up_table,
    )
    from_above = shifted_ring(up, "theta", -1)
    own = call(
        own_back_kernel, whole(2, PLANES * OWN, 128), [half(1024, SAMPLES)] * 2,
        local, child_shift, *phi, back_high, back_low,
    )
    result = call(
        merge_kernel, jax.ShapeDtypeStruct((PLANES * OWN, PHI), WHOLE),
        [whole(2, PLANES * OWN, 128), dma((8,))], own, from_below, from_above, out_specs=hbm,
    )
    return result.reshape(children.shape)


def solution(mesh):
    return jax.shard_map(
        on_device,
        mesh=mesh,
        in_specs=(
            P("clus", None, None, "theta", None),
            P("theta", None),
            P(),
            P(None, None, "theta", None),
            P(None, None, ("theta", "clus"), None),
            P(),
            P(),
            P(),
        ),
        out_specs=P("clus", None, None, "theta", None),
        check_vma=False,
    )
```

```python
import functools

import jax
import jax.numpy as jnp
from jax import lax
from jax.experimental import pallas as pl
from jax.experimental.pallas import tpu as pltpu
from jax.sharding import PartitionSpec as P


KIDS = 4
LIST = 32
GROUP = 8
PAIR = 2
PLANES = 32
ROWS = 32
OWN = 16
PHI = 256
SAMPLES = 512
GRANT = 12 * 2**20
HALF = jnp.bfloat16
WHOLE = jnp.float32


def shifted_ring(value, axis, step):
    count = lax.axis_size(axis)
    return lax.ppermute(value, axis, [(i, (i + step) % count) for i in range(count)])


def halves(value):
    high = value.astype(HALF)
    return high, (value - high.astype(WHOLE)).astype(HALF)


def dot3(left, right, contract=0):
    dims = (((1,), (contract,)), ((), ()))
    total = None
    for a, b in ((0, 0), (0, 1), (1, 0)):
        part = lax.dot_general(left[a], right[b], dims, preferred_element_type=WHOLE)
        total = part if total is None else total + part
    return total


def swap_blocks(tiles):
    sub = lax.broadcasted_iota(jnp.int32, (8, 128), 0)
    even = (sub // 2) % 2 == 0
    low = sub < 4
    a, b, c, d = tiles

    def step(first, second, shift, mask):
        one = jnp.where(mask, first, pltpu.roll(second, shift, 0))
        two = jnp.where(mask, pltpu.roll(first, 8 - shift, 0), second)
        return one, two

    a, b = step(a, b, 2, even)
    c, d = step(c, d, 2, even)
    a, c = step(a, c, 4, low)
    b, d = step(b, d, 4, low)
    return a, b, c, d


def lane_blocks(value):
    return [value[:, 128 * i : 128 * (i + 1)] for i in range(4)]


def table_times(table, value):
    wide = jnp.dot(table, jnp.concatenate([value[0], value[0]], axis=0), preferred_element_type=WHOLE)
    depth = table.shape[1] // 2
    return wide + jnp.dot(table[:, :depth], value[1], preferred_element_type=WHOLE)


def same(child, parent):
    return child, parent


def above_rows(child, parent):
    return child - 4, parent


def below_rows(child, parent):
    return child + OWN, parent + ROWS - 8


def side_table(bands, place):
    row = lax.broadcasted_iota(jnp.int32, (8, 256), 0)
    column = lax.broadcasted_iota(jnp.int32, (8, 256), 1)
    tap = tap_of(column % 4, row, place)
    part = column // 64
    high, low = (value.astype(WHOLE) for value in halves(bands))
    block = jnp.zeros((8, 256), WHOLE)
    for t in range(8):
        value = jnp.where(part == 1, low[:, t : t + 1], high[:, t : t + 1])
        block = jnp.where(jnp.logical_and(tap == t, part < 3), value, block)
    owner = (column % 64) // 4
    blocks = [jnp.where(owner == plane, block, 0.0) for plane in range(16)]
    return jnp.concatenate(blocks, axis=0).astype(HALF)


def tap_of(child, parent, place):
    child, parent = place(child, parent)
    return child - parent // 2 + 3


def forward_table(bands, planes, inner, place):
    outer = bands.shape[0]
    width = planes * inner
    row = lax.broadcasted_iota(jnp.int32, (outer, width), 0)
    column = lax.broadcasted_iota(jnp.int32, (outer, width), 1)
    tap = tap_of(column % inner, row, place)
    block = jnp.zeros((outer, width), WHOLE)
    for t in range(8):
        block = jnp.where(tap == t, jnp.broadcast_to(bands[:, t : t + 1], block.shape), block)
    owner = column // inner
    blocks = [jnp.where(owner == plane, block, 0.0) for plane in range(planes)]
    return jnp.concatenate(blocks, axis=0)


def backward_table(bands, planes, inner, place):
    outer = bands.shape[1]
    width = planes * outer
    high = max(inner, 8)
    pick = lax.broadcasted_iota(jnp.int32, (outer, width), 1) % outer
    pick = (lax.broadcasted_iota(jnp.int32, (outer, width), 0) == pick).astype(HALF)
    row = lax.broadcasted_iota(jnp.int32, (high, width), 0)
    column = lax.broadcasted_iota(jnp.int32, (high, width), 1)
    tap = tap_of(row % inner, column % outer, place)
    tables = []
    for part in halves(bands):
        tiled = jnp.dot(part, pick, preferred_element_type=WHOLE)
        block = jnp.zeros((high, width), WHOLE)
        for t in range(8):
            block = jnp.where(tap == t, jnp.broadcast_to(tiled[t : t + 1], block.shape), block)
        owner = column // outer - row // inner
        step = high // inner
        blocks = [jnp.where(owner == plane, block, 0.0) for plane in range(0, planes, step)]
        tables.append(jnp.concatenate(blocks, axis=0).astype(HALF))
    return tables


def cut_kernel(
    children_hbm, taps_hbm, children_ref, taps_ref, upper_ref, lower_ref, sems
):
    chunks = [slice(128 * i, 128 * i + 128) for i in range(4)]
    copies = [
        pltpu.make_async_copy(
            children_hbm.at[chunk, 128 * side : 128 * side + 128],
            children_ref.at[side, chunk],
            sems.at[2 * i + side],
        )
        for i, chunk in enumerate(chunks)
        for side in range(2)
    ]
    for copy in copies:
        copy.start()
    taps = pltpu.make_async_copy(taps_hbm, taps_ref, sems.at[8])
    taps.start()
    for at, copy in enumerate(copies):
        copy.wait()
        i, side = divmod(at, 2)
        for ref, first, count in ((upper_ref, 0, 4), (lower_ref, OWN - 3, 3)):
            for row in range(count):
                rows = pl.ds(128 * i + first + row, 8, stride=OWN)
                value = children_ref[side, rows, :]
                ref[row, 8 * i : 8 * i + 8, 128 * side : 128 * side + 128] = value
    taps.wait()


def both_sides(ref, first, count):
    return jnp.concatenate([ref[side, first : first + count] for side in range(2)], axis=1)


def own_forward_kernel(
    shift_hbm, source_hbm, offset_hbm, counts_hbm, phi_ref, taps_ref, children_ref,
    packed_ref, shift_ref, phi_high_ref, phi_low_ref, above_ref, below_ref, back_high_ref, back_low_ref,
    up_ref, down_ref, codes_ref, counts_ref,
    fine_ref, source_ref, offset_ref, sems, *, kinds,
):
    pairs = (
        (shift_hbm, shift_ref), (source_hbm, source_ref), (offset_hbm, offset_ref),
        (counts_hbm, counts_ref),
    )
    copies = [pltpu.make_async_copy(*pair, sems.at[i]) for i, pair in enumerate(pairs)]
    for copy in copies:
        copy.start()
    strip = lax.axis_index("theta")
    first = (strip > 0).astype(WHOLE)
    last = (strip < lax.axis_size("theta") - 1).astype(WHOLE)
    taps = taps_ref[...]
    bands = jnp.concatenate([taps] * 16, axis=0).T[:, :8]
    own = jnp.concatenate(halves(forward_table(bands, 8, 16, same)), axis=1)
    phi = halves(phi_ref[...])
    phi_high_ref[...], phi_low_ref[...] = phi

    def spread(group):
        mixed = dot3(halves(both_sides(children_ref, 128 * group, 128)), phi)
        fine_ref[256 * group : 256 * (group + 1)] = table_times(own, halves(mixed))

    def collect(parent):
        for pol in range(2):
            for block in range(4):
                rows = slice(8 * block, 8 * (block + 1))
                real, imag = gathered(fine_ref, shift_ref, parent, pol, 32, 8 * block, rows)
                for part, value in enumerate((real, imag)):
                    for pair, tile in enumerate(swap_blocks(lane_blocks(value))):
                        packed_ref[4 * block + pair, parent, 2 * pol + part] = tile

    spread(0)
    spread(1)
    for copy in copies:
        copy.wait()
    spread(2)
    collect(0)
    spread(3)
    above_ref[...] = side_table(bands[:8] * first, above_rows)
    below_ref[...] = side_table(bands[ROWS - 8 :] * last, below_rows)
    back_high_ref[...], back_low_ref[...] = backward_table(taps, 8, 16, same)
    upper, lower = taps[:, :8] * first, taps[:, ROWS - 8 :] * last
    table = backward_table(upper, 16, 4, above_rows)
    up_ref[...] = jnp.concatenate(table, axis=1)
    table = backward_table(lower, 16, 4, below_rows)
    down_ref[...] = jnp.concatenate(table, axis=1)
    lane = lax.broadcasted_iota(jnp.int32, (1, LIST), 1)
    for parent in range(source_ref.shape[0]):
        live = lane < counts_ref[parent]
        offset = jnp.where(live, offset_ref[parent : parent + 1], kinds)
        codes_ref[parent : parent + 1] = source_ref[parent : parent + 1] * 32 + offset * (24 * 65536)
    collect(1)


def gathered(fine_ref, shift_ref, parent, pol, per_plane, first, rows):
    real = imag = None
    for kid in range(KIDS):
        at = ((parent * KIDS + kid) * 4 + pol * 2) * per_plane + first
        a = fine_ref[at : at + 8]
        b = fine_ref[at + per_plane : at + per_plane + 8]
        c = shift_ref[kid, 0, rows]
        d = shift_ref[kid, 1, rows]
        one, two = c * a - d * b, c * b + d * a
        real = one if real is None else real + one
        imag = two if imag is None else imag + two
    return real, imag


def edge_forward_kernel(side):
    first, count = 12 * side, 3 + side

    def kernel(*refs):
        if side == 0:
            codes_src, halo_in, phi_high_ref, phi_low_ref, table_ref, shift_ref = refs[:6]
            _, out_ref, codes_ref, halo_ref, fine_ref, sem = refs[6:]
            codes = pltpu.make_async_copy(codes_src, codes_ref, sem)
            codes.start()
        else:
            halo_in, phi_high_ref, phi_low_ref, table_ref, shift_ref = refs[:5]
            _, out_ref, halo_ref, fine_ref = refs[5:]
        for half in range(2):
            lanes = slice(128 * half, 128 * half + 128)
            if side == 0:
                halo_ref[half, pl.ds(0, PLANES, stride=4), :] = jnp.zeros((PLANES, 128), WHOLE)
            for row in range(count):
                rows = pl.ds(row + 4 - count, PLANES, stride=4)
                halo_ref[half, rows, :] = halo_in[row, :, lanes]
        phi = (phi_high_ref[...], phi_low_ref[...])
        high, low = halves(dot3(halves(both_sides(halo_ref, 0, 128)), phi))
        table = table_ref[...]
        for parent in range(2):
            rows = slice(64 * parent, 64 * parent + 64)
            value = jnp.concatenate([high[rows], high[rows], low[rows], high[rows]], axis=0)
            fine = jnp.dot(table, value, preferred_element_type=WHOLE)
            fine_ref[128 * parent : 128 * parent + 128] = fine
        rows = slice(24 * side, 24 * side + 8)
        for parent in range(2):
            for pol in range(2):
                real, imag = gathered(fine_ref, shift_ref, parent, pol, 8, 0, rows)
                for part, value in enumerate((real, imag)):
                    for pair, tile in enumerate(swap_blocks(lane_blocks(value))):
                        at = (first + pair, parent, 2 * pol + part)
                        out_ref[at] = out_ref[at] + tile
        if side == 0:
            codes.wait()

    return kernel


def spread_back(local_ref, shift_ref, parent, pol, blocks):
    parts = []
    for part in range(2):
        pieces = []
        for first in blocks:
            tiles = [local_ref[first + pair, parent, 2 * pol + part] for pair in range(4)]
            pieces.append(jnp.concatenate(swap_blocks(tiles), axis=1))
        parts.append(pieces)
    for kid in range(KIDS):
        real, imag = [], []
        for index, first in enumerate(blocks):
            a, b = parts[0][index], parts[1][index]
            c = shift_ref[kid, 0, 2 * first : 2 * first + 8]
            d = shift_ref[kid, 1, 2 * first : 2 * first + 8]
            real.append(c * a + d * b)
            imag.append(c * b - d * a)
        yield kid, halves(jnp.concatenate(real + imag, axis=0))


def edge_back_kernel(first, skipped):
    def kernel(
        local_ref, shift_ref, phi_high_ref, phi_low_ref, table_ref, out_ref, result_ref,
    ):
        phi = (phi_high_ref[...], phi_low_ref[...])
        table = table_ref[...]
        narrow = []
        for parent in range(2):
            pieces = {}
            for pol in range(2):
                for kid, value in spread_back(local_ref, shift_ref, parent, pol, (first,)):
                    pieces[kid, pol] = value
            order = [(kid, pol) for kid in range(KIDS) for pol in range(2)]
            value = [jnp.concatenate([pieces[at][i] for at in order], axis=0) for i in range(2)]
            narrow.append(table_times(table, value))
        result = dot3(halves(jnp.concatenate(narrow, axis=0)), phi, contract=1)
        for side in range(2):
            lanes = slice(128 * side, 128 * side + 128)
            result_ref[side] = result[:, lanes]
            for row in range(4 - skipped):
                rows = pl.ds(row + skipped, PLANES, stride=4)
                out_ref[row, :, lanes] = result_ref[side, rows, :]

    return kernel


def own_back_kernel(
    local_ref, shift_ref, phi_high_ref, phi_low_ref, table_high_ref, table_low_ref,
    own_ref, high_ref, low_ref,
):
    phi = (phi_high_ref[...], phi_low_ref[...])
    table = (table_high_ref[...], table_low_ref[...])

    for parent in range(2):
        for pol in range(2):
            for kid, value in spread_back(local_ref, shift_ref, parent, pol, (0, 4, 8, 12)):
                at = ((parent * KIDS + kid) * 2 + pol) * 64
                high_ref[at : at + 64], low_ref[at : at + 64] = value
        for group in (2 * parent, 2 * parent + 1):
            rows = slice(256 * group, 256 * (group + 1))
            narrowed = dot3(table, (high_ref[rows], low_ref[rows]))
            result = dot3(halves(narrowed), phi, contract=1)
            for side in range(2):
                lanes = slice(128 * side, 128 * side + 128)
                own_ref[side, 128 * group : 128 * (group + 1)] = result[:, lanes]


def translate_kernel(codes_ref, counts_ref, field_ref, operator_ref, out_ref, table_ref, sum_ref):
    parents = counts_ref.shape[0]
    kinds = operator_ref.shape[0] // 16
    for kind in range(kinds):
        c = operator_ref[16 * kind : 16 * kind + 8]
        d = operator_ref[16 * kind + 8 : 16 * kind + 16]
        for at, value in enumerate((c, d - c, c + d)):
            table_ref[24 * kind + 8 * at : 24 * kind + 8 * at + 8] = value
    table_ref[24 * kinds : 24 * kinds + 24] = jnp.zeros((24, 128), WHOLE)
    for at in range(2 * parents):
        rows = slice(16 * at, 16 * at + 8)
        sum_ref[8 * at : 8 * at + 8] = field_ref[rows] + field_ref[16 * at + 8 : 16 * at + 16]

    def one_pair(pair, carry):
        def some_slots(step, sums):
            sums = list(sums)
            for member in range(PAIR):
                for lane in range(GROUP):
                    slot = pair * (PAIR * LIST) + step * GROUP + (member * LIST + lane)
                    code = codes_ref[slot]
                    source = pl.multiple_of(code & 0xFFFF, 8)
                    offset = pl.multiple_of(code >> 16, 8)
                    half = pl.multiple_of((code & 0xFFFF) >> 1, 8)
                    c = table_ref[pl.ds(offset, 8), :]
                    less = table_ref[pl.ds(offset + 8, 8), :]
                    more = table_ref[pl.ds(offset + 16, 8), :]
                    for pol in range(2):
                        at = member * 6 + pol * 3
                        a = field_ref[pl.ds(source + pol * 16, 8), :]
                        b = field_ref[pl.ds(source + (pol * 16 + 8), 8), :]
                        sums[at] = sums[at] + c * sum_ref[pl.ds(half + pol * 8, 8), :]
                        sums[at + 1] = sums[at + 1] + a * less
                        sums[at + 2] = sums[at + 2] + b * more
            return tuple(sums)

        zero = jnp.zeros((8, 128), WHOLE)
        longest = jnp.maximum(counts_ref[pair * PAIR], counts_ref[pair * PAIR + 1])
        steps = lax.shift_right_logical(longest + (GROUP - 1), 3)
        sums = lax.fori_loop(0, steps, some_slots, (zero,) * (6 * PAIR))
        for member in range(PAIR):
            for pol in range(2):
                both, less, more = sums[member * 6 + pol * 3 : member * 6 + pol * 3 + 3]
                at = pl.multiple_of(pair * 64 + member * 32 + pol * 16, 8)
                out_ref[pl.ds(at, 8), :] = both - more
                out_ref[pl.ds(at + 8, 8), :] = both + less
        return carry

    lax.fori_loop(0, parents // PAIR, one_pair, 0)


def in_vmem(value):
    return pltpu.with_memory_space_constraint(value, pltpu.VMEM)


def in_smem(value):
    return pltpu.with_memory_space_constraint(value, pltpu.SMEM)


def in_hbm(value):
    return pltpu.with_memory_space_constraint(value, pltpu.HBM)


def call(kernel, outs, scratch, *operands, raw=0, out_specs=None, aliases={}):
    vmem = pl.BlockSpec(memory_space=pltpu.VMEM)
    hbm = pl.BlockSpec(memory_space=pltpu.HBM)
    return pl.pallas_call(
        kernel,
        out_shape=outs,
        in_specs=[hbm] * raw + [vmem] * (len(operands) - raw),
        out_specs=out_specs if out_specs is not None else jax.tree.map(lambda _: vmem, outs),
        scratch_shapes=scratch,
        input_output_aliases=aliases,
        compiler_params=pltpu.CompilerParams(vmem_limit_bytes=GRANT),
    )(*map(in_hbm, operands[:raw]), *map(in_vmem, operands[raw:]))


def operator_rows(translators):
    kinds, _, rows, samples = translators.shape
    table = translators.reshape(kinds, 2, rows, samples // 128, 128).transpose(0, 1, 3, 2, 4)
    return table.reshape(kinds * 16, 128)


def translate(field, codes, counts, operators):
    smem = pl.BlockSpec(memory_space=pltpu.SMEM)
    vmem = pl.BlockSpec(memory_space=pltpu.VMEM)
    field = field.reshape(-1, 128)
    return pl.pallas_call(
        translate_kernel,
        out_shape=jax.ShapeDtypeStruct(field.shape, WHOLE),
        in_specs=[smem, smem, vmem, vmem],
        out_specs=vmem,
        scratch_shapes=[
            pltpu.VMEM((operators.shape[0] * 3 // 2 + 24, 128), WHOLE),
            pltpu.VMEM((field.shape[0] // 2, 128), WHOLE),
        ],
        compiler_params=pltpu.CompilerParams(vmem_limit_bytes=GRANT),
        name="translate",
    )(in_smem(codes), in_smem(counts), in_vmem(field), in_vmem(operators))


def merge_kernel(_, top_ref, bottom_ref, out_hbm, own_ref, sems):
    copies = []
    for i in range(4):
        chunk = slice(128 * i, 128 * i + 128)
        for side in range(2):
            lanes = slice(128 * side, 128 * side + 128)
            for ref, first, count in ((top_ref, 0, 4), (bottom_ref, OWN - 3, 3)):
                for row in range(count):
                    rows = pl.ds(128 * i + first + row, 8, stride=OWN)
                    value = own_ref[side, rows, :] + ref[row, 8 * i : 8 * i + 8, lanes]
                    own_ref[side, rows, :] = value
            target = out_hbm.at[chunk, lanes]
            copy = pltpu.make_async_copy(own_ref.at[side, chunk], target, sems.at[2 * i + side])
            copy.start()
            copies.append(copy)
    for copy in copies:
        copy.wait()


def on_device(
    children, theta_band, phi_interp, child_shift, translators, far_source, far_offset, far_count
):
    half = lambda *shape: pltpu.VMEM(shape, HALF)
    whole = lambda *shape: pltpu.VMEM(shape, WHOLE)
    hbm = pl.BlockSpec(memory_space=pl.ANY)
    vmem = pl.BlockSpec(memory_space=pltpu.VMEM)
    smem = pl.BlockSpec(memory_space=pltpu.SMEM)
    dma = pltpu.SemaphoreType.DMA
    planes, taps, upper, lower = call(
        cut_kernel,
        (
            whole(2, PLANES * OWN, 128), whole(8, ROWS), whole(4, PLANES, PHI),
            whole(3, PLANES, PHI),
        ),
        [dma((9,))], children.reshape(-1, PHI), theta_band.T, raw=2,
    )
    above = shifted_ring(lower, "theta", 1)
    below = shifted_ring(upper, "theta", -1)
    tables = (half(256, 512),) * 2 + (half(128, 256),) * 4
    packed, shift, *tables, codes, counts = call(
        functools.partial(own_forward_kernel, kinds=translators.shape[0]),
        (whole(16, 2, 4, 8, 128), whole(*child_shift.shape)) + tables + (half(64, 256),) * 2
        + (pltpu.VMEM(far_source.shape, jnp.int32), pltpu.SMEM(far_count.shape, jnp.int32)),
        [
            whole(1024, SAMPLES), pltpu.VMEM(far_source.shape, jnp.int32),
            pltpu.VMEM(far_source.shape, jnp.int32), dma((4,)),
        ],
        child_shift, far_source, far_offset, far_count, phi_interp, taps, planes,
        raw=4, out_specs=(vmem,) * 11 + (smem,),
    )
    *phi, above_table, below_table, back_high, back_low, up_table, down_table = tables
    operators = in_vmem(operator_rows(translators))
    scratch = [whole(2, 128, 128), whole(256, SAMPLES)]
    packed, codes = call(
        edge_forward_kernel(0),
        (whole(16, 2, 4, 8, 128), pltpu.SMEM((codes.size,), jnp.int32)), scratch + [dma],
        codes.reshape(-1), above, *phi, above_table, shift, packed,
        out_specs=(vmem, smem), aliases={6: 0},
    )
    packed = call(
        edge_forward_kernel(1), whole(16, 2, 4, 8, 128), scratch,
        below, *phi, below_table, shift, packed, aliases={5: 0},
    )
    packed, operators = lax.optimization_barrier((packed, operators))
    field = lax.all_to_all(packed, "clus", 0, 0)
    summed = translate(field, codes, counts, operators)
    local = lax.all_to_all(summed.reshape(packed.shape), "clus", 0, 0)
    scratch = [whole(2, 128, 128)]
    down = call(
        edge_back_kernel(12, 0), whole(4, PLANES, PHI), scratch,
        local, shift, *phi, down_table,
    )
    from_below = shifted_ring(down, "theta", 1)
    up = call(
        edge_back_kernel(0, 1), whole(3, PLANES, PHI), scratch,
        local, shift, *phi, up_table,
    )
    from_above = shifted_ring(up, "theta", -1)
    own = call(
        own_back_kernel, whole(2, PLANES * OWN, 128), [half(1024, SAMPLES)] * 2,
        local, shift, *phi, back_high, back_low,
    )
    result, _ = call(
        merge_kernel,
        (jax.ShapeDtypeStruct((PLANES * OWN, PHI), WHOLE), whole(2, PLANES * OWN, 128)),
        [dma((8,))], own, from_below, from_above, out_specs=(hbm, vmem), aliases={0: 1},
    )
    return result.reshape(children.shape)


def solution(mesh):
    return jax.shard_map(
        on_device,
        mesh=mesh,
        in_specs=(
            P("clus", None, None, "theta", None),
            P("theta", None),
            P(),
            P(None, None, "theta", None),
            P(None, None, ("theta", "clus"), None),
            P(),
            P(),
            P(),
        ),
        out_specs=P("clus", None, None, "theta", None),
        check_vma=False,
    )
```

```python
import jax
import jax.numpy as jnp
from jax import lax
from jax.experimental import pallas as pl
from jax.experimental.pallas import tpu as pltpu
from jax.sharding import PartitionSpec as P


KIDS = 4
LIST = 32
GROUP = 8
PAIR = 2
PLANES = 32
ROWS = 32
OWN = 16
PHI = 256
SAMPLES = 512
GRANT = 12 * 2**20
HALF = jnp.bfloat16
WHOLE = jnp.float32


def shifted_ring(value, axis, step):
    count = lax.axis_size(axis)
    return lax.ppermute(value, axis, [(i, (i + step) % count) for i in range(count)])


def halves(value):
    high = value.astype(HALF)
    return high, (value - high.astype(WHOLE)).astype(HALF)


def dot3(left, right, contract=0):
    dims = (((1,), (contract,)), ((), ()))
    total = None
    for a, b in ((0, 0), (0, 1), (1, 0)):
        part = lax.dot_general(left[a], right[b], dims, preferred_element_type=WHOLE)
        total = part if total is None else total + part
    return total


def swap_blocks(tiles):
    sub = lax.broadcasted_iota(jnp.int32, (8, 128), 0)
    even = (sub // 2) % 2 == 0
    low = sub < 4
    a, b, c, d = tiles

    def step(first, second, shift, mask):
        one = jnp.where(mask, first, pltpu.roll(second, shift, 0))
        two = jnp.where(mask, pltpu.roll(first, 8 - shift, 0), second)
        return one, two

    a, b = step(a, b, 2, even)
    c, d = step(c, d, 2, even)
    a, c = step(a, c, 4, low)
    b, d = step(b, d, 4, low)
    return a, b, c, d


def lane_blocks(value):
    return [value[:, 128 * i : 128 * (i + 1)] for i in range(4)]


def table_times(table, value):
    wide = jnp.dot(table, jnp.concatenate([value[0], value[0]], axis=0), preferred_element_type=WHOLE)
    depth = table.shape[1] // 2
    return wide + jnp.dot(table[:, :depth], value[1], preferred_element_type=WHOLE)


def same(child, parent):
    return child, parent


def above_rows(child, parent):
    return child - 4, parent


def below_rows(child, parent):
    return child + OWN, parent + ROWS - 8


def side_table(bands, place):
    row = lax.broadcasted_iota(jnp.int32, (8, 256), 0)
    column = lax.broadcasted_iota(jnp.int32, (8, 256), 1)
    tap = tap_of(column % 4, row, place)
    part = column // 64
    high, low = (value.astype(WHOLE) for value in halves(bands))
    block = jnp.zeros((8, 256), WHOLE)
    for t in range(8):
        value = jnp.where(part == 1, low[:, t : t + 1], high[:, t : t + 1])
        block = jnp.where(jnp.logical_and(tap == t, part < 3), value, block)
    owner = (column % 64) // 4
    blocks = [jnp.where(owner == plane, block, 0.0) for plane in range(16)]
    return jnp.concatenate(blocks, axis=0).astype(HALF)


def tap_of(child, parent, place):
    child, parent = place(child, parent)
    return child - parent // 2 + 3


def forward_table(bands, planes, inner, place):
    outer = bands.shape[0]
    width = planes * inner
    row = lax.broadcasted_iota(jnp.int32, (outer, width), 0)
    column = lax.broadcasted_iota(jnp.int32, (outer, width), 1)
    tap = tap_of(column % inner, row, place)
    block = jnp.zeros((outer, width), WHOLE)
    for t in range(8):
        block = jnp.where(tap == t, jnp.broadcast_to(bands[:, t : t + 1], block.shape), block)
    owner = column // inner
    blocks = [jnp.where(owner == plane, block, 0.0) for plane in range(planes)]
    return jnp.concatenate(blocks, axis=0)


def backward_table(bands, planes, inner, place):
    outer = bands.shape[1]
    width = planes * outer
    high = max(inner, 8)
    pick = lax.broadcasted_iota(jnp.int32, (outer, width), 1) % outer
    pick = (lax.broadcasted_iota(jnp.int32, (outer, width), 0) == pick).astype(HALF)
    row = lax.broadcasted_iota(jnp.int32, (high, width), 0)
    column = lax.broadcasted_iota(jnp.int32, (high, width), 1)
    tap = tap_of(row % inner, column % outer, place)
    tables = []
    for part in halves(bands):
        tiled = jnp.dot(part, pick, preferred_element_type=WHOLE)
        block = jnp.zeros((high, width), WHOLE)
        for t in range(8):
            block = jnp.where(tap == t, jnp.broadcast_to(tiled[t : t + 1], block.shape), block)
        owner = column // outer - row // inner
        step = high // inner
        blocks = [jnp.where(owner == plane, block, 0.0) for plane in range(0, planes, step)]
        tables.append(jnp.concatenate(blocks, axis=0).astype(HALF))
    return tables


def cut_kernel(children_hbm, taps_hbm, upper_ref, lower_ref, taps_ref, sems):
    copies = [
        pltpu.make_async_copy(children_hbm.at[:, row], upper_ref.at[row], sems.at[row])
        for row in range(4)
    ]
    for row in range(3):
        source = children_hbm.at[:, OWN - 3 + row]
        copies.append(pltpu.make_async_copy(source, lower_ref.at[row], sems.at[4 + row]))
    copies.append(pltpu.make_async_copy(taps_hbm, taps_ref, sems.at[7]))
    for copy in copies:
        copy.start()
    for copy in copies:
        copy.wait()


def both_sides(ref, first, count):
    return jnp.concatenate([ref[side, first : first + count] for side in range(2)], axis=1)


def own_forward_kernel(
    children_hbm, shift_hbm, source_hbm, offset_hbm, counts_hbm, operators_hbm, phi_ref, taps_ref,
    packed_ref, shift_ref, operators_ref, phi_high_ref, phi_low_ref, above_ref, below_ref, back_high_ref, back_low_ref,
    up_ref, down_ref, codes_ref, counts_ref,
    fine_ref, source_ref, offset_ref, children_ref, raw_ref, sems,
):
    kinds = raw_ref.shape[0] // 16
    pairs = (
        (children_hbm.at[:, :128], children_ref.at[0]), (children_hbm.at[:, 128:], children_ref.at[1]),
        (shift_hbm, shift_ref), (source_hbm, source_ref), (offset_hbm, offset_ref),
        (counts_hbm, counts_ref), (operators_hbm, raw_ref),
    )
    copies = [pltpu.make_async_copy(*pair, sems.at[i]) for i, pair in enumerate(pairs)]
    for copy in copies:
        copy.start()
    strip = lax.axis_index("theta")
    first = (strip > 0).astype(WHOLE)
    last = (strip < lax.axis_size("theta") - 1).astype(WHOLE)
    taps = taps_ref[...]
    bands = jnp.concatenate([taps] * 16, axis=0).T[:, :8]
    own = jnp.concatenate(halves(forward_table(bands, 8, 16, same)), axis=1)
    phi = halves(phi_ref[...])
    phi_high_ref[...], phi_low_ref[...] = phi

    def spread(group):
        mixed = dot3(halves(both_sides(children_ref, 128 * group, 128)), phi)
        fine_ref[256 * group : 256 * (group + 1)] = table_times(own, halves(mixed))

    def collect(parent):
        for pol in range(2):
            for block in range(4):
                rows = slice(8 * block, 8 * (block + 1))
                real, imag = gathered(fine_ref, shift_ref, parent, pol, 32, 8 * block, rows)
                for part, value in enumerate((real, imag)):
                    for pair, tile in enumerate(swap_blocks(lane_blocks(value))):
                        packed_ref[4 * block + pair, parent, 2 * pol + part] = tile

    for copy in copies[:2]:
        copy.wait()
    spread(0)
    spread(1)
    for copy in copies[2:]:
        copy.wait()
    spread(2)
    collect(0)
    spread(3)
    above_ref[...] = side_table(bands[:8] * first, above_rows)
    below_ref[...] = side_table(bands[ROWS - 8 :] * last, below_rows)
    back_high_ref[...], back_low_ref[...] = backward_table(taps, 8, 16, same)
    upper, lower = taps[:, :8] * first, taps[:, ROWS - 8 :] * last
    table = backward_table(upper, 16, 4, above_rows)
    up_ref[...] = jnp.concatenate(table, axis=1)
    table = backward_table(lower, 16, 4, below_rows)
    down_ref[...] = jnp.concatenate(table, axis=1)
    for kind in range(kinds):
        c = raw_ref[16 * kind : 16 * kind + 8]
        d = raw_ref[16 * kind + 8 : 16 * kind + 16]
        for at, value in enumerate((c, d - c, c + d)):
            operators_ref[24 * kind + 8 * at : 24 * kind + 8 * at + 8] = value
    operators_ref[24 * kinds : 24 * kinds + 24] = jnp.zeros((24, 128), WHOLE)
    lane = lax.broadcasted_iota(jnp.int32, (1, LIST), 1)
    for parent in range(source_ref.shape[0]):
        live = lane < counts_ref[parent]
        offset = jnp.where(live, offset_ref[parent : parent + 1], kinds)
        codes_ref[parent : parent + 1] = source_ref[parent : parent + 1] * 32 + offset * (24 * 65536)
    collect(1)


def gathered(fine_ref, shift_ref, parent, pol, per_plane, first, rows):
    real = imag = None
    for kid in range(KIDS):
        at = ((parent * KIDS + kid) * 4 + pol * 2) * per_plane + first
        a = fine_ref[at : at + 8]
        b = fine_ref[at + per_plane : at + per_plane + 8]
        c = shift_ref[kid, 0, rows]
        d = shift_ref[kid, 1, rows]
        one, two = c * a - d * b, c * b + d * a
        real = one if real is None else real + one
        imag = two if imag is None else imag + two
    return real, imag


def edge_forward_kernel(side):
    first, count = 12 * side, 3 + side

    def kernel(*refs):
        if side == 0:
            codes_src, halo_in, phi_high_ref, phi_low_ref, table_ref, shift_ref = refs[:6]
            _, out_ref, codes_ref, halo_ref, fine_ref, sem = refs[6:]
            codes = pltpu.make_async_copy(codes_src, codes_ref, sem)
            codes.start()
        else:
            halo_in, phi_high_ref, phi_low_ref, table_ref, shift_ref = refs[:5]
            _, out_ref, halo_ref, fine_ref = refs[5:]
        for half in range(2):
            lanes = slice(128 * half, 128 * half + 128)
            if side == 0:
                halo_ref[half, pl.ds(0, PLANES, stride=4), :] = jnp.zeros((PLANES, 128), WHOLE)
            for row in range(count):
                rows = pl.ds(row + 4 - count, PLANES, stride=4)
                halo_ref[half, rows, :] = halo_in[row, :, lanes]
        phi = (phi_high_ref[...], phi_low_ref[...])
        high, low = halves(dot3(halves(both_sides(halo_ref, 0, 128)), phi))
        table = table_ref[...]
        for parent in range(2):
            rows = slice(64 * parent, 64 * parent + 64)
            value = jnp.concatenate([high[rows], high[rows], low[rows], high[rows]], axis=0)
            fine = jnp.dot(table, value, preferred_element_type=WHOLE)
            fine_ref[128 * parent : 128 * parent + 128] = fine
        rows = slice(24 * side, 24 * side + 8)
        for parent in range(2):
            for pol in range(2):
                real, imag = gathered(fine_ref, shift_ref, parent, pol, 8, 0, rows)
                for part, value in enumerate((real, imag)):
                    for pair, tile in enumerate(swap_blocks(lane_blocks(value))):
                        at = (first + pair, parent, 2 * pol + part)
                        out_ref[at] = out_ref[at] + tile
        if side == 0:
            codes.wait()

    return kernel


def spread_back(local_ref, shift_ref, parent, pol, blocks):
    parts = []
    for part in range(2):
        pieces = []
        for first in blocks:
            tiles = [local_ref[first + pair, parent, 2 * pol + part] for pair in range(4)]
            pieces.append(jnp.concatenate(swap_blocks(tiles), axis=1))
        parts.append(pieces)
    for kid in range(KIDS):
        real, imag = [], []
        for index, first in enumerate(blocks):
            a, b = parts[0][index], parts[1][index]
            c = shift_ref[kid, 0, 2 * first : 2 * first + 8]
            d = shift_ref[kid, 1, 2 * first : 2 * first + 8]
            real.append(c * a + d * b)
            imag.append(c * b - d * a)
        yield kid, halves(jnp.concatenate(real + imag, axis=0))


def edge_back_kernel(
    local_ref, shift_ref, phi_high_ref, phi_low_ref, up_table_ref, down_table_ref,
    up_ref, down_ref, result_ref,
):
    phi = (phi_high_ref[...], phi_low_ref[...])
    narrow = []
    for first, table_ref in ((12, down_table_ref), (0, up_table_ref)):
        table = table_ref[...]
        for parent in range(2):
            pieces = {}
            for pol in range(2):
                for kid, value in spread_back(local_ref, shift_ref, parent, pol, (first,)):
                    pieces[kid, pol] = value
            order = [(kid, pol) for kid in range(KIDS) for pol in range(2)]
            value = [jnp.concatenate([pieces[at][i] for at in order], axis=0) for i in range(2)]
            narrow.append(table_times(table, value))
    result = dot3(halves(jnp.concatenate(narrow, axis=0)), phi, contract=1)
    for side in range(2):
        lanes = slice(128 * side, 128 * side + 128)
        result_ref[side] = result[:, lanes]
        for row in range(4):
            down_ref[row, :, lanes] = result_ref[side, pl.ds(row, PLANES, stride=4), :]
        for row in range(3):
            rows = pl.ds(4 * PLANES + row + 1, PLANES, stride=4)
            up_ref[row, :, lanes] = result_ref[side, rows, :]


def own_back_kernel(
    local_ref, shift_ref, phi_high_ref, phi_low_ref, table_high_ref, table_low_ref,
    own_ref, high_ref, low_ref,
):
    phi = (phi_high_ref[...], phi_low_ref[...])
    table = (table_high_ref[...], table_low_ref[...])

    for parent in range(2):
        for pol in range(2):
            for kid, value in spread_back(local_ref, shift_ref, parent, pol, (0, 4, 8, 12)):
                at = ((parent * KIDS + kid) * 2 + pol) * 64
                high_ref[at : at + 64], low_ref[at : at + 64] = value
        for group in (2 * parent, 2 * parent + 1):
            rows = slice(256 * group, 256 * (group + 1))
            narrowed = dot3(table, (high_ref[rows], low_ref[rows]))
            result = dot3(halves(narrowed), phi, contract=1)
            for side in range(2):
                lanes = slice(128 * side, 128 * side + 128)
                own_ref[side, 128 * group : 128 * (group + 1)] = result[:, lanes]


def translate_kernel(codes_ref, counts_ref, field_ref, table_ref, out_ref, sum_ref):
    parents = counts_ref.shape[0]
    for at in range(2 * parents):
        rows = slice(16 * at, 16 * at + 8)
        sum_ref[8 * at : 8 * at + 8] = field_ref[rows] + field_ref[16 * at + 8 : 16 * at + 16]

    def one_pair(pair, carry):
        def some_slots(step, sums):
            sums = list(sums)
            for member in range(PAIR):
                for lane in range(GROUP):
                    slot = pair * (PAIR * LIST) + step * GROUP + (member * LIST + lane)
                    code = codes_ref[slot]
                    source = pl.multiple_of(code & 0xFFFF, 8)
                    offset = pl.multiple_of(code >> 16, 8)
                    half = pl.multiple_of((code & 0xFFFF) >> 1, 8)
                    c = table_ref[pl.ds(offset, 8), :]
                    less = table_ref[pl.ds(offset + 8, 8), :]
                    more = table_ref[pl.ds(offset + 16, 8), :]
                    for pol in range(2):
                        at = member * 6 + pol * 3
                        a = field_ref[pl.ds(source + pol * 16, 8), :]
                        b = field_ref[pl.ds(source + (pol * 16 + 8), 8), :]
                        sums[at] = sums[at] + c * sum_ref[pl.ds(half + pol * 8, 8), :]
                        sums[at + 1] = sums[at + 1] + a * less
                        sums[at + 2] = sums[at + 2] + b * more
            return tuple(sums)

        zero = jnp.zeros((8, 128), WHOLE)
        longest = jnp.maximum(counts_ref[pair * PAIR], counts_ref[pair * PAIR + 1])
        steps = lax.shift_right_logical(longest + (GROUP - 1), 3)
        sums = lax.fori_loop(0, steps, some_slots, (zero,) * (6 * PAIR))
        for member in range(PAIR):
            for pol in range(2):
                both, less, more = sums[member * 6 + pol * 3 : member * 6 + pol * 3 + 3]
                at = pl.multiple_of(pair * 64 + member * 32 + pol * 16, 8)
                out_ref[pl.ds(at, 8), :] = both - more
                out_ref[pl.ds(at + 8, 8), :] = both + less
        return carry

    lax.fori_loop(0, parents // PAIR, one_pair, 0)


def in_vmem(value):
    return pltpu.with_memory_space_constraint(value, pltpu.VMEM)


def in_smem(value):
    return pltpu.with_memory_space_constraint(value, pltpu.SMEM)


def in_hbm(value):
    return pltpu.with_memory_space_constraint(value, pltpu.HBM)


def call(kernel, outs, scratch, *operands, raw=0, out_specs=None, aliases={}):
    vmem = pl.BlockSpec(memory_space=pltpu.VMEM)
    hbm = pl.BlockSpec(memory_space=pltpu.HBM)
    return pl.pallas_call(
        kernel,
        out_shape=outs,
        in_specs=[hbm] * raw + [vmem] * (len(operands) - raw),
        out_specs=out_specs if out_specs is not None else jax.tree.map(lambda _: vmem, outs),
        scratch_shapes=scratch,
        input_output_aliases=aliases,
        compiler_params=pltpu.CompilerParams(vmem_limit_bytes=GRANT),
    )(*map(in_hbm, operands[:raw]), *map(in_vmem, operands[raw:]))


def operator_rows(translators):
    kinds, _, rows, samples = translators.shape
    table = translators.reshape(kinds, 2, rows, samples // 128, 128).transpose(0, 1, 3, 2, 4)
    return table.reshape(kinds * 16, 128)


def translate(field, codes, counts, operators):
    smem = pl.BlockSpec(memory_space=pltpu.SMEM)
    vmem = pl.BlockSpec(memory_space=pltpu.VMEM)
    field = field.reshape(-1, 128)
    return pl.pallas_call(
        translate_kernel,
        out_shape=jax.ShapeDtypeStruct(field.shape, WHOLE),
        in_specs=[smem, smem, vmem, vmem],
        out_specs=vmem,
        scratch_shapes=[
            pltpu.VMEM((field.shape[0] // 2, 128), WHOLE),
        ],
        compiler_params=pltpu.CompilerParams(vmem_limit_bytes=GRANT),
        name="translate",
    )(in_smem(codes), in_smem(counts), in_vmem(field), in_vmem(operators))


def merge_kernel(_, top_ref, bottom_ref, out_hbm, own_ref, sems):
    copies = []
    for i in range(4):
        chunk = slice(128 * i, 128 * i + 128)
        for side in range(2):
            lanes = slice(128 * side, 128 * side + 128)
            for ref, first, count in ((top_ref, 0, 4), (bottom_ref, OWN - 3, 3)):
                for row in range(count):
                    rows = pl.ds(128 * i + first + row, 8, stride=OWN)
                    value = own_ref[side, rows, :] + ref[row, 8 * i : 8 * i + 8, lanes]
                    own_ref[side, rows, :] = value
            target = out_hbm.at[chunk, lanes]
            copy = pltpu.make_async_copy(own_ref.at[side, chunk], target, sems.at[2 * i + side])
            copy.start()
            copies.append(copy)
    for copy in copies:
        copy.wait()


def on_device(
    children, theta_band, phi_interp, child_shift, translators, far_source, far_offset, far_count
):
    half = lambda *shape: pltpu.VMEM(shape, HALF)
    whole = lambda *shape: pltpu.VMEM(shape, WHOLE)
    hbm = pl.BlockSpec(memory_space=pl.ANY)
    vmem = pl.BlockSpec(memory_space=pltpu.VMEM)
    smem = pl.BlockSpec(memory_space=pltpu.SMEM)
    dma = pltpu.SemaphoreType.DMA
    upper, lower, taps = call(
        cut_kernel, (whole(4, PLANES, PHI), whole(3, PLANES, PHI), whole(8, ROWS)),
        [dma((8,))], children.reshape(PLANES, OWN, PHI), theta_band.T, raw=2,
    )
    above = shifted_ring(lower, "theta", 1)
    below = shifted_ring(upper, "theta", -1)
    tables = (half(256, 512),) * 2 + (half(128, 256),) * 4
    operators = operator_rows(translators)
    packed, shift, operators, *tables, codes, counts = call(
        own_forward_kernel,
        (
            whole(16, 2, 4, 8, 128), whole(*child_shift.shape),
            whole(operators.shape[0] * 3 // 2 + 24, 128),
        )
        + tables + (half(64, 256),) * 2
        + (pltpu.VMEM(far_source.shape, jnp.int32), pltpu.SMEM(far_count.shape, jnp.int32)),
        [
            whole(1024, SAMPLES), pltpu.VMEM(far_source.shape, jnp.int32),
            pltpu.VMEM(far_source.shape, jnp.int32), whole(2, PLANES * OWN, 128),
            whole(*operators.shape), dma((7,)),
        ],
        children.reshape(-1, PHI), child_shift, far_source, far_offset, far_count, operators,
        phi_interp, taps, raw=6, out_specs=(vmem,) * 12 + (smem,),
    )
    *phi, above_table, below_table, back_high, back_low, up_table, down_table = tables
    scratch = [whole(2, 128, 128), whole(256, SAMPLES)]
    packed, codes = call(
        edge_forward_kernel(0),
        (whole(16, 2, 4, 8, 128), pltpu.SMEM((codes.size,), jnp.int32)), scratch + [dma],
        codes.reshape(-1), above, *phi, above_table, shift, packed,
        out_specs=(vmem, smem), aliases={6: 0},
    )
    packed = call(
        edge_forward_kernel(1), whole(16, 2, 4, 8, 128), scratch,
        below, *phi, below_table, shift, packed, aliases={5: 0},
    )
    field = lax.all_to_all(packed, "clus", 0, 0)
    summed = translate(field, codes, counts, operators)
    local = lax.all_to_all(summed.reshape(packed.shape), "clus", 0, 0)
    up, down = call(
        edge_back_kernel, (whole(3, PLANES, PHI), whole(4, PLANES, PHI)),
        [whole(2, 256, 128)], local, shift, *phi, up_table, down_table,
    )
    from_below = shifted_ring(down, "theta", 1)
    from_above = shifted_ring(up, "theta", -1)
    own = call(
        own_back_kernel, whole(2, PLANES * OWN, 128), [half(1024, SAMPLES)] * 2,
        local, shift, *phi, back_high, back_low,
    )
    result, _ = call(
        merge_kernel,
        (jax.ShapeDtypeStruct((PLANES * OWN, PHI), WHOLE), whole(2, PLANES * OWN, 128)),
        [dma((8,))], own, from_below, from_above, out_specs=(hbm, vmem), aliases={0: 1},
    )
    return result.reshape(children.shape)


def solution(mesh):
    return jax.shard_map(
        on_device,
        mesh=mesh,
        in_specs=(
            P("clus", None, None, "theta", None),
            P("theta", None),
            P(),
            P(None, None, "theta", None),
            P(None, None, ("theta", "clus"), None),
            P(),
            P(),
            P(),
        ),
        out_specs=P("clus", None, None, "theta", None),
        check_vma=False,
    )
```

```python
import functools

import jax
import jax.numpy as jnp
from jax import lax
from jax.experimental import pallas as pl
from jax.experimental.pallas import tpu as pltpu
from jax.sharding import PartitionSpec as P


KIDS = 4
LIST = 32
GROUP = 8
PAIR = 2
PLANES = 32
ROWS = 32
OWN = 16
PHI = 256
SAMPLES = 512
GRANT = 12 * 2**20
HALF = jnp.bfloat16
WHOLE = jnp.float32


def shifted_ring(value, axis, step):
    count = lax.axis_size(axis)
    return lax.ppermute(value, axis, [(i, (i + step) % count) for i in range(count)])


def halves(value):
    high = value.astype(HALF)
    return high, (value - high.astype(WHOLE)).astype(HALF)


def dot3(left, right, contract=0):
    dims = (((1,), (contract,)), ((), ()))
    total = None
    for a, b in ((0, 0), (0, 1), (1, 0)):
        part = lax.dot_general(left[a], right[b], dims, preferred_element_type=WHOLE)
        total = part if total is None else total + part
    return total


def swap_blocks(tiles):
    sub = lax.broadcasted_iota(jnp.int32, (8, 128), 0)
    even = (sub // 2) % 2 == 0
    low = sub < 4
    a, b, c, d = tiles

    def step(first, second, shift, mask):
        one = jnp.where(mask, first, pltpu.roll(second, shift, 0))
        two = jnp.where(mask, pltpu.roll(first, 8 - shift, 0), second)
        return one, two

    a, b = step(a, b, 2, even)
    c, d = step(c, d, 2, even)
    a, c = step(a, c, 4, low)
    b, d = step(b, d, 4, low)
    return a, b, c, d


def lane_blocks(value):
    return [value[:, 128 * i : 128 * (i + 1)] for i in range(4)]


def table_times(table, value):
    wide = jnp.dot(table, jnp.concatenate([value[0], value[0]], axis=0), preferred_element_type=WHOLE)
    depth = table.shape[1] // 2
    return wide + jnp.dot(table[:, :depth], value[1], preferred_element_type=WHOLE)


def same(child, parent):
    return child, parent


def above_rows(child, parent):
    return child - 4, parent


def below_rows(child, parent):
    return child + OWN, parent + ROWS - 8


def side_table(bands, place):
    row = lax.broadcasted_iota(jnp.int32, (8, 256), 0)
    column = lax.broadcasted_iota(jnp.int32, (8, 256), 1)
    tap = tap_of(column % 4, row, place)
    part = column // 64
    high, low = (value.astype(WHOLE) for value in halves(bands))
    block = jnp.zeros((8, 256), WHOLE)
    for t in range(8):
        value = jnp.where(part == 1, low[:, t : t + 1], high[:, t : t + 1])
        block = jnp.where(jnp.logical_and(tap == t, part < 3), value, block)
    owner = (column % 64) // 4
    blocks = [jnp.where(owner == plane, block, 0.0) for plane in range(16)]
    return jnp.concatenate(blocks, axis=0).astype(HALF)


def tap_of(child, parent, place):
    child, parent = place(child, parent)
    return child - parent // 2 + 3


def forward_table(bands, planes, inner, place):
    outer = bands.shape[0]
    width = planes * inner
    row = lax.broadcasted_iota(jnp.int32, (outer, width), 0)
    column = lax.broadcasted_iota(jnp.int32, (outer, width), 1)
    tap = tap_of(column % inner, row, place)
    block = jnp.zeros((outer, width), WHOLE)
    for t in range(8):
        block = jnp.where(tap == t, jnp.broadcast_to(bands[:, t : t + 1], block.shape), block)
    owner = column // inner
    blocks = [jnp.where(owner == plane, block, 0.0) for plane in range(planes)]
    return jnp.concatenate(blocks, axis=0)


def backward_table(bands, planes, inner, place):
    outer = bands.shape[1]
    width = planes * outer
    high = max(inner, 8)
    pick = lax.broadcasted_iota(jnp.int32, (outer, width), 1) % outer
    pick = (lax.broadcasted_iota(jnp.int32, (outer, width), 0) == pick).astype(HALF)
    row = lax.broadcasted_iota(jnp.int32, (high, width), 0)
    column = lax.broadcasted_iota(jnp.int32, (high, width), 1)
    tap = tap_of(row % inner, column % outer, place)
    tables = []
    for part in halves(bands):
        tiled = jnp.dot(part, pick, preferred_element_type=WHOLE)
        block = jnp.zeros((high, width), WHOLE)
        for t in range(8):
            block = jnp.where(tap == t, jnp.broadcast_to(tiled[t : t + 1], block.shape), block)
        owner = column // outer - row // inner
        step = high // inner
        blocks = [jnp.where(owner == plane, block, 0.0) for plane in range(0, planes, step)]
        tables.append(jnp.concatenate(blocks, axis=0).astype(HALF))
    return tables


def cut_kernel(
    children_hbm, taps_hbm, children_ref, taps_ref, upper_ref, lower_ref, sems
):
    chunks = [slice(128 * i, 128 * i + 128) for i in range(4)]
    copies = [
        pltpu.make_async_copy(
            children_hbm.at[chunk, 128 * side : 128 * side + 128],
            children_ref.at[side, chunk],
            sems.at[2 * i + side],
        )
        for i, chunk in enumerate(chunks)
        for side in range(2)
    ]
    for copy in copies:
        copy.start()
    taps = pltpu.make_async_copy(taps_hbm, taps_ref, sems.at[8])
    taps.start()
    for at, copy in enumerate(copies):
        copy.wait()
        i, side = divmod(at, 2)
        for ref, first, count in ((upper_ref, 0, 4), (lower_ref, OWN - 3, 3)):
            for row in range(count):
                rows = pl.ds(128 * i + first + row, 8, stride=OWN)
                value = children_ref[side, rows, :]
                ref[row, 8 * i : 8 * i + 8, 128 * side : 128 * side + 128] = value
    taps.wait()


def both_sides(ref, first, count):
    return jnp.concatenate([ref[side, first : first + count] for side in range(2)], axis=1)


def own_forward_kernel(
    shift_hbm, source_hbm, offset_hbm, counts_hbm, phi_ref, taps_ref, children_ref,
    packed_ref, shift_ref, phi_high_ref, phi_low_ref, above_ref, below_ref, back_high_ref, back_low_ref,
    up_ref, down_ref, codes_ref, counts_ref,
    fine_ref, source_ref, offset_ref, sems, *, kinds,
):
    pairs = (
        (shift_hbm, shift_ref), (source_hbm, source_ref), (offset_hbm, offset_ref),
        (counts_hbm, counts_ref),
    )
    copies = [pltpu.make_async_copy(*pair, sems.at[i]) for i, pair in enumerate(pairs)]
    for copy in copies:
        copy.start()
    strip = lax.axis_index("theta")
    first = (strip > 0).astype(WHOLE)
    last = (strip < lax.axis_size("theta") - 1).astype(WHOLE)
    taps = taps_ref[...]
    bands = jnp.concatenate([taps] * 16, axis=0).T[:, :8]
    own = jnp.concatenate(halves(forward_table(bands, 8, 16, same)), axis=1)
    phi = halves(phi_ref[...])
    phi_high_ref[...], phi_low_ref[...] = phi

    def spread(group):
        mixed = dot3(halves(both_sides(children_ref, 128 * group, 128)), phi)
        fine_ref[256 * group : 256 * (group + 1)] = table_times(own, halves(mixed))

    def collect(parent):
        for pol in range(2):
            for block in range(4):
                rows = slice(8 * block, 8 * (block + 1))
                real, imag = gathered(fine_ref, shift_ref, parent, pol, 32, 8 * block, rows)
                for part, value in enumerate((real, imag)):
                    for pair, tile in enumerate(swap_blocks(lane_blocks(value))):
                        packed_ref[4 * block + pair, parent, 2 * pol + part] = tile

    spread(0)
    spread(1)
    for copy in copies:
        copy.wait()
    spread(2)
    collect(0)
    spread(3)
    above_ref[...] = side_table(bands[:8] * first, above_rows)
    below_ref[...] = side_table(bands[ROWS - 8 :] * last, below_rows)
    back_high_ref[...], back_low_ref[...] = backward_table(taps, 8, 16, same)
    upper, lower = taps[:, :8] * first, taps[:, ROWS - 8 :] * last
    table = backward_table(upper, 16, 4, above_rows)
    up_ref[...] = jnp.concatenate(table, axis=1)
    table = backward_table(lower, 16, 4, below_rows)
    down_ref[...] = jnp.concatenate(table, axis=1)
    lane = lax.broadcasted_iota(jnp.int32, (1, LIST), 1)
    for parent in range(source_ref.shape[0]):
        live = lane < counts_ref[parent]
        offset = jnp.where(live, offset_ref[parent : parent + 1], kinds)
        codes_ref[parent : parent + 1] = source_ref[parent : parent + 1] * 32 + offset * (24 * 65536)
    collect(1)


def gathered(fine_ref, shift_ref, parent, pol, per_plane, first, rows):
    real = imag = None
    for kid in range(KIDS):
        at = ((parent * KIDS + kid) * 4 + pol * 2) * per_plane + first
        a = fine_ref[at : at + 8]
        b = fine_ref[at + per_plane : at + per_plane + 8]
        c = shift_ref[kid, 0, rows]
        d = shift_ref[kid, 1, rows]
        one, two = c * a - d * b, c * b + d * a
        real = one if real is None else real + one
        imag = two if imag is None else imag + two
    return real, imag


def edge_forward_kernel(side):
    first, count = 12 * side, 3 + side

    def kernel(*refs):
        if side == 0:
            codes_src, halo_in, phi_high_ref, phi_low_ref, table_ref, shift_ref = refs[:6]
            _, out_ref, codes_ref, halo_ref, fine_ref, sem = refs[6:]
            codes = pltpu.make_async_copy(codes_src, codes_ref, sem)
            codes.start()
        else:
            halo_in, phi_high_ref, phi_low_ref, table_ref, shift_ref = refs[:5]
            _, out_ref, halo_ref, fine_ref = refs[5:]
        for half in range(2):
            lanes = slice(128 * half, 128 * half + 128)
            if side == 0:
                halo_ref[half, pl.ds(0, PLANES, stride=4), :] = jnp.zeros((PLANES, 128), WHOLE)
            for row in range(count):
                rows = pl.ds(row + 4 - count, PLANES, stride=4)
                halo_ref[half, rows, :] = halo_in[row, :, lanes]
        phi = (phi_high_ref[...], phi_low_ref[...])
        high, low = halves(dot3(halves(both_sides(halo_ref, 0, 128)), phi))
        table = table_ref[...]
        for parent in range(2):
            rows = slice(64 * parent, 64 * parent + 64)
            value = jnp.concatenate([high[rows], high[rows], low[rows], high[rows]], axis=0)
            fine = jnp.dot(table, value, preferred_element_type=WHOLE)
            fine_ref[128 * parent : 128 * parent + 128] = fine
        rows = slice(24 * side, 24 * side + 8)
        for parent in range(2):
            for pol in range(2):
                real, imag = gathered(fine_ref, shift_ref, parent, pol, 8, 0, rows)
                for part, value in enumerate((real, imag)):
                    for pair, tile in enumerate(swap_blocks(lane_blocks(value))):
                        at = (first + pair, parent, 2 * pol + part)
                        out_ref[at] = out_ref[at] + tile
        if side == 0:
            codes.wait()

    return kernel


def spread_back(local_ref, shift_ref, parent, pol, blocks):
    parts = []
    for part in range(2):
        pieces = []
        for first in blocks:
            tiles = [local_ref[first + pair, parent, 2 * pol + part] for pair in range(4)]
            pieces.append(jnp.concatenate(swap_blocks(tiles), axis=1))
        parts.append(pieces)
    for kid in range(KIDS):
        real, imag = [], []
        for index, first in enumerate(blocks):
            a, b = parts[0][index], parts[1][index]
            c = shift_ref[kid, 0, 2 * first : 2 * first + 8]
            d = shift_ref[kid, 1, 2 * first : 2 * first + 8]
            real.append(c * a + d * b)
            imag.append(c * b - d * a)
        yield kid, halves(jnp.concatenate(real + imag, axis=0))


def edge_back_kernel(
    local_ref, shift_ref, phi_high_ref, phi_low_ref, up_table_ref, down_table_ref,
    up_ref, down_ref, result_ref,
):
    phi = (phi_high_ref[...], phi_low_ref[...])
    narrow = []
    for first, table_ref in ((12, down_table_ref), (0, up_table_ref)):
        table = table_ref[...]
        for parent in range(2):
            pieces = {}
            for pol in range(2):
                for kid, value in spread_back(local_ref, shift_ref, parent, pol, (first,)):
                    pieces[kid, pol] = value
            order = [(kid, pol) for kid in range(KIDS) for pol in range(2)]
            value = [jnp.concatenate([pieces[at][i] for at in order], axis=0) for i in range(2)]
            narrow.append(table_times(table, value))
    result = dot3(halves(jnp.concatenate(narrow, axis=0)), phi, contract=1)
    for side in range(2):
        lanes = slice(128 * side, 128 * side + 128)
        result_ref[side] = result[:, lanes]
        for row in range(4):
            down_ref[row, :, lanes] = result_ref[side, pl.ds(row, PLANES, stride=4), :]
        for row in range(3):
            rows = pl.ds(4 * PLANES + row + 1, PLANES, stride=4)
            up_ref[row, :, lanes] = result_ref[side, rows, :]


def own_back_kernel(
    local_ref, shift_ref, phi_high_ref, phi_low_ref, table_high_ref, table_low_ref,
    own_ref, high_ref, low_ref,
):
    phi = (phi_high_ref[...], phi_low_ref[...])
    table = (table_high_ref[...], table_low_ref[...])

    for parent in range(2):
        for pol in range(2):
            for kid, value in spread_back(local_ref, shift_ref, parent, pol, (0, 4, 8, 12)):
                at = ((parent * KIDS + kid) * 2 + pol) * 64
                high_ref[at : at + 64], low_ref[at : at + 64] = value
        for group in (2 * parent, 2 * parent + 1):
            rows = slice(256 * group, 256 * (group + 1))
            narrowed = dot3(table, (high_ref[rows], low_ref[rows]))
            result = dot3(halves(narrowed), phi, contract=1)
            for side in range(2):
                lanes = slice(128 * side, 128 * side + 128)
                own_ref[side, 128 * group : 128 * (group + 1)] = result[:, lanes]


def translate_kernel(codes_ref, counts_ref, field_ref, operator_ref, out_ref, table_ref, sum_ref):
    parents = counts_ref.shape[0]
    kinds = operator_ref.shape[0] // 16
    for kind in range(kinds):
        c = operator_ref[16 * kind : 16 * kind + 8]
        d = operator_ref[16 * kind + 8 : 16 * kind + 16]
        for at, value in enumerate((c, d - c, c + d)):
            table_ref[24 * kind + 8 * at : 24 * kind + 8 * at + 8] = value
    table_ref[24 * kinds : 24 * kinds + 24] = jnp.zeros((24, 128), WHOLE)
    for at in range(2 * parents):
        rows = slice(16 * at, 16 * at + 8)
        sum_ref[8 * at : 8 * at + 8] = field_ref[rows] + field_ref[16 * at + 8 : 16 * at + 16]

    def one_pair(pair, carry):
        def some_slots(step, sums):
            sums = list(sums)
            for member in range(PAIR):
                for lane in range(GROUP):
                    slot = pair * (PAIR * LIST) + step * GROUP + (member * LIST + lane)
                    code = codes_ref[slot]
                    source = pl.multiple_of(code & 0xFFFF, 8)
                    offset = pl.multiple_of(code >> 16, 8)
                    half = pl.multiple_of((code & 0xFFFF) >> 1, 8)
                    c = table_ref[pl.ds(offset, 8), :]
                    less = table_ref[pl.ds(offset + 8, 8), :]
                    more = table_ref[pl.ds(offset + 16, 8), :]
                    for pol in range(2):
                        at = member * 6 + pol * 3
                        a = field_ref[pl.ds(source + pol * 16, 8), :]
                        b = field_ref[pl.ds(source + (pol * 16 + 8), 8), :]
                        sums[at] = sums[at] + c * sum_ref[pl.ds(half + pol * 8, 8), :]
                        sums[at + 1] = sums[at + 1] + a * less
                        sums[at + 2] = sums[at + 2] + b * more
            return tuple(sums)

        zero = jnp.zeros((8, 128), WHOLE)
        longest = jnp.maximum(counts_ref[pair * PAIR], counts_ref[pair * PAIR + 1])
        steps = lax.shift_right_logical(longest + (GROUP - 1), 3)
        sums = lax.fori_loop(0, steps, some_slots, (zero,) * (6 * PAIR))
        for member in range(PAIR):
            for pol in range(2):
                both, less, more = sums[member * 6 + pol * 3 : member * 6 + pol * 3 + 3]
                at = pl.multiple_of(pair * 64 + member * 32 + pol * 16, 8)
                out_ref[pl.ds(at, 8), :] = both - more
                out_ref[pl.ds(at + 8, 8), :] = both + less
        return carry

    lax.fori_loop(0, parents // PAIR, one_pair, 0)


def in_vmem(value):
    return pltpu.with_memory_space_constraint(value, pltpu.VMEM)


def in_smem(value):
    return pltpu.with_memory_space_constraint(value, pltpu.SMEM)


def in_hbm(value):
    return pltpu.with_memory_space_constraint(value, pltpu.HBM)


def call(kernel, outs, scratch, *operands, raw=0, out_specs=None, aliases={}):
    vmem = pl.BlockSpec(memory_space=pltpu.VMEM)
    hbm = pl.BlockSpec(memory_space=pltpu.HBM)
    return pl.pallas_call(
        kernel,
        out_shape=outs,
        in_specs=[hbm] * raw + [vmem] * (len(operands) - raw),
        out_specs=out_specs if out_specs is not None else jax.tree.map(lambda _: vmem, outs),
        scratch_shapes=scratch,
        input_output_aliases=aliases,
        compiler_params=pltpu.CompilerParams(vmem_limit_bytes=GRANT),
    )(*map(in_hbm, operands[:raw]), *map(in_vmem, operands[raw:]))


def operator_rows(translators):
    kinds, _, rows, samples = translators.shape
    table = translators.reshape(kinds, 2, rows, samples // 128, 128).transpose(0, 1, 3, 2, 4)
    return table.reshape(kinds * 16, 128)


def translate(field, codes, counts, operators):
    smem = pl.BlockSpec(memory_space=pltpu.SMEM)
    vmem = pl.BlockSpec(memory_space=pltpu.VMEM)
    field = field.reshape(-1, 128)
    return pl.pallas_call(
        translate_kernel,
        out_shape=jax.ShapeDtypeStruct(field.shape, WHOLE),
        in_specs=[smem, smem, vmem, vmem],
        out_specs=vmem,
        scratch_shapes=[
            pltpu.VMEM((operators.shape[0] * 3 // 2 + 24, 128), WHOLE),
            pltpu.VMEM((field.shape[0] // 2, 128), WHOLE),
        ],
        compiler_params=pltpu.CompilerParams(vmem_limit_bytes=GRANT),
        name="translate",
    )(in_smem(codes), in_smem(counts), in_vmem(field), in_vmem(operators))


def merge_kernel(_, top_ref, bottom_ref, out_hbm, own_ref, sems):
    copies = []
    for i in range(4):
        chunk = slice(128 * i, 128 * i + 128)
        for side in range(2):
            lanes = slice(128 * side, 128 * side + 128)
            for ref, first, count in ((top_ref, 0, 4), (bottom_ref, OWN - 3, 3)):
                for row in range(count):
                    rows = pl.ds(128 * i + first + row, 8, stride=OWN)
                    value = own_ref[side, rows, :] + ref[row, 8 * i : 8 * i + 8, lanes]
                    own_ref[side, rows, :] = value
            target = out_hbm.at[chunk, lanes]
            copy = pltpu.make_async_copy(own_ref.at[side, chunk], target, sems.at[2 * i + side])
            copy.start()
            copies.append(copy)
    for copy in copies:
        copy.wait()


def on_device(
    children, theta_band, phi_interp, child_shift, translators, far_source, far_offset, far_count
):
    half = lambda *shape: pltpu.VMEM(shape, HALF)
    whole = lambda *shape: pltpu.VMEM(shape, WHOLE)
    hbm = pl.BlockSpec(memory_space=pl.ANY)
    vmem = pl.BlockSpec(memory_space=pltpu.VMEM)
    smem = pl.BlockSpec(memory_space=pltpu.SMEM)
    dma = pltpu.SemaphoreType.DMA
    planes, taps, upper, lower = call(
        cut_kernel,
        (
            whole(2, PLANES * OWN, 128), whole(8, ROWS), whole(4, PLANES, PHI),
            whole(3, PLANES, PHI),
        ),
        [dma((9,))], children.reshape(-1, PHI), theta_band.T, raw=2,
    )
    above = shifted_ring(lower, "theta", 1)
    below = shifted_ring(upper, "theta", -1)
    tables = (half(256, 512),) * 2 + (half(128, 256),) * 4
    packed, shift, *tables, codes, counts = call(
        functools.partial(own_forward_kernel, kinds=translators.shape[0]),
        (whole(16, 2, 4, 8, 128), whole(*child_shift.shape)) + tables + (half(64, 256),) * 2
        + (pltpu.VMEM(far_source.shape, jnp.int32), pltpu.SMEM(far_count.shape, jnp.int32)),
        [
            whole(1024, SAMPLES), pltpu.VMEM(far_source.shape, jnp.int32),
            pltpu.VMEM(far_source.shape, jnp.int32), dma((4,)),
        ],
        child_shift, far_source, far_offset, far_count, phi_interp, taps, planes,
        raw=4, out_specs=(vmem,) * 11 + (smem,),
    )
    *phi, above_table, below_table, back_high, back_low, up_table, down_table = tables
    operators = in_vmem(operator_rows(translators))
    scratch = [whole(2, 128, 128), whole(256, SAMPLES)]
    packed, codes = call(
        edge_forward_kernel(0),
        (whole(16, 2, 4, 8, 128), pltpu.SMEM((codes.size,), jnp.int32)), scratch + [dma],
        codes.reshape(-1), above, *phi, above_table, shift, packed,
        out_specs=(vmem, smem), aliases={6: 0},
    )
    packed = call(
        edge_forward_kernel(1), whole(16, 2, 4, 8, 128), scratch,
        below, *phi, below_table, shift, packed, aliases={5: 0},
    )
    packed, operators = lax.optimization_barrier((packed, operators))
    field = lax.all_to_all(packed, "clus", 0, 0)
    summed = translate(field, codes, counts, operators)
    local = lax.all_to_all(summed.reshape(packed.shape), "clus", 0, 0)
    up, down = call(
        edge_back_kernel, (whole(3, PLANES, PHI), whole(4, PLANES, PHI)),
        [whole(2, 256, 128)], local, shift, *phi, up_table, down_table,
    )
    from_below = shifted_ring(down, "theta", 1)
    from_above = shifted_ring(up, "theta", -1)
    own = call(
        own_back_kernel, whole(2, PLANES * OWN, 128), [half(1024, SAMPLES)] * 2,
        local, shift, *phi, back_high, back_low,
    )
    result, _ = call(
        merge_kernel,
        (jax.ShapeDtypeStruct((PLANES * OWN, PHI), WHOLE), whole(2, PLANES * OWN, 128)),
        [dma((8,))], own, from_below, from_above, out_specs=(hbm, vmem), aliases={0: 1},
    )
    return result.reshape(children.shape)


def solution(mesh):
    return jax.shard_map(
        on_device,
        mesh=mesh,
        in_specs=(
            P("clus", None, None, "theta", None),
            P("theta", None),
            P(),
            P(None, None, "theta", None),
            P(None, None, ("theta", "clus"), None),
            P(),
            P(),
            P(),
        ),
        out_specs=P("clus", None, None, "theta", None),
        check_vma=False,
    )
```

```python
import functools

import jax
import jax.numpy as jnp
from jax import lax
from jax.experimental import pallas as pl
from jax.experimental.pallas import tpu as pltpu
from jax.sharding import PartitionSpec as P


KIDS = 4
LIST = 32
GROUP = 8
PAIR = 2
PLANES = 32
ROWS = 32
OWN = 16
PHI = 256
SAMPLES = 512
GRANT = 12 * 2**20
HALF = jnp.bfloat16
WHOLE = jnp.float32


def shifted_ring(value, axis, step):
    count = lax.axis_size(axis)
    return lax.ppermute(value, axis, [(i, (i + step) % count) for i in range(count)])


def halves(value):
    high = value.astype(HALF)
    return high, (value - high.astype(WHOLE)).astype(HALF)


def dot3(left, right, contract=0):
    dims = (((1,), (contract,)), ((), ()))
    total = None
    for a, b in ((0, 0), (0, 1), (1, 0)):
        part = lax.dot_general(left[a], right[b], dims, preferred_element_type=WHOLE)
        total = part if total is None else total + part
    return total


def swap_blocks(tiles):
    sub = lax.broadcasted_iota(jnp.int32, (8, 128), 0)
    even = (sub // 2) % 2 == 0
    low = sub < 4
    a, b, c, d = tiles

    def step(first, second, shift, mask):
        one = jnp.where(mask, first, pltpu.roll(second, shift, 0))
        two = jnp.where(mask, pltpu.roll(first, 8 - shift, 0), second)
        return one, two

    a, b = step(a, b, 2, even)
    c, d = step(c, d, 2, even)
    a, c = step(a, c, 4, low)
    b, d = step(b, d, 4, low)
    return a, b, c, d


def lane_blocks(value):
    return [value[:, 128 * i : 128 * (i + 1)] for i in range(4)]


def table_times(table, value):
    wide = jnp.dot(table, jnp.concatenate([value[0], value[0]], axis=0), preferred_element_type=WHOLE)
    depth = table.shape[1] // 2
    return wide + jnp.dot(table[:, :depth], value[1], preferred_element_type=WHOLE)


def same(child, parent):
    return child, parent


def above_rows(child, parent):
    return child - 4, parent


def below_rows(child, parent):
    return child + OWN, parent + ROWS - 8


def side_table(bands, place):
    row = lax.broadcasted_iota(jnp.int32, (8, 256), 0)
    column = lax.broadcasted_iota(jnp.int32, (8, 256), 1)
    tap = tap_of(column % 4, row, place)
    part = column // 64
    high, low = (value.astype(WHOLE) for value in halves(bands))
    block = jnp.zeros((8, 256), WHOLE)
    for t in range(8):
        value = jnp.where(part == 1, low[:, t : t + 1], high[:, t : t + 1])
        block = jnp.where(jnp.logical_and(tap == t, part < 3), value, block)
    owner = (column % 64) // 4
    blocks = [jnp.where(owner == plane, block, 0.0) for plane in range(16)]
    return jnp.concatenate(blocks, axis=0).astype(HALF)


def tap_of(child, parent, place):
    child, parent = place(child, parent)
    return child - parent // 2 + 3


def forward_table(bands, planes, inner, place):
    outer = bands.shape[0]
    width = planes * inner
    row = lax.broadcasted_iota(jnp.int32, (outer, width), 0)
    column = lax.broadcasted_iota(jnp.int32, (outer, width), 1)
    tap = tap_of(column % inner, row, place)
    block = jnp.zeros((outer, width), WHOLE)
    for t in range(8):
        block = jnp.where(tap == t, jnp.broadcast_to(bands[:, t : t + 1], block.shape), block)
    owner = column // inner
    blocks = [jnp.where(owner == plane, block, 0.0) for plane in range(planes)]
    return jnp.concatenate(blocks, axis=0)


def backward_table(bands, planes, inner, place):
    outer = bands.shape[1]
    width = planes * outer
    high = max(inner, 8)
    pick = lax.broadcasted_iota(jnp.int32, (outer, width), 1) % outer
    pick = (lax.broadcasted_iota(jnp.int32, (outer, width), 0) == pick).astype(HALF)
    row = lax.broadcasted_iota(jnp.int32, (high, width), 0)
    column = lax.broadcasted_iota(jnp.int32, (high, width), 1)
    tap = tap_of(row % inner, column % outer, place)
    tables = []
    for part in halves(bands):
        tiled = jnp.dot(part, pick, preferred_element_type=WHOLE)
        block = jnp.zeros((high, width), WHOLE)
        for t in range(8):
            block = jnp.where(tap == t, jnp.broadcast_to(tiled[t : t + 1], block.shape), block)
        owner = column // outer - row // inner
        step = high // inner
        blocks = [jnp.where(owner == plane, block, 0.0) for plane in range(0, planes, step)]
        tables.append(jnp.concatenate(blocks, axis=0).astype(HALF))
    return tables


def cut_kernel(
    children_hbm, taps_hbm, children_ref, taps_ref, upper_ref, lower_ref, sems
):
    chunks = [slice(128 * i, 128 * i + 128) for i in range(4)]
    copies = [
        pltpu.make_async_copy(
            children_hbm.at[chunk, 128 * side : 128 * side + 128],
            children_ref.at[side, chunk],
            sems.at[2 * i + side],
        )
        for i, chunk in enumerate(chunks)
        for side in range(2)
    ]
    for copy in copies:
        copy.start()
    taps = pltpu.make_async_copy(taps_hbm, taps_ref, sems.at[8])
    taps.start()
    for at, copy in enumerate(copies):
        copy.wait()
        i, side = divmod(at, 2)
        for ref, first, count in ((upper_ref, 0, 4), (lower_ref, OWN - 3, 3)):
            for row in range(count):
                rows = pl.ds(128 * i + first + row, 8, stride=OWN)
                value = children_ref[side, rows, :]
                ref[row, 8 * i : 8 * i + 8, 128 * side : 128 * side + 128] = value
    taps.wait()


def both_sides(ref, first, count):
    return jnp.concatenate([ref[side, first : first + count] for side in range(2)], axis=1)


def own_forward_kernel(
    shift_hbm, source_hbm, offset_hbm, counts_hbm, phi_ref, taps_ref, children_ref,
    packed_ref, shift_ref, phi_high_ref, phi_low_ref, above_ref, below_ref,
    up_ref, down_ref, codes_ref, counts_ref,
    fine_ref, source_ref, offset_ref, sems, *, kinds,
):
    pairs = (
        (shift_hbm, shift_ref), (source_hbm, source_ref), (offset_hbm, offset_ref),
        (counts_hbm, counts_ref),
    )
    copies = [pltpu.make_async_copy(*pair, sems.at[i]) for i, pair in enumerate(pairs)]
    for copy in copies:
        copy.start()
    strip = lax.axis_index("theta")
    first = (strip > 0).astype(WHOLE)
    last = (strip < lax.axis_size("theta") - 1).astype(WHOLE)
    taps = taps_ref[...]
    bands = jnp.concatenate([taps] * 16, axis=0).T[:, :8]
    own = jnp.concatenate(halves(forward_table(bands, 8, 16, same)), axis=1)
    phi = halves(phi_ref[...])
    phi_high_ref[...], phi_low_ref[...] = phi

    def spread(group):
        mixed = dot3(halves(both_sides(children_ref, 128 * group, 128)), phi)
        fine_ref[256 * group : 256 * (group + 1)] = table_times(own, halves(mixed))

    def collect(parent):
        for pol in range(2):
            for block in range(4):
                rows = slice(8 * block, 8 * (block + 1))
                real, imag = gathered(fine_ref, shift_ref, parent, pol, 32, 8 * block, rows)
                for part, value in enumerate((real, imag)):
                    for pair, tile in enumerate(swap_blocks(lane_blocks(value))):
                        packed_ref[4 * block + pair, parent, 2 * pol + part] = tile

    spread(0)
    spread(1)
    for copy in copies:
        copy.wait()
    spread(2)
    collect(0)
    spread(3)
    above_ref[...] = side_table(bands[:8] * first, above_rows)
    below_ref[...] = side_table(bands[ROWS - 8 :] * last, below_rows)
    upper, lower = taps[:, :8] * first, taps[:, ROWS - 8 :] * last
    table = backward_table(upper, 16, 4, above_rows)
    up_ref[...] = jnp.concatenate(table, axis=1)
    table = backward_table(lower, 16, 4, below_rows)
    down_ref[...] = jnp.concatenate(table, axis=1)
    lane = lax.broadcasted_iota(jnp.int32, (1, LIST), 1)
    for parent in range(source_ref.shape[0]):
        live = lane < counts_ref[parent]
        offset = jnp.where(live, offset_ref[parent : parent + 1], kinds)
        codes_ref[parent : parent + 1] = source_ref[parent : parent + 1] * 32 + offset * (24 * 65536)
    collect(1)


def gathered(fine_ref, shift_ref, parent, pol, per_plane, first, rows):
    real = imag = None
    for kid in range(KIDS):
        at = ((parent * KIDS + kid) * 4 + pol * 2) * per_plane + first
        a = fine_ref[at : at + 8]
        b = fine_ref[at + per_plane : at + per_plane + 8]
        c = shift_ref[kid, 0, rows]
        d = shift_ref[kid, 1, rows]
        one, two = c * a - d * b, c * b + d * a
        real = one if real is None else real + one
        imag = two if imag is None else imag + two
    return real, imag


def edge_forward_kernel(side):
    first, count = 12 * side, 3 + side

    def kernel(*refs):
        if side == 0:
            codes_src, halo_in, phi_high_ref, phi_low_ref, table_ref, shift_ref = refs[:6]
            _, out_ref, codes_ref, halo_ref, fine_ref, sem = refs[6:]
            codes = pltpu.make_async_copy(codes_src, codes_ref, sem)
            codes.start()
        else:
            halo_in, phi_high_ref, phi_low_ref, table_ref, shift_ref = refs[:5]
            _, out_ref, halo_ref, fine_ref = refs[5:]
        for half in range(2):
            lanes = slice(128 * half, 128 * half + 128)
            if side == 0:
                halo_ref[half, pl.ds(0, PLANES, stride=4), :] = jnp.zeros((PLANES, 128), WHOLE)
            for row in range(count):
                rows = pl.ds(row + 4 - count, PLANES, stride=4)
                halo_ref[half, rows, :] = halo_in[row, :, lanes]
        phi = (phi_high_ref[...], phi_low_ref[...])
        high, low = halves(dot3(halves(both_sides(halo_ref, 0, 128)), phi))
        table = table_ref[...]
        for parent in range(2):
            rows = slice(64 * parent, 64 * parent + 64)
            value = jnp.concatenate([high[rows], high[rows], low[rows], high[rows]], axis=0)
            fine = jnp.dot(table, value, preferred_element_type=WHOLE)
            fine_ref[128 * parent : 128 * parent + 128] = fine
        rows = slice(24 * side, 24 * side + 8)
        for parent in range(2):
            for pol in range(2):
                real, imag = gathered(fine_ref, shift_ref, parent, pol, 8, 0, rows)
                for part, value in enumerate((real, imag)):
                    for pair, tile in enumerate(swap_blocks(lane_blocks(value))):
                        at = (first + pair, parent, 2 * pol + part)
                        out_ref[at] = out_ref[at] + tile
        if side == 0:
            codes.wait()

    return kernel


def spread_back(local_ref, shift_ref, parent, pol, blocks):
    parts = []
    for part in range(2):
        pieces = []
        for first in blocks:
            tiles = [local_ref[first + pair, parent, 2 * pol + part] for pair in range(4)]
            pieces.append(jnp.concatenate(swap_blocks(tiles), axis=1))
        parts.append(pieces)
    for kid in range(KIDS):
        real, imag = [], []
        for index, first in enumerate(blocks):
            a, b = parts[0][index], parts[1][index]
            c = shift_ref[kid, 0, 2 * first : 2 * first + 8]
            d = shift_ref[kid, 1, 2 * first : 2 * first + 8]
            real.append(c * a + d * b)
            imag.append(c * b - d * a)
        yield kid, halves(jnp.concatenate(real + imag, axis=0))


def edge_back_kernel(first, skipped):
    def kernel(
        local_ref, shift_ref, phi_high_ref, phi_low_ref, table_ref, out_ref, result_ref,
    ):
        phi = (phi_high_ref[...], phi_low_ref[...])
        table = table_ref[...]
        narrow = []
        for parent in range(2):
            pieces = {}
            for pol in range(2):
                for kid, value in spread_back(local_ref, shift_ref, parent, pol, (first,)):
                    pieces[kid, pol] = value
            order = [(kid, pol) for kid in range(KIDS) for pol in range(2)]
            value = [jnp.concatenate([pieces[at][i] for at in order], axis=0) for i in range(2)]
            narrow.append(table_times(table, value))
        result = dot3(halves(jnp.concatenate(narrow, axis=0)), phi, contract=1)
        for side in range(2):
            lanes = slice(128 * side, 128 * side + 128)
            result_ref[side] = result[:, lanes]
            for row in range(4 - skipped):
                rows = pl.ds(row + skipped, PLANES, stride=4)
                out_ref[row, :, lanes] = result_ref[side, rows, :]

    return kernel


def own_back_kernel(
    local_ref, shift_ref, phi_high_ref, phi_low_ref, taps_ref,
    own_ref, high_ref, low_ref,
):
    phi = (phi_high_ref[...], phi_low_ref[...])
    table = backward_table(taps_ref[...], 8, 16, same)

    for parent in range(2):
        for pol in range(2):
            for kid, value in spread_back(local_ref, shift_ref, parent, pol, (0, 4, 8, 12)):
                at = ((parent * KIDS + kid) * 2 + pol) * 64
                high_ref[at : at + 64], low_ref[at : at + 64] = value
        for group in (2 * parent, 2 * parent + 1):
            rows = slice(256 * group, 256 * (group + 1))
            narrowed = dot3(table, (high_ref[rows], low_ref[rows]))
            result = dot3(halves(narrowed), phi, contract=1)
            for side in range(2):
                lanes = slice(128 * side, 128 * side + 128)
                own_ref[side, 128 * group : 128 * (group + 1)] = result[:, lanes]


def translate_kernel(codes_ref, counts_ref, field_ref, operator_ref, out_ref, table_ref, sum_ref):
    parents = counts_ref.shape[0]
    kinds = operator_ref.shape[0] // 16
    for kind in range(kinds):
        c = operator_ref[16 * kind : 16 * kind + 8]
        d = operator_ref[16 * kind + 8 : 16 * kind + 16]
        for at, value in enumerate((c, d - c, c + d)):
            table_ref[24 * kind + 8 * at : 24 * kind + 8 * at + 8] = value
    table_ref[24 * kinds : 24 * kinds + 24] = jnp.zeros((24, 128), WHOLE)
    for at in range(2 * parents):
        rows = slice(16 * at, 16 * at + 8)
        sum_ref[8 * at : 8 * at + 8] = field_ref[rows] + field_ref[16 * at + 8 : 16 * at + 16]

    def one_pair(pair, carry):
        def some_slots(step, sums):
            sums = list(sums)
            for member in range(PAIR):
                for lane in range(GROUP):
                    slot = pair * (PAIR * LIST) + step * GROUP + (member * LIST + lane)
                    code = codes_ref[slot]
                    source = pl.multiple_of(code & 0xFFFF, 8)
                    offset = pl.multiple_of(code >> 16, 8)
                    half = pl.multiple_of((code & 0xFFFF) >> 1, 8)
                    c = table_ref[pl.ds(offset, 8), :]
                    less = table_ref[pl.ds(offset + 8, 8), :]
                    more = table_ref[pl.ds(offset + 16, 8), :]
                    for pol in range(2):
                        at = member * 6 + pol * 3
                        a = field_ref[pl.ds(source + pol * 16, 8), :]
                        b = field_ref[pl.ds(source + (pol * 16 + 8), 8), :]
                        sums[at] = sums[at] + c * sum_ref[pl.ds(half + pol * 8, 8), :]
                        sums[at + 1] = sums[at + 1] + a * less
                        sums[at + 2] = sums[at + 2] + b * more
            return tuple(sums)

        zero = jnp.zeros((8, 128), WHOLE)
        longest = jnp.maximum(counts_ref[pair * PAIR], counts_ref[pair * PAIR + 1])
        steps = lax.shift_right_logical(longest + (GROUP - 1), 3)
        sums = lax.fori_loop(0, steps, some_slots, (zero,) * (6 * PAIR))
        for member in range(PAIR):
            for pol in range(2):
                both, less, more = sums[member * 6 + pol * 3 : member * 6 + pol * 3 + 3]
                at = pl.multiple_of(pair * 64 + member * 32 + pol * 16, 8)
                out_ref[pl.ds(at, 8), :] = both - more
                out_ref[pl.ds(at + 8, 8), :] = both + less
        return carry

    lax.fori_loop(0, parents // PAIR, one_pair, 0)


def in_vmem(value):
    return pltpu.with_memory_space_constraint(value, pltpu.VMEM)


def in_smem(value):
    return pltpu.with_memory_space_constraint(value, pltpu.SMEM)


def in_hbm(value):
    return pltpu.with_memory_space_constraint(value, pltpu.HBM)


def call(kernel, outs, scratch, *operands, raw=0, out_specs=None, aliases={}):
    vmem = pl.BlockSpec(memory_space=pltpu.VMEM)
    hbm = pl.BlockSpec(memory_space=pltpu.HBM)
    return pl.pallas_call(
        kernel,
        out_shape=outs,
        in_specs=[hbm] * raw + [vmem] * (len(operands) - raw),
        out_specs=out_specs if out_specs is not None else jax.tree.map(lambda _: vmem, outs),
        scratch_shapes=scratch,
        input_output_aliases=aliases,
        compiler_params=pltpu.CompilerParams(vmem_limit_bytes=GRANT),
    )(*map(in_hbm, operands[:raw]), *map(in_vmem, operands[raw:]))


def operator_rows(translators):
    kinds, _, rows, samples = translators.shape
    table = translators.reshape(kinds, 2, rows, samples // 128, 128).transpose(0, 1, 3, 2, 4)
    return table.reshape(kinds * 16, 128)


def translate(field, codes, counts, operators):
    smem = pl.BlockSpec(memory_space=pltpu.SMEM)
    vmem = pl.BlockSpec(memory_space=pltpu.VMEM)
    field = field.reshape(-1, 128)
    return pl.pallas_call(
        translate_kernel,
        out_shape=jax.ShapeDtypeStruct(field.shape, WHOLE),
        in_specs=[smem, smem, vmem, vmem],
        out_specs=vmem,
        scratch_shapes=[
            pltpu.VMEM((operators.shape[0] * 3 // 2 + 24, 128), WHOLE),
            pltpu.VMEM((field.shape[0] // 2, 128), WHOLE),
        ],
        compiler_params=pltpu.CompilerParams(vmem_limit_bytes=GRANT),
        name="translate",
    )(in_smem(codes), in_smem(counts), in_vmem(field), in_vmem(operators))


def merge_kernel(_, top_ref, bottom_ref, out_hbm, own_ref, sems):
    copies = []
    for i in range(4):
        chunk = slice(128 * i, 128 * i + 128)
        for side in range(2):
            lanes = slice(128 * side, 128 * side + 128)
            for ref, first, count in ((top_ref, 0, 4), (bottom_ref, OWN - 3, 3)):
                for row in range(count):
                    rows = pl.ds(128 * i + first + row, 8, stride=OWN)
                    value = own_ref[side, rows, :] + ref[row, 8 * i : 8 * i + 8, lanes]
                    own_ref[side, rows, :] = value
            target = out_hbm.at[chunk, lanes]
            copy = pltpu.make_async_copy(own_ref.at[side, chunk], target, sems.at[2 * i + side])
            copy.start()
            copies.append(copy)
    for copy in copies:
        copy.wait()


def on_device(
    children, theta_band, phi_interp, child_shift, translators, far_source, far_offset, far_count
):
    half = lambda *shape: pltpu.VMEM(shape, HALF)
    whole = lambda *shape: pltpu.VMEM(shape, WHOLE)
    hbm = pl.BlockSpec(memory_space=pl.ANY)
    vmem = pl.BlockSpec(memory_space=pltpu.VMEM)
    smem = pl.BlockSpec(memory_space=pltpu.SMEM)
    dma = pltpu.SemaphoreType.DMA
    planes, taps, upper, lower = call(
        cut_kernel,
        (
            whole(2, PLANES * OWN, 128), whole(8, ROWS), whole(4, PLANES, PHI),
            whole(3, PLANES, PHI),
        ),
        [dma((9,))], children.reshape(-1, PHI), theta_band.T, raw=2,
    )
    above = shifted_ring(lower, "theta", 1)
    below = shifted_ring(upper, "theta", -1)
    tables = (half(256, 512),) * 2 + (half(128, 256),) * 2
    packed, shift, *tables, codes, counts = call(
        functools.partial(own_forward_kernel, kinds=translators.shape[0]),
        (whole(16, 2, 4, 8, 128), whole(*child_shift.shape)) + tables + (half(64, 256),) * 2
        + (pltpu.VMEM(far_source.shape, jnp.int32), pltpu.SMEM(far_count.shape, jnp.int32)),
        [
            whole(1024, SAMPLES), pltpu.VMEM(far_source.shape, jnp.int32),
            pltpu.VMEM(far_source.shape, jnp.int32), dma((4,)),
        ],
        child_shift, far_source, far_offset, far_count, phi_interp, taps, planes,
        raw=4, out_specs=(vmem,) * 9 + (smem,),
    )
    *phi, above_table, below_table, up_table, down_table = tables
    operators = in_vmem(operator_rows(translators))
    scratch = [whole(2, 128, 128), whole(256, SAMPLES)]
    packed, codes = call(
        edge_forward_kernel(0),
        (whole(16, 2, 4, 8, 128), pltpu.SMEM((codes.size,), jnp.int32)), scratch + [dma],
        codes.reshape(-1), above, *phi, above_table, shift, packed,
        out_specs=(vmem, smem), aliases={6: 0},
    )
    packed = call(
        edge_forward_kernel(1), whole(16, 2, 4, 8, 128), scratch,
        below, *phi, below_table, shift, packed, aliases={5: 0},
    )
    packed, operators = lax.optimization_barrier((packed, operators))
    field = lax.all_to_all(packed, "clus", 0, 0)
    summed = translate(field, codes, counts, operators)
    local = lax.all_to_all(summed.reshape(packed.shape), "clus", 0, 0)
    scratch = [whole(2, 128, 128)]
    down = call(
        edge_back_kernel(12, 0), whole(4, PLANES, PHI), scratch,
        local, shift, *phi, down_table,
    )
    from_below = shifted_ring(down, "theta", 1)
    up = call(
        edge_back_kernel(0, 1), whole(3, PLANES, PHI), scratch,
        local, shift, *phi, up_table,
    )
    from_above = shifted_ring(up, "theta", -1)
    own = call(
        own_back_kernel, whole(2, PLANES * OWN, 128), [half(1024, SAMPLES)] * 2,
        local, shift, *phi, taps,
    )
    result, _ = call(
        merge_kernel,
        (jax.ShapeDtypeStruct((PLANES * OWN, PHI), WHOLE), whole(2, PLANES * OWN, 128)),
        [dma((8,))], own, from_below, from_above, out_specs=(hbm, vmem), aliases={0: 1},
    )
    return result.reshape(children.shape)


def solution(mesh):
    return jax.shard_map(
        on_device,
        mesh=mesh,
        in_specs=(
            P("clus", None, None, "theta", None),
            P("theta", None),
            P(),
            P(None, None, "theta", None),
            P(None, None, ("theta", "clus"), None),
            P(),
            P(),
            P(),
        ),
        out_specs=P("clus", None, None, "theta", None),
        check_vma=False,
    )
```
